32 devices in a mesh: cells: 8 (over y, x, core), spec: 4 (over z).
Axes of the slice: x: 2, y: 2, z: 4, core: 2. Of those that a mesh axis runs over, the one named last changes fastest.
Arguments:
- spectrum_start: float32 [32, 36, 128, 512], P('spec', None, 'cells'), may hold values from 0.05 to 1
- input_coef: float32 [128, 512], P('cells'), may hold values from 0.5 to 2
- white_coef: float32 [128, 512], P('cells'), may hold values from 0.5 to 2
- wind_speed: float32 [128, 512], P('cells'), may hold values from 0.2 to 1.5
- wind_angle: float32 [128, 512], P('cells'), may hold values from -3.140625 to 3.140625
- sea_mask: int32 [128, 512], P('cells'), may hold values 0 or 1
- cotangent: float32 [32, 36, 128, 512], P('spec', None, 'cells'), may hold values from -6 to 6
Outputs:
- adjoint_start: float32 [32, 36, 128, 512], P('spec', None, 'cells')
- grad_input: float32 [128, 512], P('cells')
- grad_white: float32 [128, 512], P('cells')
The draws below stay inside these ranges and needn't reach their ends.
All inputs are finite; a program needn't handle non-finite values. No bound on the sum of `sea_mask` on one device may be relied on, other than what follows from the above.
Results may differ from the reference program's by a relative error of at most 0.00013.
Values sent between devices are 32-bit elements; how exact they have to be, the bound alone decides.
No kernel may reach another device: no remote copies, remote signals or barrier semaphores. Data moves between devices by JAX's collectives and lax.ppermute only.
A program may use at most 128 MiB of HBM per device.

```python
import math
import jax
import jax.numpy as jnp
from jax import lax

NF = 32
ND = 36
NC = 512
STEPS = 2
NR = 128


def with_ends(drawn, rng, smallest, largest):
    shape = drawn.shape
    place = [jax.random.randint(jax.random.fold_in(rng, axis), (), 0, shape[axis]) for axis in range(len(shape))]
    drawn = drawn.at[tuple(place)].set(smallest)
    longest = shape.index(max(shape))
    place[longest] = (place[longest] + 1) % shape[longest]
    return drawn.at[tuple(place)].set(largest)


def levels(stream_key, shape, shards, low, largest):
    def one(axis_at, shards_of):
        draws = jax.random.uniform(jax.random.fold_in(jax.random.fold_in(stream_key, 6), axis_at), (shards_of,), jnp.float32, low / len(shards), largest / len(shards))
        return jnp.repeat(jnp.exp(draws), shape[axis_at] // shards_of).reshape((-1,) + (1,) * (len(shape) - axis_at - 1))

    factor_of = one(*shards[0])
    for cut in shards[1:]:
        factor_of = factor_of * one(*cut)
    return factor_of


def normal_values(own_key, extent, width, most, pieces=(), kind=jnp.bfloat16):
    array = width * jax.random.normal(own_key, extent, jnp.float32)
    if pieces:
        array = array * levels(own_key, extent, pieces, -0.22, 0.18)
    return jnp.clip(array, -most, most).astype(kind)


def setup_inputs(seed: int = 0) -> dict:
    key_list = jax.random.split(jax.random.key(seed), 8)
    return {
        "spectrum_start": jnp.clip(jnp.exp(math.log(1.0) - 2.9957323 * jax.random.uniform(key_list[0], (NF, ND, NR, NC), jnp.float32) ** levels(key_list[0], (NF, ND, NR, NC), ((0, 4), (2, 8)), -0.2, 0.2)), 0.05, 1.0),
        "input_coef": jnp.clip(jnp.exp(math.log(2.0) - 1.3862944 * jax.random.uniform(key_list[1], (NR, NC), jnp.float32) ** levels(key_list[1], (NR, NC), ((0, 8),), -0.2, 0.2)), 0.5, 2.0),
        "white_coef": jnp.clip(jnp.exp(math.log(2.0) - 1.3862944 * jax.random.uniform(key_list[2], (NR, NC), jnp.float32) ** levels(key_list[2], (NR, NC), ((0, 8),), -0.2, 0.2)), 0.5, 2.0),
        "wind_speed": jnp.clip(0.2 + 1.3 * jax.random.uniform(key_list[3], (NR, NC), jnp.float32) ** levels(key_list[3], (NR, NC), ((0, 8),), -0.2, 0.2), 0.2, 1.5),
        "wind_angle": jnp.clip(jax.random.uniform(key_list[4], (NR, NC), jnp.float32, -3.140625, 3.140625), -3.140625, 3.140625),
        "sea_mask": with_ends((jax.random.randint(key_list[5], (NR, NC), 0, 5) < 4).astype(jnp.int32), jax.random.fold_in(key_list[5], 1), 0, 1),
        "cotangent": normal_values(key_list[6], (NF, ND, NR, NC), 1.0, 6.0, ((0, 4), (2, 8)), jnp.float32),
    }


epsilon = 1e-06
energy_ref = 0.5
time_step = 0.5
courant = 0.7
ratio_step = 1.1

def advect(spectra, cos_dir, sin_dir, courant_x, courant_y):
    up_x = jnp.where(cos_dir >= 0, jnp.roll(spectra, 1, axis=3), jnp.roll(spectra, -1, axis=3))
    padded = jnp.pad(spectra, ((0, 0), (0, 0), (1, 1), (0, 0)))
    up_y = jnp.where(sin_dir >= 0, padded[:, :, :-2], padded[:, :, 2:])
    return (1.0 - courant_x - courant_y) * spectra + courant_x * up_x + courant_y * up_y

def reference(spectrum_start, input_coef, white_coef, wind_speed, wind_angle, sea_mask, cotangent):
    ocean = sea_mask.astype(jnp.float32)
    every = jnp.exp(jnp.arange(NF, dtype=jnp.float32) * math.log(ratio_step))
    frequency = every[:, None, None, None]
    highest = every[NF - 1]
    total = jnp.sum(every)
    mean_ratio = jnp.sum(every * every) / total
    weights = frequency / (ND * total)
    damp_shape = (frequency / highest) ** 2
    angle = 2.0 * math.pi * jnp.arange(ND, dtype=jnp.float32) / ND
    cos_dir = jnp.cos(angle)[None, :, None, None]
    sin_dir = jnp.sin(angle)[None, :, None, None]
    courant_x = courant * jnp.abs(cos_dir) / frequency
    courant_y = courant * jnp.abs(sin_dir) / frequency
    align = jnp.maximum(cos_dir * jnp.cos(wind_angle) + sin_dir * jnp.sin(wind_angle), 0.0)
    forcing = wind_speed * (frequency / highest) * align * align

    def forward(spectrum, coef_in, coef_white):
        spectra = ocean * spectrum
        for step_index in range(STEPS):
            advected = ocean * advect(spectra, cos_dir, sin_dir, courant_x, courant_y)
            energy = lax.optimization_barrier(jnp.sum(weights * advected, axis=(0, 1)))
            moment = lax.optimization_barrier(jnp.sum(weights * frequency * advected, axis=(0, 1)))
            ratio = moment / ((energy + epsilon) * mean_ratio)
            steep = energy * ratio ** 4 / energy_ref
            damping = steep * steep * ratio
            spectra = advected * jnp.exp(time_step * (coef_in * forcing - coef_white * damp_shape * damping))
        return spectra
    result, pullback = jax.vjp(forward, spectrum_start, input_coef, white_coef)
    grads = pullback(cotangent)
    return (grads[0], grads[1], grads[2])
```

```python
import functools
import math

import jax
import jax.numpy as jnp
import numpy as np
from jax import lax
from jax.experimental import pallas as pl
from jax.experimental.pallas import tpu as pltpu
from jax.sharding import PartitionSpec as P

NF = 32
ND = 36
STEPS = 2

epsilon = 1e-06
energy_ref = 0.5
time_step = 0.5
courant = 0.7
ratio_step = 1.1

F32 = jnp.float32
LOG2E = math.log2(math.e)

_every = np.exp(np.arange(NF, dtype=np.float32) * np.float32(math.log(ratio_step))).astype(np.float32)
_total = _every.sum(dtype=np.float32)
HIGHEST = float(_every[-1])
MEAN_RATIO = float((_every * _every).sum(dtype=np.float32) / _total)
_weights = _every / (np.float32(ND) * _total)
_q = (_every / _every[-1]) ** 2
NTAB = 5
TABLE = np.stack([_every, 1 / _every, _weights, _q, _weights * _every], axis=1).astype(np.float32).reshape(-1)

_angle = (np.float32(2.0 * math.pi) * np.arange(ND, dtype=np.float32) / np.float32(ND)).astype(np.float32)
COS, SIN = np.cos(_angle).astype(np.float32), np.sin(_angle).astype(np.float32)
KX, KY = np.float32(courant) * np.abs(COS), np.float32(courant) * np.abs(SIN)
XP, YP = [bool(c >= 0) for c in COS], [bool(s >= 0) for s in SIN]
NL = sum(YP)
NH = ND - NL
assert YP == [True] * NL + [False] * NH and NL == NH
QUADS = [[d for d in range(ND) if (XP[d], YP[d]) == quad] for quad in ((1, 1), (0, 1), (0, 0), (1, 0))]
DIRS = np.stack([v[a:b] for a, b in ((0, NL), (NL, ND)) for v in (KX, KY, COS, SIN)]).astype(np.float32)
DIRS = np.ascontiguousarray(np.broadcast_to(DIRS[:, :, None], DIRS.shape + (128,)))

MIB = 1 << 20


def coef(tab, j, nf, which):
    return tab[(lax.axis_index("spec") * nf + j) * NTAB + which]


def shift_x(x, plus):
    return pltpu.roll(x, 1 if plus else x.shape[1] - 1, 1)


def first_row(x):
    return lax.broadcasted_iota(jnp.int32, x.shape, 0) == 0


def last_row(x):
    return lax.broadcasted_iota(jnp.int32, x.shape, 0) == x.shape[0] - 1


def from_before(x, above):
    return jnp.where(first_row(x), above, pltpu.roll(x, 1, 0))


def from_after(x, below):
    return jnp.where(last_row(x), below, pltpu.roll(x, x.shape[0] - 1, 0))


def shift_y(x, plus, outside):
    return from_before(x, outside) if plus else from_after(x, outside)


def damping_of(energy, moment):
    shifted = energy + epsilon
    ratio = moment / (shifted * MEAN_RATIO)
    r2 = ratio * ratio
    steep = energy * (r2 * r2) / energy_ref
    return shifted, ratio, steep, steep * steep * ratio


def grads_of(energy, moment, white, damp_total):
    shifted, ratio, steep, damping = damping_of(energy, moment)
    grad_damp = -time_step * white * damp_total
    grad_ratio = 9.0 * grad_damp * steep * steep
    r2 = ratio * ratio
    grad_energy = grad_damp * 2.0 * steep * (r2 * r2) * ratio / energy_ref - grad_ratio * ratio / shifted
    grad_moment = grad_ratio / (shifted * MEAN_RATIO)
    return grad_energy, grad_moment, damping


def gate(q, white, damping, ocean):
    return ocean * jnp.exp2((-time_step * LOG2E) * q * (white * damping))


def start_kernel(nf, tab, s_ref, mask, coef_in, white, speed, angle, t0_ref, up_ref, dn_ref, sums):
    j = pl.program_id(0)
    rows, nc = mask.shape
    rj, w, wf = coef(tab, j, nf, 1), coef(tab, j, nf, 2), coef(tab, j, nf, 4)
    for t in range(0, rows, 8):
        acc = [None] * 5

        def add(k, v):
            acc[k] = v if acc[k] is None else acc[k] + v

        for d in range(ND):
            x = s_ref[0, d, t : t + 8, :]
            add(0, x)
            add(1 if XP[d] else 2, float(KX[d]) * x)
            add(3 if YP[d] else 4, float(KY[d]) * x)
        for k in range(5):
            sums[k, t : t + 8, :] = acc[k]
    ocean = mask[...].astype(F32)
    total, xp, xm, yp, ym = [ocean * sums[k] for k in range(5)]
    adv = total + rj * (
        shift_x(xp, True) + shift_x(xm, False) + from_before(yp, 0.0) + from_after(ym, 0.0) - (xp + xm + yp + ym)
    )
    push_up, push_dn = rj * yp[rows - 1 : rows], rj * ym[0:1]

    @pl.when(j == 0)
    def _():
        t0_ref[...] = jnp.zeros_like(t0_ref)
        up_ref[nf] = jnp.zeros_like(up_ref[nf])
        dn_ref[nf] = jnp.zeros_like(dn_ref[nf])
        kappa = (time_step * LOG2E / HIGHEST) * (coef_in[...] * speed[...])
        for k, v in enumerate((kappa, jnp.cos(angle[...]), jnp.sin(angle[...]), ocean, white[...])):
            for r in range(2):
                up_ref[nf, r, k : k + 1, :] = v[rows - 2 + r : rows - 1 + r]
                dn_ref[nf, r, k : k + 1, :] = v[r : r + 1]

    t0_ref[0:rows, :] += w * adv
    t0_ref[rows : 2 * rows, :] += wf * adv
    for k, v in enumerate((w * push_up, wf * push_up, w * push_dn, wf * push_dn)):
        t0_ref[2 * rows + k : 2 * rows + k + 1, :] += v
    for r in range(2):
        for d in range(NL):
            up_ref[j, r, d : d + 1, :] = s_ref[0, d, rows - 2 + r : rows - 1 + r, :]
            dn_ref[j, r, d : d + 1, :] = s_ref[0, NL + d, r : r + 1, :]


def wind_kernel(nf, tab, lam, coef_in, speed, angle, g_ref, p_ref, al_ref, up_ref, dn_ref, expo):
    j = pl.program_id(0)
    rows, nc = angle.shape
    fr = coef(tab, j, nf, 0)

    @pl.when(j == 0)
    def _():
        kappa = (time_step * LOG2E / HIGHEST) * (coef_in[...] * speed[...])
        ca, sa = jnp.cos(angle[...]), jnp.sin(angle[...])
        for d in range(ND):
            align = jnp.maximum(float(COS[d]) * ca + float(SIN[d]) * sa, 0.0)
            al = align * align
            al_ref[d] = al
            expo[d] = kappa * al

    for d in range(ND):
        g = jnp.exp2(fr * expo[d])
        p = g * lam[0, d]
        g_ref[0, d] = g
        p_ref[0, d] = p
        for r in range(2):
            if d < NL:
                dn_ref[0, r, d : d + 1, :] = p[r : r + 1]
            else:
                up_ref[0, r, d - NL : d - NL + 1, :] = p[rows - 2 + r : rows - 1 + r]


def halo_growth(fr, dirs, half, misc, r):
    cosd, sind = dirs[4 * half + 2][:, 0:1], dirs[4 * half + 3][:, 0:1]
    align = jnp.maximum(cosd * misc[0, r, 1:2, :] + sind * misc[0, r, 2:3, :], 0.0)
    return jnp.exp2(fr * (misc[0, r, 0:1, :] * (align * align)))


def halo_shift_x(x, cosd, transpose):
    before, after = shift_x(x, True), shift_x(x, False)
    if transpose:
        before, after = after, before
    return jnp.where(cosd >= 0, before, after)


def halo_adv(rj, dirs, half, near, far, transpose):
    kx, ky, cosd = [dirs[4 * half + k][:, 0:1] for k in range(3)]
    cx, cy = kx * rj, ky * rj
    return (1.0 - cx - cy) * near + cx * halo_shift_x(near, cosd, transpose) + cy * far


def grown_kernel(nf, tab, dirs, s_ref, mask, g_ref, lo, lo_misc, hi, hi_misc, u_ref, sum_ref, ul_ref, uh_ref, sy_ref):
    j = pl.program_id(0)
    rows, nc = mask.shape
    fr, rj = coef(tab, j, nf, 0), coef(tab, j, nf, 1)
    edges = []
    for half, (blk, misc, near, far, out) in enumerate(((lo, lo_misc, 1, 0, ul_ref), (hi, hi_misc, 0, 1, uh_ref))):
        o_near, o_far = misc[0, near, 3:4, :], misc[0, far, 3:4, :]
        adv = halo_adv(rj, dirs, half, o_near * blk[0, near], o_far * blk[0, far], False)
        u = halo_growth(fr, dirs, half, misc, near) * adv
        out[0] = u
        sy_ref[0, half : half + 1, :] = jnp.sum(dirs[4 * half + 1][:, 0:1] * u, axis=0, keepdims=True)
        edges.append(o_near)
    ocean = mask[...].astype(F32)
    zero = jnp.zeros((8, nc), F32)
    for t in range(0, rows, 8):
        ot = ocean[t : t + 8]
        total, sxp, sxm, syp, sym = zero, zero, zero, zero, zero
        for d in range(ND):
            cx, cy = float(KX[d]) * rj, float(KY[d]) * rj
            x = ot * s_ref[0, d, t : t + 8, :]
            if YP[d]:
                if t == 0:
                    out_row = edges[0] * lo[0, 1, d : d + 1, :]
                else:
                    out_row = ocean[t - 1 : t] * s_ref[0, d, t - 1 : t, :]
            else:
                if t + 8 == rows:
                    out_row = edges[1] * hi[0, 0, d - NL : d - NL + 1, :]
                else:
                    out_row = ocean[t + 8 : t + 9] * s_ref[0, d, t + 8 : t + 9, :]
            adv = (1.0 - cx - cy) * x + cx * shift_x(x, XP[d]) + cy * shift_y(x, YP[d], out_row)
            u = g_ref[0, d, t : t + 8, :] * adv
            u_ref[0, d, t : t + 8, :] = u
            total = total + u
            if XP[d]:
                sxp = sxp + float(KX[d]) * u
            else:
                sxm = sxm + float(KX[d]) * u
            if YP[d]:
                syp = syp + float(KY[d]) * u
            else:
                sym = sym + float(KY[d]) * u
        for k, v in enumerate((total - rj * (sxp + sxm + syp + sym), sxp, sxm, syp, sym)):
            sum_ref[k, 0, t : t + 8, :] = v


def product_kernel(nf, tab, u_ref, p_ref, al_ref, ul_ref, uh_ref, r_ref, t_ref):
    j = pl.program_id(0)
    rows, nc = u_ref.shape[2:]
    rj = coef(tab, j, nf, 1)
    zero = jnp.zeros((8, nc), F32)
    for t in range(0, rows, 8):
        out = {}
        for quad in QUADS:
            acc = [zero] * 8
            for d in quad:
                kx, ky = float(KX[d]), float(KY[d])
                u, p, al = u_ref[0, d, t : t + 8, :], p_ref[0, d, t : t + 8, :], al_ref[d, t : t + 8, :]
                if YP[d]:
                    row = ul_ref[0, d : d + 1, :] if t == 0 else u_ref[0, d, t - 1 : t, :]
                elif t + 8 == rows:
                    row = uh_ref[0, d - NL : d - NL + 1, :]
                else:
                    row = u_ref[0, d, t + 8 : t + 9, :]
                pu = p * u
                px = kx * (p * shift_x(u, XP[d]))
                py = ky * (p * shift_y(u, YP[d], row))
                for k, v in enumerate((pu, (kx + ky) * pu, px, py)):
                    acc[k] = acc[k] + v
                apu = al * pu
                for k, v in enumerate((apu, (kx + ky) * apu, al * px, al * py)):
                    acc[4 + k] = acc[4 + k] + v
            xk, yk = (1 if XP[quad[0]] else 2), (3 if YP[quad[0]] else 4)
            for b in (0, 4):
                for key, v in ((0, acc[b] - rj * acc[b + 1]), (xk, acc[b + 2]), (yk, acc[b + 3])):
                    out[b, key] = out[b, key] + v if (b, key) in out else v
        for k in range(5):
            r_ref[k, 0, t : t + 8, :] = out[0, k]
            t_ref[k, 0, t : t + 8, :] = out[4, k]


def total_kernel(rows, *refs):
    parts, (tot, up, dn) = refs[:-3], refs[-3:]
    total = parts[0][...]
    for part in parts[1:]:
        total = total + part[...]
    tot[...] = total
    up[...] = jnp.zeros_like(up)
    dn[...] = jnp.zeros_like(dn)
    for k, row in enumerate((rows - 1, 2 * rows - 1, 2 * rows, 2 * rows + 1)):
        up[k : k + 1, :] = total[row : row + 1]
    for k, row in enumerate((0, rows, 2 * rows + 2, 2 * rows + 3)):
        dn[k : k + 1, :] = total[row : row + 1]


def advected_sum(rj, h, above, below, s):
    return h * s[0], rj * (
        shift_x(h * s[1], True) + shift_x(h * s[2], False) + from_before(h * s[3], above) + from_after(h * s[4], below)
    )


def first_kernel(nf, tab, tot, lo, hi, lo_misc, hi_misc, mask, white, sum_ref, sy_ref, t0_ref, t0h_ref, h0_ref, h0h_ref, t1_ref):
    rows, nc = mask.shape
    ocean = mask[...].astype(F32)
    row = lax.broadcasted_iota(jnp.int32, (rows, nc), 0)
    total = tot[...]
    field = []
    halo = []
    t0h_ref[...] = jnp.zeros_like(t0h_ref)
    for k in range(2):
        v = total[k * rows : (k + 1) * rows]
        v = v + jnp.where(row == 0, lo[2 + k : 3 + k, :], 0.0) + jnp.where(row == rows - 1, hi[2 + k : 3 + k, :], 0.0)
        field.append(ocean * v)
        t0_ref[k] = field[k]
        above = lo_misc[0, 1, 3:4, :] * (lo[k : k + 1, :] + total[2 * rows + 2 + k : 2 * rows + 3 + k])
        below = hi_misc[0, 0, 3:4, :] * (hi[k : k + 1, :] + total[2 * rows + k : 2 * rows + 1 + k])
        halo.append((above, below))
        t0h_ref[k : k + 1, :] = above
        t0h_ref[2 + k : 3 + k, :] = below
    damping = damping_of(*field)[3]
    damp_lo = damping_of(halo[0][0], halo[1][0])[3]
    damp_hi = damping_of(halo[0][1], halo[1][1])[3]
    energy, moment = jnp.zeros((rows, nc), F32), jnp.zeros((rows, nc), F32)
    for j in range(nf):
        rj, w, q, wf = [coef(tab, j, nf, k) for k in (1, 2, 3, 4)]
        h = gate(q, white[...], damping, ocean)
        h_lo = gate(q, lo_misc[0, 1, 4:5, :], damp_lo, lo_misc[0, 1, 3:4, :])
        h_hi = gate(q, hi_misc[0, 0, 4:5, :], damp_hi, hi_misc[0, 0, 3:4, :])
        h0_ref[j] = h
        h0h_ref[j, 0:1, :] = h_lo
        h0h_ref[j, 1:2, :] = h_hi
        centre, around = advected_sum(
            rj, h, h_lo * sy_ref[j, 0:1, :], h_hi * sy_ref[j, 1:2, :], [sum_ref[k, j] for k in range(5)]
        )
        adv = centre + around
        energy, moment = energy + w * adv, moment + wf * adv
    t1_ref[0:rows, :] = energy
    t1_ref[rows : 2 * rows, :] = moment


def gathered(rj, h, h_lo, h_hi, r):
    return h * r[0] + rj * (
        shift_x(h, True) * r[1] + shift_x(h, False) * r[2] + from_before(h, h_lo) * r[3] + from_after(h, h_hi) * r[4]
    )


def second_kernel(nf, n, tab, *refs):
    parts, (mask, white, h0_ref, h0h_ref, r_ref, t1_ref, h1_ref, d1_ref) = refs[:n], refs[n:]
    rows, nc = mask.shape
    ocean = mask[...].astype(F32)
    total = parts[0][...]
    for part in parts[1:]:
        total = total + part[...]
    energy, moment = ocean * total[:rows], ocean * total[rows:]
    t1_ref[0] = energy
    t1_ref[1] = moment
    damping = damping_of(energy, moment)[3]
    acc = jnp.zeros((rows, nc), F32)
    for j in range(nf):
        rj, q = coef(tab, j, nf, 1), coef(tab, j, nf, 3)
        h1 = gate(q, white[...], damping, ocean)
        h1_ref[j] = h1
        part = gathered(rj, h0_ref[j], h0h_ref[j, 0:1, :], h0h_ref[j, 1:2, :], [r_ref[k, j] for k in range(5)])
        acc = acc + q * (h1 * part)
    d1_ref[...] = acc


def third_kernel(nf, n, tab, *refs):
    parts = refs[:n]
    mask, white, speed, t1, h0_ref, h0h_ref, h1_ref, sum_ref, sy_ref, r_ref, t_ref = refs[n : n + 11]
    d1_ref, v1_ref, d0_ref, f1_ref, up, dn = refs[n + 11 :]
    rows, nc = mask.shape
    ocean = mask[...].astype(F32)
    damp = parts[0][...]
    for part in parts[1:]:
        damp = damp + part[...]
    d1_ref[...] = damp
    up[...] = jnp.zeros_like(up)
    dn[...] = jnp.zeros_like(dn)
    for k, v in enumerate((t1[0], t1[1], damp)):
        up[2 * k : 2 * k + 2, :] = v[rows - 2 : rows]
        dn[2 * k : 2 * k + 2, :] = v[0:2]
    grad_e, grad_m, _ = grads_of(t1[0], t1[1], white[...], damp)
    acc, force = jnp.zeros((rows, nc), F32), jnp.zeros((rows, nc), F32)
    push_lo, push_hi = jnp.zeros((1, nc), F32), jnp.zeros((1, nc), F32)
    for j in range(nf):
        fr, rj, w, q = [coef(tab, j, nf, k) for k in range(4)]
        h0, h1 = h0_ref[j], h1_ref[j]
        h_lo, h_hi = h0h_ref[j, 0:1, :], h0h_ref[j, 1:2, :]
        v1 = ocean * (w * (grad_e + fr * grad_m))
        v1_ref[j] = v1
        s, r = [sum_ref[k, j] for k in range(5)], [r_ref[k, j] for k in range(5)]
        inner = (
            shift_x(h1 * r[1], False)
            + shift_x(h1 * r[2], True)
            + from_after(h1 * r[3], 0.0)
            + from_before(h1 * r[4], 0.0)
            + s[1] * shift_x(v1, False)
            + s[2] * shift_x(v1, True)
            + s[3] * from_after(v1, 0.0)
            + s[4] * from_before(v1, 0.0)
        )
        acc = acc + q * (h0 * (h1 * r[0] + v1 * s[0] + rj * inner))
        push_lo = push_lo + (q * rj) * (h_lo * (h1[0:1] * r[3][0:1] + v1[0:1] * sy_ref[j, 0:1, :]))
        e = rows - 1
        push_hi = push_hi + (q * rj) * (
            h_hi * (h1[e : e + 1] * r[4][e : e + 1] + v1[e : e + 1] * sy_ref[j, 1:2, :])
        )
        part = gathered(rj, h0, h_lo, h_hi, [t_ref[k, j] for k in range(5)])
        force = force + fr * (h1 * part)
    d0_ref[0:rows, :] = acc
    d0_ref[rows:, :] = jnp.zeros_like(d0_ref[rows:, :])
    d0_ref[rows : rows + 1, :] = push_lo
    d0_ref[rows + 1 : rows + 2, :] = push_hi
    f1_ref[...] = (speed[...] / HIGHEST) * force


def back_kernel(nf, tab, dirs, p_ref, u_ref, g_ref, al_ref, h0_ref, h0h_ref, h1_ref, v1_ref, pl_ref, ph_ref, lo_misc, hi_misc, lo, hi, f1_ref, speed, z_ref, zl_ref, zh_ref, f_ref, edge, halo):
    j = pl.program_id(0)
    rows, nc = speed.shape
    fr, rj, w, q = [coef(tab, j, nf, k) for k in range(4)]
    for side, (half, blk, misc, got, near, far, h0, out) in enumerate(
        ((0, ph_ref, hi_misc, hi, 0, 1, h0h_ref[0, 1:2, :], zh_ref), (1, pl_ref, lo_misc, lo, 1, 0, h0h_ref[0, 0:1, :], zl_ref))
    ):

        @pl.when(j == 0)
        def _():
            for r in range(2):
                energy, moment, damp = [got[2 * k + r : 2 * k + r + 1, :] for k in range(3)]
                white = misc[0, r, 4:5, :]
                grad_e, grad_m, damping = grads_of(energy, moment, white, damp)
                for k, v in enumerate((grad_e, grad_m, white * damping)):
                    halo[side, r, k : k + 1, :] = v

        rows_out = []
        for r in range(2):
            ocean = misc[0, r, 3:4, :]
            h1 = gate(q, halo[side, r, 2:3, :], 1.0, ocean)
            v1 = ocean * (w * (halo[side, r, 0:1, :] + fr * halo[side, r, 1:2, :]))
            rows_out.append(blk[0, r] * h1 + v1)
        edge[side] = rows_out[near]
        back = halo_adv(rj, dirs, half, rows_out[near], rows_out[far], True)
        out[0] = back * halo_growth(fr, dirs, half, misc, near) * h0

    @pl.when(j == 0)
    def _():
        f_ref[...] = jnp.zeros_like(f_ref)

    zero = jnp.zeros((8, nc), F32)
    for t in range(0, rows, 8):
        h0, h1, v1 = h0_ref[0, t : t + 8, :], h1_ref[0, t : t + 8, :], v1_ref[0, t : t + 8, :]
        force = zero
        for d in range(ND):
            cx, cy = float(KX[d]) * rj, float(KY[d]) * rj
            x = p_ref[0, d, t : t + 8, :] * h1 + v1
            if YP[d]:
                if t + 8 == rows:
                    row = edge[0, d : d + 1, :]
                else:
                    n = t + 8
                    row = p_ref[0, d, n : n + 1, :] * h1_ref[0, n : n + 1, :] + v1_ref[0, n : n + 1, :]
            elif t == 0:
                row = edge[1, d - NL : d - NL + 1, :]
            else:
                n = t - 1
                row = p_ref[0, d, n : n + 1, :] * h1_ref[0, n : n + 1, :] + v1_ref[0, n : n + 1, :]
            back = (1.0 - cx - cy) * x + cx * shift_x(x, not XP[d]) + cy * shift_y(x, not YP[d], row)
            force = force + al_ref[d, t : t + 8, :] * (back * u_ref[0, d, t : t + 8, :])
            z_ref[0, d, t : t + 8, :] = back * (g_ref[0, d, t : t + 8, :] * h0)
        f_ref[t : t + 8, :] += fr * (h0 * force)

    @pl.when(j == nf - 1)
    def _():
        f_ref[...] = (speed[...] / HIGHEST) * f_ref[...] + f1_ref[...]


def fourth_kernel(rows, *refs):
    parts, (tot, up, dn) = refs[:-3], refs[-3:]
    total = parts[0][...]
    for part in parts[1:]:
        total = total + part[...]
    tot[...] = total
    up[...] = jnp.zeros_like(up)
    dn[...] = jnp.zeros_like(dn)
    up[0:1, :] = total[rows - 1 : rows]
    up[1:2, :] = total[rows + 1 : rows + 2]
    dn[0:1, :] = total[0:1]
    dn[1:2, :] = total[rows : rows + 1]


def out_kernel(nf, tab, z_ref, zl_ref, zh_ref, tot, lo, hi, t0, t0h, t1, d1, mask, white, lo_misc, hi_misc, out_ref, gw_ref, own, halo, edge):
    j = pl.program_id(0)
    rows, nc = mask.shape
    fr, rj, w = [coef(tab, j, nf, k) for k in range(3)]
    ocean = mask[...].astype(F32)

    @pl.when(j == 0)
    def _():
        row = lax.broadcasted_iota(jnp.int32, (rows, nc), 0)
        damp = tot[0:rows, :]
        damp = damp + jnp.where(row == 0, lo[1:2, :], 0.0) + jnp.where(row == rows - 1, hi[1:2, :], 0.0)
        grad_e, grad_m, damping = grads_of(t0[0], t0[1], white[...], damp)
        own[0] = grad_e
        own[1] = grad_m
        gw_ref[...] = -time_step * (damping * damp + damping_of(t1[0], t1[1])[3] * d1[...])
        above = lo[0:1, :] + tot[rows : rows + 1, :]
        below = hi[0:1, :] + tot[rows + 1 : rows + 2, :]
        e, m, _ = grads_of(t0h[0:1, :], t0h[1:2, :], lo_misc[0, 1, 4:5, :], above)
        halo[0, 0:1, :] = e
        halo[0, 1:2, :] = m
        e, m, _ = grads_of(t0h[2:3, :], t0h[3:4, :], hi_misc[0, 0, 4:5, :], below)
        halo[1, 0:1, :] = e
        halo[1, 1:2, :] = m

    v_lo = lo_misc[0, 1, 3:4, :] * (w * (halo[0, 0:1, :] + fr * halo[0, 1:2, :]))
    v_hi = hi_misc[0, 0, 3:4, :] * (w * (halo[1, 0:1, :] + fr * halo[1, 1:2, :]))
    edge[0] = zh_ref[0] + v_hi
    edge[1] = zl_ref[0] + v_lo
    v = ocean * (w * (own[0] + fr * own[1]))
    for t in range(0, rows, 8):
        ot, vt = ocean[t : t + 8], v[t : t + 8]
        for d in range(ND):
            cx, cy = float(KX[d]) * rj, float(KY[d]) * rj
            x = z_ref[0, d, t : t + 8, :] + vt
            if YP[d]:
                if t + 8 == rows:
                    row = edge[0, d : d + 1, :]
                else:
                    row = z_ref[0, d, t + 8 : t + 9, :] + v[t + 8 : t + 9]
            elif t == 0:
                row = edge[1, d - NL : d - NL + 1, :]
            else:
                row = z_ref[0, d, t - 1 : t, :] + v[t - 1 : t]
            back = (1.0 - cx - cy) * x + cx * shift_x(x, not XP[d]) + cy * shift_y(x, not YP[d], row)
            out_ref[0, d, t : t + 8, :] = ot * back


def whole(shape):
    return pl.BlockSpec(shape, lambda *_: (0,) * len(shape))


def part(shape, axis=0):
    block = list(shape)
    block[axis] = 1
    return pl.BlockSpec(tuple(block), lambda j: tuple(j if k == axis else 0 for k in range(len(shape))))


def at(shape, index):
    return pl.BlockSpec((1,) + tuple(shape[1:]), lambda *_: (index,) + (0,) * (len(shape) - 1))


def spaces():
    return pl.BlockSpec(memory_space=pltpu.SMEM)


def f32(*shape):
    return jax.ShapeDtypeStruct(shape, F32)


def cost(flops, size):
    return pl.CostEstimate(flops=int(flops), bytes_accessed=int(size), transcendentals=0)


def small(kernel, name, outs, *args):
    return pl.pallas_call(
        kernel,
        name=name,
        grid=(1,),
        out_shape=outs,
        in_specs=[spaces() if a.ndim == 1 else whole(a.shape) if s is None else s for a, s in args],
        out_specs=[whole(o.shape) for o in outs],
        compiler_params=pltpu.CompilerParams(vmem_limit_bytes=32 * MIB),
        cost_estimate=cost(4e6, 4e6),
    )(*[a for a, _ in args])


def heavy(kernel, name, nf, outs, args, scratch=(), flops=1e8, size=3e7):
    return pl.pallas_call(
        kernel,
        name=name,
        grid=(nf,),
        out_shape=[o for o, _ in outs],
        in_specs=[s for _, s in args],
        out_specs=[s for _, s in outs],
        scratch_shapes=list(scratch),
        compiler_params=pltpu.CompilerParams(vmem_limit_bytes=32 * MIB, dimension_semantics=("arbitrary",)),
        cost_estimate=cost(flops, size),
    )(*[a for a, _ in args])


def peers(x):
    n = lax.axis_size("spec")
    if n & (n - 1) == 0:
        return [lax.ppermute(x, "spec", [(i, i ^ k) for i in range(n)]) for k in range(1, n)]
    return [lax.ppermute(x, "spec", [(i, (i + k) % n) for i in range(n)]) for k in range(1, n)]


def exchange(up, dn):
    n = lax.axis_size("cells")
    lo = lax.ppermute(up, "cells", [(i, i + 1) for i in range(n - 1)])
    hi = lax.ppermute(dn, "cells", [(i + 1, i) for i in range(n - 1)])
    return lo, hi


def shards(spectrum_start, input_coef, white_coef, wind_speed, wind_angle, sea_mask, cotangent):
    nf, _, rows, nc = spectrum_start.shape
    n = lax.axis_size("spec")
    tab, dirs = jnp.asarray(TABLE), jnp.asarray(DIRS)
    big, flat = (nf, ND, rows, nc), (rows, nc)
    tab_s, flat_s, dirs_s = (tab, spaces()), whole(flat), (dirs, whole(dirs.shape))
    mask, white, speed = (sea_mask, flat_s), (white_coef, flat_s), (wind_speed, flat_s)
    vm = lambda a: (a, None)
    band = (nf + 1, 2, NL, nc)
    edge = (nf, 2, NL, nc)

    t0_part, s_up, s_dn = heavy(
        functools.partial(start_kernel, nf),
        "start",
        nf,
        [(f32(2 * rows + 8, nc), whole((2 * rows + 8, nc))), (f32(*band), whole(band)), (f32(*band), whole(band))],
        [tab_s, (spectrum_start, part(big)), mask, (input_coef, flat_s), white, speed, (wind_angle, flat_s)],
        [pltpu.VMEM((5, rows, nc), F32)],
    )
    t0_parts = [t0_part] + peers(t0_part)
    s_lo, s_hi = exchange(s_up, s_dn)

    g, p, al, p_up, p_dn = heavy(
        functools.partial(wind_kernel, nf),
        "wind",
        nf,
        [
            (f32(*big), part(big)),
            (f32(*big), part(big)),
            (f32(ND, rows, nc), whole((ND, rows, nc))),
            (f32(*edge), part(edge)),
            (f32(*edge), part(edge)),
        ],
        [tab_s, (cotangent, part(big)), (input_coef, flat_s), speed, (wind_angle, flat_s)],
        [pltpu.VMEM((ND, rows, nc), F32)],
    )

    tot0, e_up, e_dn = small(
        functools.partial(total_kernel, rows), "total", [f32(2 * rows + 8, nc), f32(8, nc), f32(8, nc)], *map(vm, t0_parts)
    )
    e_lo, e_hi = exchange(e_up, e_dn)
    p_lo, p_hi = exchange(p_up, p_dn)

    sums, prod = (5, nf, rows, nc), (5, nf, rows, nc)
    line = (nf, NL, nc)
    duo = (nf, 8, nc)
    misc = [(s_lo, at(band, nf)), (s_hi, at(band, nf))]
    u, s5, u_lo, u_hi, sy = heavy(
        functools.partial(grown_kernel, nf),
        "grown",
        nf,
        [(f32(*big), part(big)), (f32(*sums), part(sums, 1)), (f32(*line), part(line)), (f32(*line), part(line)), (f32(*duo), part(duo))],
        [tab_s, dirs_s, (spectrum_start, part(big)), mask, (g, part(big)), (s_lo, part(band)), misc[0], (s_hi, part(band)), misc[1]],
    )
    mlo, mhi = misc
    t0, t0h, h0, h0h, t1_part = small(
        functools.partial(first_kernel, nf),
        "first",
        [f32(2, rows, nc), f32(8, nc), f32(nf, rows, nc), f32(*duo), f32(2 * rows, nc)],
        vm(tab), vm(tot0), vm(e_lo), vm(e_hi), mlo, mhi, vm(sea_mask), vm(white_coef), vm(s5), vm(sy),
    )
    t1_parts = [t1_part] + peers(t1_part)

    r5, t5 = heavy(
        functools.partial(product_kernel, nf),
        "product",
        nf,
        [(f32(*prod), part(prod, 1)), (f32(*prod), part(prod, 1))],
        [tab_s, (u, part(big)), (p, part(big)), (al, whole((ND, rows, nc))), (u_lo, part(line)), (u_hi, part(line))],
    )
    t1, h1, d1_part = small(
        functools.partial(second_kernel, nf, n),
        "second",
        [f32(2, rows, nc), f32(nf, rows, nc), f32(rows, nc)],
        vm(tab), *map(vm, t1_parts), vm(sea_mask), vm(white_coef), vm(h0), vm(h0h), vm(r5),
    )
    d1_parts = [d1_part] + peers(d1_part)
    d1, v1, d0_part, f1, b_up, b_dn = small(
        functools.partial(third_kernel, nf, n),
        "third",
        [f32(rows, nc), f32(nf, rows, nc), f32(rows + 8, nc), f32(rows, nc), f32(8, nc), f32(8, nc)],
        vm(tab), *map(vm, d1_parts), vm(sea_mask), vm(white_coef), vm(wind_speed), vm(t1), vm(h0), vm(h0h), vm(h1), vm(s5), vm(sy), vm(r5), vm(t5),
    )
    d0_parts = [d0_part] + peers(d0_part)
    b_lo, b_hi = exchange(b_up, b_dn)

    hs = (nf, rows, nc)
    z, z_lo, z_hi, f_part = heavy(
        functools.partial(back_kernel, nf),
        "back",
        nf,
        [(f32(*big), part(big)), (f32(*line), part(line)), (f32(*line), part(line)), (f32(rows, nc), flat_s)],
        [
            tab_s, dirs_s, (p, part(big)), (u, part(big)), (g, part(big)), (al, whole((ND, rows, nc))),
            (h0, part(hs)), (h0h, part(duo)), (h1, part(hs)), (v1, part(hs)), (p_lo, part(edge)), (p_hi, part(edge)),
            mlo, mhi, (b_lo, whole((8, nc))), (b_hi, whole((8, nc))), (f1, flat_s), speed,
        ],
        [pltpu.VMEM((2, NL, nc), F32), pltpu.VMEM((2, 2, 8, nc), F32)],
    )
    f_parts = [f_part] + peers(f_part)

    tot, c_up, c_dn = small(
        functools.partial(fourth_kernel, rows), "fourth", [f32(rows + 8, nc), f32(8, nc), f32(8, nc)], *map(vm, d0_parts)
    )
    c_lo, c_hi = exchange(c_up, c_dn)
    out, grad_white = heavy(
        functools.partial(out_kernel, nf),
        "out",
        nf,
        [(f32(*big), part(big)), (f32(rows, nc), flat_s)],
        [
            tab_s, (z, part(big)), (z_lo, part(line)), (z_hi, part(line)), (tot, whole((rows + 8, nc))), (c_lo, whole((8, nc))),
            (c_hi, whole((8, nc))), (t0, whole((2, rows, nc))), (t0h, whole((8, nc))), (t1, whole((2, rows, nc))), (d1, flat_s),
            mask, white, mlo, mhi,
        ],
        [pltpu.VMEM((2, rows, nc), F32), pltpu.VMEM((2, 8, nc), F32), pltpu.VMEM((2, NL, nc), F32)],
    )
    grad_input = f_parts[0]
    for other in f_parts[1:]:
        grad_input = grad_input + other
    return out, time_step * grad_input, grad_white


def solution(mesh):
    return jax.shard_map(
        shards,
        mesh=mesh,
        in_specs=(
            P("spec", None, "cells", None),
            P("cells", None),
            P("cells", None),
            P("cells", None),
            P("cells", None),
            P("cells", None),
            P("spec", None, "cells", None),
        ),
        out_specs=(P("spec", None, "cells", None), P("cells", None), P("cells", None)),
        check_vma=False,
    )
```

```python
import functools
import math

import jax
import jax.numpy as jnp
import numpy as np
from jax import lax
from jax.experimental import pallas as pl
from jax.experimental.pallas import tpu as pltpu
from jax.sharding import PartitionSpec as P

NF = 32
ND = 36
STEPS = 2

epsilon = 1e-06
energy_ref = 0.5
time_step = 0.5
courant = 0.7
ratio_step = 1.1

F32 = jnp.float32
LOG2E = math.log2(math.e)

_every = np.exp(np.arange(NF, dtype=np.float32) * np.float32(math.log(ratio_step))).astype(np.float32)
_total = _every.sum(dtype=np.float32)
HIGHEST = float(_every[-1])
MEAN_RATIO = float((_every * _every).sum(dtype=np.float32) / _total)
_weights = _every / (np.float32(ND) * _total)
_q = (_every / _every[-1]) ** 2
NTAB = 5
TABLE = np.stack([_every, 1 / _every, _weights, _q, _weights * _every], axis=1).astype(np.float32).reshape(-1)

_angle = (np.float32(2.0 * math.pi) * np.arange(ND, dtype=np.float32) / np.float32(ND)).astype(np.float32)
COS, SIN = np.cos(_angle).astype(np.float32), np.sin(_angle).astype(np.float32)
KX, KY = np.float32(courant) * np.abs(COS), np.float32(courant) * np.abs(SIN)
XP, YP = [bool(c >= 0) for c in COS], [bool(s >= 0) for s in SIN]
NL = sum(YP)
NH = ND - NL
assert YP == [True] * NL + [False] * NH and NL == NH
QUADS = [[d for d in range(ND) if (XP[d], YP[d]) == quad] for quad in ((1, 1), (0, 1), (0, 0), (1, 0))]
DIRS = np.stack([v[a:b] for a, b in ((0, NL), (NL, ND)) for v in (KX, KY, COS, SIN)]).astype(np.float32)
DIRS = np.ascontiguousarray(np.broadcast_to(DIRS[:, :, None], DIRS.shape + (128,)))
MISC = 2 * NL
MROWS = 4
NMISC = 5

MIB = 1 << 20


def coef(tab, j, nf, which):
    return tab[(lax.axis_index("spec") * nf + j) * NTAB + which]


def shift_x(x, plus):
    return pltpu.roll(x, 1 if plus else x.shape[1] - 1, 1)


def first_row(x):
    return lax.broadcasted_iota(jnp.int32, x.shape, 0) == 0


def last_row(x):
    return lax.broadcasted_iota(jnp.int32, x.shape, 0) == x.shape[0] - 1


def from_before(x, above):
    return jnp.where(first_row(x), above, pltpu.roll(x, 1, 0))


def from_after(x, below):
    return jnp.where(last_row(x), below, pltpu.roll(x, x.shape[0] - 1, 0))


def shift_y(x, plus, outside):
    return from_before(x, outside) if plus else from_after(x, outside)


def damping_of(energy, moment):
    shifted = energy + epsilon
    ratio = moment / (shifted * MEAN_RATIO)
    r2 = ratio * ratio
    steep = energy * (r2 * r2) / energy_ref
    return shifted, ratio, steep, steep * steep * ratio


def grads_of(energy, moment, white, damp_total):
    shifted, ratio, steep, damping = damping_of(energy, moment)
    grad_damp = -time_step * white * damp_total
    grad_ratio = 9.0 * grad_damp * steep * steep
    r2 = ratio * ratio
    grad_energy = grad_damp * 2.0 * steep * (r2 * r2) * ratio / energy_ref - grad_ratio * ratio / shifted
    grad_moment = grad_ratio / (shifted * MEAN_RATIO)
    return grad_energy, grad_moment, damping


def gate(q, white, damping, ocean):
    return ocean * jnp.exp2((-time_step * LOG2E) * q * (white * damping))


def rows_from(tiles, plus, outside):
    moved = [pltpu.roll(x, 1 if plus else 7, 0) for x in tiles]
    mark = first_row(tiles[0]) if plus else last_row(tiles[0])
    feed = [outside] + moved[:-1] if plus else moved[1:] + [outside]
    return [jnp.where(mark, a, b) for a, b in zip(feed, moved)]


def slab(ref, *index):
    return [ref[(*index, slice(t, t + 8))] for t in range(0, ref.shape[-2], 8)]


def misc_at(r, k):
    m = r * NMISC + k
    return m // MROWS, MISC + m % MROWS


def misc_row(ref, r, k):
    j, row = misc_at(r, k)
    return ref[j, row : row + 1, :]


def halo_rows(ref, j, r):
    return ref[j, r * NL : (r + 1) * NL, :]


def copies(hbm, buf, sem, count, n):
    def make(j):
        return pltpu.make_async_copy(hbm.at[j], buf.at[j % n], sem.at[j % n])

    return make


NBUF = 3


def start_kernel(s_hbm, mask_h, coef_h, white_h, speed_h, angle_h, t0_ref, up_ref, dn_ref, buf, sems, fields, ints, small_sems, sums):
    nf = s_hbm.shape[0]
    rows, nc = ints.shape
    fetch = copies(s_hbm, buf, sems, nf, NBUF)
    for j in range(NBUF):
        fetch(j).start()
    smalls = [pltpu.make_async_copy(mask_h, ints, small_sems.at[0])]
    for k, f in enumerate((coef_h, white_h, speed_h, angle_h)):
        smalls.append(pltpu.make_async_copy(f, fields.at[k], small_sems.at[1 + k]))
    for c in smalls:
        c.start()
    t0_ref[...] = jnp.zeros_like(t0_ref)
    for c in smalls:
        c.wait()

    @pl.loop(0, nf)
    def _(j):
        up_ref[j, MISC:, :] = jnp.zeros_like(up_ref[j, MISC:, :])
        dn_ref[j, MISC:, :] = jnp.zeros_like(dn_ref[j, MISC:, :])

    kappa = (time_step * LOG2E / HIGHEST) * (fields[0] * fields[2])
    angle = fields[3]
    for k, v in enumerate((kappa, jnp.cos(angle), jnp.sin(angle), ints[...].astype(F32), fields[1])):
        for r in range(2):
            a, b = misc_at(r, k)
            up_ref[a, b : b + 1, :] = v[rows - 2 + r : rows - 1 + r]
            dn_ref[a, b : b + 1, :] = v[r : r + 1]

    @pl.loop(0, nf)
    def _(j):
        slot = j % NBUF
        fetch(j).wait()
        for t in range(0, rows, 8):
            acc = [None] * 5

            def add(k, v):
                acc[k] = v if acc[k] is None else acc[k] + v

            for d in range(ND):
                x = buf[slot, d, t : t + 8, :]
                add(0, x)
                add(1 if XP[d] else 2, float(KX[d]) * x)
                add(3 if YP[d] else 4, float(KY[d]) * x)
            for k in range(5):
                sums[k, t : t + 8, :] = acc[k]
        for r in range(2):
            for d in range(NL):
                up_ref[j, r * NL + d : r * NL + d + 1, :] = buf[slot, d, rows - 2 + r : rows - 1 + r, :]
                dn_ref[j, r * NL + d : r * NL + d + 1, :] = buf[slot, NL + d, r : r + 1, :]

        @pl.when(j + NBUF < nf)
        def _():
            fetch(j + NBUF).start()

        ocean = ints[...].astype(F32)
        index = lax.axis_index("spec") * nf + j
        fr = jnp.exp(jnp.full((rows, nc), index, jnp.int32).astype(F32) * math.log(ratio_step))
        rj, w = 1.0 / fr, float(_weights[0]) * fr
        wf = w * fr
        total, xp, xm, yp, ym = [ocean * sums[k] for k in range(5)]
        adv = total + rj * (
            shift_x(xp, True) + shift_x(xm, False) + from_before(yp, 0.0) + from_after(ym, 0.0) - (xp + xm + yp + ym)
        )
        t0_ref[0:rows, :] += w * adv
        t0_ref[rows : 2 * rows, :] += wf * adv
        wj, mj, rj = w[0:1], wf[0:1], rj[0:1]
        push_up, push_dn = rj * yp[rows - 1 : rows], rj * ym[0:1]
        for k, v in enumerate((wj * push_up, mj * push_up, wj * push_dn, mj * push_dn)):
            t0_ref[2 * rows + k : 2 * rows + k + 1, :] += v


def wind_kernel(tab, lam_hbm, coef_in, speed, angle, g_ref, p_ref, al_ref, up_ref, dn_ref, buf, sems, expo):
    nf = lam_hbm.shape[0]
    rows, nc = angle.shape
    fetch = copies(lam_hbm, buf, sems, nf, NBUF)
    for j in range(NBUF):
        fetch(j).start()
    up_ref[:, MISC:, :] = jnp.zeros_like(up_ref[:, MISC:, :])
    dn_ref[:, MISC:, :] = jnp.zeros_like(dn_ref[:, MISC:, :])
    kappa = (time_step * LOG2E / HIGHEST) * (coef_in[...] * speed[...])
    ca, sa = jnp.cos(angle[...]), jnp.sin(angle[...])
    for d in range(ND):
        align = jnp.maximum(float(COS[d]) * ca + float(SIN[d]) * sa, 0.0)
        al = align * align
        al_ref[d] = al
        expo[d] = kappa * al

    @pl.loop(0, nf)
    def _(j):
        slot = j % NBUF
        fr = coef(tab, j, nf, 0)
        fetch(j).wait()
        for d in range(ND):
            g = jnp.exp2(fr * expo[d])
            p = g * buf[slot, d]
            g_ref[j, d] = g
            p_ref[j, d] = p
            for r in range(2):
                if d < NL:
                    dn_ref[j, r * NL + d : r * NL + d + 1, :] = p[r : r + 1]
                else:
                    up_ref[j, r * NL + d - NL : r * NL + d - NL + 1, :] = p[rows - 2 + r : rows - 1 + r]

        @pl.when(j + NBUF < nf)
        def _():
            fetch(j + NBUF).start()


def halo_growth(fr, dirs, half, misc, r):
    cosd, sind = dirs[4 * half + 2][:, 0:1], dirs[4 * half + 3][:, 0:1]
    align = jnp.maximum(cosd * misc_row(misc, r, 1) + sind * misc_row(misc, r, 2), 0.0)
    return jnp.exp2(fr * (misc_row(misc, r, 0) * (align * align)))


def halo_adv(rj, dirs, half, near, far, transpose):
    kx, ky, cosd = [dirs[4 * half + k][:, 0:1] for k in range(3)]
    before, after = shift_x(near, not transpose), shift_x(near, transpose)
    moved = jnp.where(cosd >= 0, before, after)
    return near + rj * (kx * (moved - near) + ky * (far - near))


def grown_kernel(tab, dirs, s_hbm, mask, g_ref, lo, hi, u_ref, sum_ref, ul_ref, uh_ref, sy_ref, buf, sems):
    nf = s_hbm.shape[0]
    rows, nc = mask.shape
    fetch = copies(s_hbm, buf, sems, nf, NBUF)
    for j in range(NBUF):
        fetch(j).start()
    ocean = mask[...].astype(F32)
    o_lo, o_hi = misc_row(lo, 1, 3), misc_row(hi, 0, 3)

    @pl.loop(0, nf)
    def _(j):
        slot = j % NBUF
        fr, rj = coef(tab, j, nf, 0), coef(tab, j, nf, 1)
        for half, (blk, near, far, out) in enumerate(((lo, 1, 0, ul_ref), (hi, 0, 1, uh_ref))):
            o_near, o_far = misc_row(blk, near, 3), misc_row(blk, far, 3)
            adv = halo_adv(rj, dirs, half, o_near * halo_rows(blk, j, near), o_far * halo_rows(blk, j, far), False)
            u = halo_growth(fr, dirs, half, blk, near) * adv
            out[j] = u
            sy_ref[half, pl.ds(j, 1), :] = jnp.sum(dirs[4 * half + 1][:, 0:1] * u, axis=0, keepdims=True)
        fetch(j).wait()
        tiles = range(rows // 8)
        oj = [rj * ocean[8 * t : 8 * t + 8] for t in tiles]
        o_out = rj * o_lo, rj * o_hi
        acc = [[None] * 5 for _ in tiles]
        for d in range(ND):
            kx, ky = float(KX[d]), float(KY[d])
            x = [o * v for o, v in zip(oj, slab(buf, slot, d))]
            if YP[d]:
                row = o_out[0] * lo[j, NL + d : NL + d + 1, :]
            else:
                row = o_out[1] * hi[j, d - NL : d - NL + 1, :]
            y = rows_from(x, YP[d], row)
            for t in tiles:
                u = g_ref[j, d, 8 * t : 8 * t + 8, :] * (
                    (fr - (kx + ky)) * x[t] + kx * shift_x(x[t], XP[d]) + ky * y[t]
                )
                u_ref[j, d, 8 * t : 8 * t + 8, :] = u
                for k, v in ((0, u), (1 if XP[d] else 2, kx * u), (3 if YP[d] else 4, ky * u)):
                    acc[t][k] = v if acc[t][k] is None else acc[t][k] + v

        @pl.when(j + NBUF < nf)
        def _():
            fetch(j + NBUF).start()

        for t in tiles:
            total, sxp, sxm, syp, sym = acc[t]
            for k, v in enumerate((total - rj * (sxp + sxm + syp + sym), sxp, sxm, syp, sym)):
                sum_ref[k, j, 8 * t : 8 * t + 8, :] = v


def product_kernel(tab, u_ref, p_ref, al_ref, ul_ref, uh_ref, r_ref, t_ref):
    nf, _, rows, nc = u_ref.shape

    @pl.loop(0, nf)
    def _(j):
        rj = coef(tab, j, nf, 1)
        for t in range(0, rows, 8):
            out = {}
            for quad in QUADS:
                acc = [None] * 8
                for d in quad:
                    kx, ky = float(KX[d]), float(KY[d])
                    u, p, al = u_ref[j, d, t : t + 8, :], p_ref[j, d, t : t + 8, :], al_ref[d, t : t + 8, :]
                    if YP[d]:
                        row = ul_ref[j, d : d + 1, :] if t == 0 else u_ref[j, d, t - 1 : t, :]
                        y = jnp.where(first_row(u), row, pltpu.roll(u, 1, 0))
                    else:
                        row = uh_ref[j, d - NL : d - NL + 1, :] if t + 8 == rows else u_ref[j, d, t + 8 : t + 9, :]
                        y = jnp.where(last_row(u), row, pltpu.roll(u, 7, 0))
                    pu, px, py = p * u, kx * (p * shift_x(u, XP[d])), ky * (p * y)
                    apu = al * pu
                    for k, v in enumerate(
                        (pu, (kx + ky) * pu, px, py, apu, (kx + ky) * apu, al * px, al * py)
                    ):
                        acc[k] = v if acc[k] is None else acc[k] + v
                xk, yk = (1 if XP[quad[0]] else 2), (3 if YP[quad[0]] else 4)
                for b in (0, 4):
                    for key, v in ((0, acc[b] - rj * acc[b + 1]), (xk, acc[b + 2]), (yk, acc[b + 3])):
                        out[b, key] = out[b, key] + v if (b, key) in out else v
            for k in range(5):
                r_ref[k, j, t : t + 8, :] = out[0, k]
                t_ref[k, j, t : t + 8, :] = out[4, k]


def total_kernel(rows, *refs):
    parts, (tot, up, dn) = refs[:-3], refs[-3:]
    total = parts[0][...]
    for part in parts[1:]:
        total = total + part[...]
    tot[...] = total
    up[...] = jnp.zeros_like(up)
    dn[...] = jnp.zeros_like(dn)
    for k, row in enumerate((rows - 1, 2 * rows - 1, 2 * rows, 2 * rows + 1)):
        up[k : k + 1, :] = total[row : row + 1]
    for k, row in enumerate((0, rows, 2 * rows + 2, 2 * rows + 3)):
        dn[k : k + 1, :] = total[row : row + 1]


def advected_sum(rj, h, above, below, s):
    return h * s[0], rj * (
        shift_x(h * s[1], True) + shift_x(h * s[2], False) + from_before(h * s[3], above) + from_after(h * s[4], below)
    )


def first_kernel(nf, tab, tot, lo, hi, lo_misc, hi_misc, mask, white, sum_ref, sy_ref, t0_ref, t0h_ref, h0_ref, h0h_ref, t1_ref):
    rows, nc = mask.shape
    ocean = mask[...].astype(F32)
    row = lax.broadcasted_iota(jnp.int32, (rows, nc), 0)
    total = tot[...]
    field = []
    halo = []
    t0h_ref[...] = jnp.zeros_like(t0h_ref)
    for k in range(2):
        v = total[k * rows : (k + 1) * rows]
        v = v + jnp.where(row == 0, lo[2 + k : 3 + k, :], 0.0) + jnp.where(row == rows - 1, hi[2 + k : 3 + k, :], 0.0)
        field.append(ocean * v)
        t0_ref[k] = field[k]
        above = misc_row(lo_misc, 1, 3) * (lo[k : k + 1, :] + total[2 * rows + 2 + k : 2 * rows + 3 + k])
        below = misc_row(hi_misc, 0, 3) * (hi[k : k + 1, :] + total[2 * rows + k : 2 * rows + 1 + k])
        halo.append((above, below))
        t0h_ref[k : k + 1, :] = above
        t0h_ref[2 + k : 3 + k, :] = below
    damping = damping_of(*field)[3]
    damp_lo = damping_of(halo[0][0], halo[1][0])[3]
    damp_hi = damping_of(halo[0][1], halo[1][1])[3]
    energy, moment = jnp.zeros((rows, nc), F32), jnp.zeros((rows, nc), F32)
    for j in range(nf):
        rj, w, q, wf = [coef(tab, j, nf, k) for k in (1, 2, 3, 4)]
        h = gate(q, white[...], damping, ocean)
        h_lo = gate(q, misc_row(lo_misc, 1, 4), damp_lo, misc_row(lo_misc, 1, 3))
        h_hi = gate(q, misc_row(hi_misc, 0, 4), damp_hi, misc_row(hi_misc, 0, 3))
        h0_ref[j] = h
        h0h_ref[0, j : j + 1, :] = h_lo
        h0h_ref[1, j : j + 1, :] = h_hi
        centre, around = advected_sum(
            rj, h, h_lo * sy_ref[0, j : j + 1, :], h_hi * sy_ref[1, j : j + 1, :], [sum_ref[k, j] for k in range(5)]
        )
        adv = centre + around
        energy, moment = energy + w * adv, moment + wf * adv
    t1_ref[0:rows, :] = energy
    t1_ref[rows : 2 * rows, :] = moment


def gathered(rj, h, h_lo, h_hi, r):
    return h * r[0] + rj * (
        shift_x(h, True) * r[1] + shift_x(h, False) * r[2] + from_before(h, h_lo) * r[3] + from_after(h, h_hi) * r[4]
    )


def second_kernel(nf, n, tab, *refs):
    parts, (mask, white, h0_ref, h0h_ref, r_ref, t1_ref, h1_ref, d1_ref) = refs[:n], refs[n:]
    rows, nc = mask.shape
    ocean = mask[...].astype(F32)
    total = parts[0][...]
    for part in parts[1:]:
        total = total + part[...]
    energy, moment = ocean * total[:rows], ocean * total[rows:]
    t1_ref[0] = energy
    t1_ref[1] = moment
    damping = damping_of(energy, moment)[3]
    acc = jnp.zeros((rows, nc), F32)
    for j in range(nf):
        rj, q = coef(tab, j, nf, 1), coef(tab, j, nf, 3)
        h1 = gate(q, white[...], damping, ocean)
        h1_ref[j] = h1
        part = gathered(rj, h0_ref[j], h0h_ref[0, j : j + 1, :], h0h_ref[1, j : j + 1, :], [r_ref[k, j] for k in range(5)])
        acc = acc + q * (h1 * part)
    d1_ref[...] = acc


def third_kernel(nf, n, tab, *refs):
    parts = refs[:n]
    mask, white, speed, t1, h0_ref, h0h_ref, h1_ref, sum_ref, sy_ref, r_ref, t_ref = refs[n : n + 11]
    d1_ref, v1_ref, d0_ref, f1_ref, up, dn = refs[n + 11 :]
    rows, nc = mask.shape
    ocean = mask[...].astype(F32)
    damp = parts[0][...]
    for part in parts[1:]:
        damp = damp + part[...]
    d1_ref[...] = damp
    up[...] = jnp.zeros_like(up)
    dn[...] = jnp.zeros_like(dn)
    for k, v in enumerate((t1[0], t1[1], damp)):
        up[2 * k : 2 * k + 2, :] = v[rows - 2 : rows]
        dn[2 * k : 2 * k + 2, :] = v[0:2]
    grad_e, grad_m, _ = grads_of(t1[0], t1[1], white[...], damp)
    acc, force = jnp.zeros((rows, nc), F32), jnp.zeros((rows, nc), F32)
    push_lo, push_hi = jnp.zeros((1, nc), F32), jnp.zeros((1, nc), F32)
    for j in range(nf):
        fr, rj, w, q = [coef(tab, j, nf, k) for k in range(4)]
        h0, h1 = h0_ref[j], h1_ref[j]
        h_lo, h_hi = h0h_ref[0, j : j + 1, :], h0h_ref[1, j : j + 1, :]
        v1 = ocean * (w * (grad_e + fr * grad_m))
        v1_ref[j] = v1
        s, r = [sum_ref[k, j] for k in range(5)], [r_ref[k, j] for k in range(5)]
        inner = (
            shift_x(h1 * r[1], False)
            + shift_x(h1 * r[2], True)
            + from_after(h1 * r[3], 0.0)
            + from_before(h1 * r[4], 0.0)
            + s[1] * shift_x(v1, False)
            + s[2] * shift_x(v1, True)
            + s[3] * from_after(v1, 0.0)
            + s[4] * from_before(v1, 0.0)
        )
        acc = acc + q * (h0 * (h1 * r[0] + v1 * s[0] + rj * inner))
        push_lo = push_lo + (q * rj) * (h_lo * (h1[0:1] * r[3][0:1] + v1[0:1] * sy_ref[0, j : j + 1, :]))
        e = rows - 1
        push_hi = push_hi + (q * rj) * (
            h_hi * (h1[e : e + 1] * r[4][e : e + 1] + v1[e : e + 1] * sy_ref[1, j : j + 1, :])
        )
        part = gathered(rj, h0, h_lo, h_hi, [t_ref[k, j] for k in range(5)])
        force = force + fr * (h1 * part)
    d0_ref[0:rows, :] = acc
    d0_ref[rows:, :] = jnp.zeros_like(d0_ref[rows:, :])
    d0_ref[rows : rows + 1, :] = push_lo
    d0_ref[rows + 1 : rows + 2, :] = push_hi
    f1_ref[...] = (speed[...] / HIGHEST) * force


def back_kernel(tab, dirs, p_ref, u_ref, g_ref, al_ref, h0_ref, h0h_ref, h1_ref, v1_ref, pl_ref, ph_ref, lo_misc, hi_misc, lo, hi, f1_ref, speed, z_ref, zl_ref, zh_ref, f_ref, edge, halo):
    nf, _, rows, nc = p_ref.shape
    sides = ((0, ph_ref, hi_misc, hi, 0, 1, 1, zh_ref), (1, pl_ref, lo_misc, lo, 1, 0, 0, zl_ref))
    for side, (_, _, misc, got, *_) in enumerate(sides):
        for r in range(2):
            energy, moment, damp = [got[2 * k + r : 2 * k + r + 1, :] for k in range(3)]
            white = misc_row(misc, r, 4)
            grad_e, grad_m, damping = grads_of(energy, moment, white, damp)
            for k, v in enumerate((grad_e, grad_m, white * damping)):
                halo[side, r, k : k + 1, :] = v
    f_ref[...] = jnp.zeros_like(f_ref)

    @pl.loop(0, nf)
    def _(j):
        fr, rj = coef(tab, j, nf, 0), coef(tab, j, nf, 1)
        w, q = coef(tab, j, nf, 2), coef(tab, j, nf, 3)
        for side, (half, blk, misc, _, near, far, which, out) in enumerate(sides):
            x = []
            for r in range(2):
                ocean = misc_row(misc, r, 3)
                h = gate(q, halo[side, r, 2:3, :], 1.0, ocean)
                v = ocean * (w * (halo[side, r, 0:1, :] + fr * halo[side, r, 1:2, :]))
                x.append(halo_rows(blk, j, r) * h + v)
            edge[side] = x[near]
            moved = halo_adv(rj, dirs, half, x[near], x[far], True) * halo_growth(fr, dirs, half, misc, near)
            out[j] = moved * h0h_ref[which, pl.ds(j, 1), :]
        tiles = range(rows // 8)
        h0, h1, v1 = [slab(ref, j) for ref in (h0_ref, h1_ref, v1_ref)]
        h0 = [rj * h for h in h0]
        force = [None for _ in tiles]
        for d in range(ND):
            kx, ky = float(KX[d]), float(KY[d])
            x = [p * h1[t] + v1[t] for t, p in enumerate(slab(p_ref, j, d))]
            row = edge[0, d : d + 1, :] if YP[d] else edge[1, d - NL : d - NL + 1, :]
            y = rows_from(x, not YP[d], row)
            for t in tiles:
                back = (fr - (kx + ky)) * x[t] + kx * shift_x(x[t], not XP[d]) + ky * y[t]
                at = (j, d, slice(8 * t, 8 * t + 8))
                v = al_ref[d, 8 * t : 8 * t + 8, :] * (back * u_ref[at])
                force[t] = v if force[t] is None else force[t] + v
                z_ref[at] = back * (g_ref[at] * h0[t])
        for t in tiles:
            f_ref[8 * t : 8 * t + 8, :] += fr * (h0[t] * force[t])

    f_ref[...] = (speed[...] / HIGHEST) * f_ref[...] + f1_ref[...]


def fourth_kernel(rows, *refs):
    parts, (tot, up, dn) = refs[:-3], refs[-3:]
    total = parts[0][...]
    for part in parts[1:]:
        total = total + part[...]
    tot[...] = total
    up[...] = jnp.zeros_like(up)
    dn[...] = jnp.zeros_like(dn)
    up[0:1, :] = total[rows - 1 : rows]
    up[1:2, :] = total[rows + 1 : rows + 2]
    dn[0:1, :] = total[0:1]
    dn[1:2, :] = total[rows : rows + 1]


def out_kernel(tab, z_ref, zl_ref, zh_ref, tot, lo, hi, t0, t0h, t1, d1, mask, white, lo_misc, hi_misc, out_hbm, gw_ref, own, halo, edge, buf, sems):
    nf, _, rows, nc = z_ref.shape
    ocean = mask[...].astype(F32)
    row = lax.broadcasted_iota(jnp.int32, (rows, nc), 0)
    damp = tot[0:rows, :]
    damp = damp + jnp.where(row == 0, lo[1:2, :], 0.0) + jnp.where(row == rows - 1, hi[1:2, :], 0.0)
    grad_e, grad_m, damping = grads_of(t0[0], t0[1], white[...], damp)
    own[0] = grad_e
    own[1] = grad_m
    gw_ref[...] = -time_step * (damping * damp + damping_of(t1[0], t1[1])[3] * d1[...])
    above = lo[0:1, :] + tot[rows : rows + 1, :]
    below = hi[0:1, :] + tot[rows + 1 : rows + 2, :]
    sides = ((hi_misc, 0, 2, below, zh_ref), (lo_misc, 1, 0, above, zl_ref))
    for side, (misc, r, k, damp, _) in enumerate(sides):
        e, m, _ = grads_of(t0h[k : k + 1, :], t0h[k + 1 : k + 2, :], misc_row(misc, r, 4), damp)
        halo[side, 0:1, :] = e
        halo[side, 1:2, :] = m

    def put(j):
        return pltpu.make_async_copy(buf.at[j % NBUF], out_hbm.at[j], sems.at[j % NBUF])

    @pl.loop(0, nf)
    def _(j):
        slot = j % NBUF
        fr, rj, w = [coef(tab, j, nf, k) for k in range(3)]
        for side, (misc, r, _, _, z) in enumerate(sides):
            edge[side] = z[j] + misc_row(misc, r, 3) * (w * (halo[side, 0:1, :] + fr * halo[side, 1:2, :]))
        tiles = range(rows // 8)
        o = [ocean[8 * t : 8 * t + 8] for t in tiles]
        v = [o[t] * (w * (own[0, 8 * t : 8 * t + 8] + fr * own[1, 8 * t : 8 * t + 8])) for t in tiles]
        o = [rj * x for x in o]

        @pl.when(j >= NBUF)
        def _():
            put(j - NBUF).wait()

        for d in range(ND):
            kx, ky = float(KX[d]), float(KY[d])
            x = [z + v[t] for t, z in enumerate(slab(z_ref, j, d))]
            row = edge[0, d : d + 1, :] if YP[d] else edge[1, d - NL : d - NL + 1, :]
            y = rows_from(x, not YP[d], row)
            for t in tiles:
                back = (fr - (kx + ky)) * x[t] + kx * shift_x(x[t], not XP[d]) + ky * y[t]
                buf[slot, d, 8 * t : 8 * t + 8, :] = o[t] * back
        put(j).start()

    for j in range(max(0, nf - NBUF), nf):
        put(j).wait()


VMEM = pl.BlockSpec(memory_space=pltpu.VMEM)
SMEM = pl.BlockSpec(memory_space=pltpu.SMEM)
HBM = pl.BlockSpec(memory_space=pltpu.HBM)


def f32(*shape):
    return jax.ShapeDtypeStruct(shape, F32)


def vmem(*shape):
    return pltpu.VMEM(shape, F32)


def call(kernel, name, outs, args, scratch=(), hbm=(), held=(), out_hbm=(), flops=4e6, size=4e6, limit=6, alias=None):
    put = {**dict.fromkeys(hbm, pltpu.HBM), **dict.fromkeys(held, pltpu.VMEM)}
    args = [pltpu.with_memory_space_constraint(a, put[k]) if k in put else a for k, a in enumerate(args)]
    return pl.pallas_call(
        kernel,
        name=name,
        out_shape=outs,
        in_specs=[HBM if k in hbm else SMEM if a.ndim == 1 else VMEM for k, a in enumerate(args)],
        out_specs=[HBM if k in out_hbm else VMEM for k in range(len(outs))],
        scratch_shapes=list(scratch),
        input_output_aliases=alias or {},
        compiler_params=pltpu.CompilerParams(vmem_limit_bytes=limit * MIB),
        cost_estimate=pl.CostEstimate(flops=int(flops), bytes_accessed=int(size), transcendentals=0),
    )(*args)


def peers(x):
    n = lax.axis_size("spec")
    if n & (n - 1) == 0:
        return [lax.ppermute(x, "spec", [(i, i ^ k) for i in range(n)]) for k in range(1, n)]
    return [lax.ppermute(x, "spec", [(i, (i + k) % n) for i in range(n)]) for k in range(1, n)]


def exchange(up, dn):
    n = lax.axis_size("cells")
    lo = lax.ppermute(up, "cells", [(i, i + 1) for i in range(n - 1)])
    hi = lax.ppermute(dn, "cells", [(i + 1, i) for i in range(n - 1)])
    return lo, hi


def after(first, *later):
    return lax.optimization_barrier((first, *later))[1:]


def shards(spectrum_start, input_coef, white_coef, wind_speed, wind_angle, sea_mask, cotangent):
    nf, _, rows, nc = spectrum_start.shape
    n = lax.axis_size("spec")
    tab, dirs = jnp.asarray(TABLE), jnp.asarray(DIRS)
    big = vmem(nf, ND, rows, nc)
    band = f32(nf, MISC + MROWS, nc)
    line, duo, hs, sums = f32(nf, NL, nc), f32(2, nf, nc), f32(nf, rows, nc), f32(5, nf, rows, nc)
    flat, two, push = f32(rows, nc), f32(2, rows, nc), f32(8, nc)
    stream = [vmem(NBUF, ND, rows, nc), pltpu.SemaphoreType.DMA((NBUF,))]
    heavy = dict(flops=6e7, size=1e7, limit=12)

    t0_part, s_up, s_dn = call(
        start_kernel, "start", [f32(2 * rows + 8, nc), band, band],
        [spectrum_start, sea_mask, input_coef, white_coef, wind_speed, wind_angle],
        stream + [vmem(4, rows, nc), pltpu.VMEM((rows, nc), jnp.int32), pltpu.SemaphoreType.DMA((5,)), vmem(5, rows, nc)],
        hbm=range(6), **heavy,
    )
    t0_parts = peers(t0_part)
    (speed,) = after(t0_part, wind_speed)
    g, p, al, p_up, p_dn = call(
        wind_kernel, "wind", [big, big, vmem(ND, rows, nc), band, band], [tab, cotangent, input_coef, speed, wind_angle],
        stream + [vmem(ND, rows, nc)], hbm=(1,), **heavy,
    )
    s_up, s_dn = after(p_up, s_up, s_dn)
    s_lo, s_hi = exchange(s_up, s_dn)
    (t0_own,) = after(s_up, t0_part)
    tot0, e_up, e_dn = call(functools.partial(total_kernel, rows), "total", [f32(2 * rows + 8, nc), push, push], [t0_own, *t0_parts])
    e_lo, e_hi = exchange(e_up, e_dn)
    (mask,) = after(tot0, sea_mask)
    u, s5, u_lo, u_hi, sy = call(
        grown_kernel, "grown", [big, sums, line, line, duo], [tab, dirs, spectrum_start, mask, g, s_lo, s_hi],
        stream, hbm=(2,), held=(4,), **heavy,
    )
    t0, t0h, h0, h0h, t1_part = call(
        functools.partial(first_kernel, nf), "first", [two, push, hs, duo, f32(2 * rows, nc)],
        [tab, tot0, e_lo, e_hi, s_lo, s_hi, sea_mask, white_coef, s5, sy],
    )
    t1_parts = peers(t1_part)
    p_up, p_dn = after(t1_part, p_up, p_dn)
    p_lo, p_hi = exchange(p_up, p_dn)
    r5, t5 = call(product_kernel, "product", [sums, sums], [tab, u, p, al, u_lo, u_hi], held=(1, 2, 3), **heavy)
    (t1_own,) = after(r5, t1_part)
    t1, h1, d1_part = call(
        functools.partial(second_kernel, nf, n), "second", [two, hs, flat],
        [tab, t1_own, *t1_parts, sea_mask, white_coef, h0, h0h, r5],
    )
    d1_parts = [d1_part] + peers(d1_part)
    d1, v1, d0_part, f1, b_up, b_dn = call(
        functools.partial(third_kernel, nf, n), "third", [flat, hs, f32(rows + 8, nc), flat, push, push],
        [tab, *d1_parts, sea_mask, white_coef, wind_speed, t1, h0, h0h, h1, s5, sy, r5, t5],
    )
    d0_parts = peers(d0_part)
    b_lo, b_hi = exchange(b_up, b_dn)
    z, z_lo, z_hi, f_part = call(
        back_kernel, "back", [big, line, line, flat],
        [tab, dirs, p, u, g, al, h0, h0h, h1, v1, p_lo, p_hi, s_lo, s_hi, b_lo, b_hi, f1, wind_speed],
        [vmem(2, NL, nc), vmem(2, 2, 8, nc)], held=(2, 3, 4, 5), alias={4: 0}, **heavy,
    )
    (d0_own,) = after(f_part, d0_part)
    tot, c_up, c_dn = call(
        functools.partial(fourth_kernel, rows), "fourth", [f32(rows + 8, nc), push, push], [d0_own, *d0_parts]
    )
    c_lo, c_hi = exchange(c_up, c_dn)
    (f_part,) = after(tot, f_part)
    f_parts = peers(f_part)
    out, grad_white = call(
        out_kernel, "out", [f32(nf, ND, rows, nc), flat],
        [tab, z, z_lo, z_hi, tot, c_lo, c_hi, t0, t0h, t1, d1, sea_mask, white_coef, s_lo, s_hi],
        [vmem(2, rows, nc), vmem(2, 8, nc), vmem(2, NL, nc)] + stream, held=(1,), out_hbm=(0,), **heavy,
    )
    grad_input = f_part
    for other in f_parts:
        grad_input = grad_input + other
    return out, time_step * grad_input, grad_white


def solution(mesh):
    return jax.shard_map(
        shards,
        mesh=mesh,
        in_specs=(
            P("spec", None, "cells", None),
            P("cells", None),
            P("cells", None),
            P("cells", None),
            P("cells", None),
            P("cells", None),
            P("spec", None, "cells", None),
        ),
        out_specs=(P("spec", None, "cells", None), P("cells", None), P("cells", None)),
        check_vma=False,
    )
```

```python
import functools
import math

import jax
import jax.numpy as jnp
import numpy as np
from jax import lax
from jax.experimental import pallas as pl
from jax.experimental.pallas import tpu as pltpu
from jax.sharding import PartitionSpec as P

NF = 32
ND = 36
STEPS = 2

epsilon = 1e-06
energy_ref = 0.5
time_step = 0.5
courant = 0.7
ratio_step = 1.1

F32 = jnp.float32
LOG2E = math.log2(math.e)

_every = np.exp(np.arange(NF, dtype=np.float32) * np.float32(math.log(ratio_step))).astype(np.float32)
_total = _every.sum(dtype=np.float32)
HIGHEST = float(_every[-1])
MEAN_RATIO = float((_every * _every).sum(dtype=np.float32) / _total)
_weights = _every / (np.float32(ND) * _total)
_q = (_every / _every[-1]) ** 2
NTAB = 5
TABLE = np.stack([_every, 1 / _every, _weights, _q, _weights * _every], axis=1).astype(np.float32).reshape(-1)

_angle = (np.float32(2.0 * math.pi) * np.arange(ND, dtype=np.float32) / np.float32(ND)).astype(np.float32)
COS, SIN = np.cos(_angle).astype(np.float32), np.sin(_angle).astype(np.float32)
KX, KY = np.float32(courant) * np.abs(COS), np.float32(courant) * np.abs(SIN)
XP, YP = [bool(c >= 0) for c in COS], [bool(s >= 0) for s in SIN]
NL = sum(YP)
NH = ND - NL
assert YP == [True] * NL + [False] * NH and NL == NH
QUADS = [[d for d in range(ND) if (XP[d], YP[d]) == quad] for quad in ((1, 1), (0, 1), (0, 0), (1, 0))]
DIRS = np.stack([v[a:b] for a, b in ((0, NL), (NL, ND)) for v in (KX, KY, COS, SIN)]).astype(np.float32)
DIRS = np.ascontiguousarray(np.broadcast_to(DIRS[:, :, None], DIRS.shape + (128,)))
MISC = 2 * NL
MROWS = 4
NMISC = 5

MIB = 1 << 20


def coef(tab, j, nf, which):
    return tab[(lax.axis_index("spec") * nf + j) * NTAB + which]


def shift_x(x, plus):
    return pltpu.roll(x, 1 if plus else x.shape[1] - 1, 1)


def first_row(x):
    return lax.broadcasted_iota(jnp.int32, x.shape, 0) == 0


def last_row(x):
    return lax.broadcasted_iota(jnp.int32, x.shape, 0) == x.shape[0] - 1


def from_before(x, above):
    return jnp.where(first_row(x), above, pltpu.roll(x, 1, 0))


def from_after(x, below):
    return jnp.where(last_row(x), below, pltpu.roll(x, x.shape[0] - 1, 0))


def shift_y(x, plus, outside):
    return from_before(x, outside) if plus else from_after(x, outside)


def damping_of(energy, moment):
    shifted = energy + epsilon
    ratio = moment / (shifted * MEAN_RATIO)
    r2 = ratio * ratio
    steep = energy * (r2 * r2) / energy_ref
    return shifted, ratio, steep, steep * steep * ratio


def grads_of(energy, moment, white, damp_total):
    shifted, ratio, steep, damping = damping_of(energy, moment)
    grad_damp = -time_step * white * damp_total
    grad_ratio = 9.0 * grad_damp * steep * steep
    r2 = ratio * ratio
    grad_energy = grad_damp * 2.0 * steep * (r2 * r2) * ratio / energy_ref - grad_ratio * ratio / shifted
    grad_moment = grad_ratio / (shifted * MEAN_RATIO)
    return grad_energy, grad_moment, damping


def gate(q, white, damping, ocean):
    return ocean * jnp.exp2((-time_step * LOG2E) * q * (white * damping))


def rows_from(tiles, plus, outside):
    moved = [pltpu.roll(x, 1 if plus else 7, 0) for x in tiles]
    mark = first_row(tiles[0]) if plus else last_row(tiles[0])
    feed = [outside] + moved[:-1] if plus else moved[1:] + [outside]
    return [jnp.where(mark, a, b) for a, b in zip(feed, moved)]


def slab(ref, *index):
    return [ref[(*index, slice(t, t + 8))] for t in range(0, ref.shape[-2], 8)]


def misc_at(r, k):
    m = r * NMISC + k
    return m // MROWS, MISC + m % MROWS


def misc_row(ref, r, k):
    j, row = misc_at(r, k)
    return ref[j, row : row + 1, :]


def halo_rows(ref, j, r):
    return ref[j, r * NL : (r + 1) * NL, :]


def fetches(hbm, ref, sems):
    return lambda j: pltpu.make_async_copy(hbm.at[j], ref.at[j], sems.at[j])


NBUF = 3


def edge_kernel(s_hbm, mask_h, coef_h, white_h, speed_h, angle_h, up_ref, dn_ref, low, high, sems, fields, ints, small_sems):
    nf, _, rows, nc = s_hbm.shape

    def fetch(j):
        return (
            pltpu.make_async_copy(s_hbm.at[j, 0:NL, rows - 8 : rows, :], low.at[j], sems.at[0, j]),
            pltpu.make_async_copy(s_hbm.at[j, NL:ND, 0:8, :], high.at[j], sems.at[1, j]),
        )

    smalls = [pltpu.make_async_copy(mask_h, ints, small_sems.at[0])]
    for k, f in enumerate((coef_h, white_h, speed_h, angle_h)):
        smalls.append(pltpu.make_async_copy(f, fields.at[k], small_sems.at[1 + k]))
    for c in smalls:
        c.start()
    for j in range(nf):
        for c in fetch(j):
            c.start()
    for c in smalls:
        c.wait()

    @pl.loop(0, nf)
    def _(j):
        up_ref[j, MISC:, :] = jnp.zeros_like(up_ref[j, MISC:, :])
        dn_ref[j, MISC:, :] = jnp.zeros_like(dn_ref[j, MISC:, :])

    for side, out in ((slice(rows - 2, rows), up_ref), (slice(0, 2), dn_ref)):
        kappa = (time_step * LOG2E / HIGHEST) * (fields[0, side] * fields[2, side])
        angle = fields[3, side]
        for k, v in enumerate((kappa, jnp.cos(angle), jnp.sin(angle), ints[side].astype(F32), fields[1, side])):
            for r in range(2):
                a, b = misc_at(r, k)
                out[a, b : b + 1, :] = v[r : r + 1]

    @pl.loop(0, nf)
    def _(j):
        for c in fetch(j):
            c.wait()
        for r in range(2):
            for d in range(NL):
                up_ref[j, r * NL + d : r * NL + d + 1, :] = low[j, d, 6 + r : 7 + r, :]
                dn_ref[j, r * NL + d : r * NL + d + 1, :] = high[j, d, r : r + 1, :]


def start_kernel(s_hbm, tab_h, mask, s_ref, t0_ref, sems, tab, small_sem, sums):
    nf = s_hbm.shape[0]
    rows, nc = mask.shape
    fetch = fetches(s_hbm, s_ref, sems)
    get_tab = pltpu.make_async_copy(tab_h, tab, small_sem)
    get_tab.start()
    for j in range(nf):
        fetch(j).start()
    sums[...] = jnp.zeros_like(sums)
    get_tab.wait()

    @pl.loop(0, nf)
    def _(j):
        rj, w, wf = [coef(tab, j, nf, k) for k in (1, 2, 4)]
        fetch(j).wait()
        for t in range(0, rows, 8):
            acc = [None] * 5

            def add(k, v):
                acc[k] = v if acc[k] is None else acc[k] + v

            for d in range(ND):
                x = s_ref[j, d, t : t + 8, :]
                add(0, x)
                add(1 if XP[d] else 2, float(KX[d]) * x)
                add(3 if YP[d] else 4, float(KY[d]) * x)
            for k in range(5):
                sums[0, k, t : t + 8, :] += (w if k == 0 else w * rj) * acc[k]
                sums[1, k, t : t + 8, :] += (wf if k == 0 else wf * rj) * acc[k]

    ocean = mask[...].astype(F32)
    t0_ref[2 * rows :, :] = jnp.zeros_like(t0_ref[2 * rows :, :])
    for e in range(2):
        total, xp, xm, yp, ym = [ocean * sums[e, k] for k in range(5)]
        t0_ref[e * rows : (e + 1) * rows, :] = total + (
            shift_x(xp, True) + shift_x(xm, False) + from_before(yp, 0.0) + from_after(ym, 0.0) - (xp + xm + yp + ym)
        )
        t0_ref[2 * rows + e : 2 * rows + e + 1, :] = yp[rows - 1 : rows]
        t0_ref[2 * rows + 2 + e : 2 * rows + 3 + e, :] = ym[0:1]


def wind_kernel(tab, lam_hbm, coef_in, speed, angle, p_ref, al_ref, up_ref, dn_ref, sems, expo):
    nf = lam_hbm.shape[0]
    rows, nc = angle.shape
    fetch = fetches(lam_hbm, p_ref, sems)
    for j in range(nf):
        fetch(j).start()
    up_ref[:, MISC:, :] = jnp.zeros_like(up_ref[:, MISC:, :])
    dn_ref[:, MISC:, :] = jnp.zeros_like(dn_ref[:, MISC:, :])
    kappa = (time_step * LOG2E / HIGHEST) * (coef_in[...] * speed[...])
    ca, sa = jnp.cos(angle[...]), jnp.sin(angle[...])
    for d in range(ND):
        align = jnp.maximum(float(COS[d]) * ca + float(SIN[d]) * sa, 0.0)
        al = align * align
        al_ref[d] = al
        expo[d] = kappa * al

    @pl.loop(0, nf)
    def _(j):
        fr = coef(tab, j, nf, 0)
        fetch(j).wait()
        for d in range(ND):
            p = jnp.exp2(fr * expo[d]) * p_ref[j, d]
            p_ref[j, d] = p
            for r in range(2):
                at = slice(r * NL + d % NL, r * NL + d % NL + 1)
                if d < NL:
                    dn_ref[j, at, :] = p[r : r + 1]
                else:
                    up_ref[j, at, :] = p[rows - 2 + r : rows - 1 + r]


def halo_growth(fr, dirs, half, misc, r):
    cosd, sind = dirs[4 * half + 2][:, 0:1], dirs[4 * half + 3][:, 0:1]
    align = jnp.maximum(cosd * misc_row(misc, r, 1) + sind * misc_row(misc, r, 2), 0.0)
    return jnp.exp2(fr * (misc_row(misc, r, 0) * (align * align)))


def halo_adv(rj, dirs, half, near, far, transpose):
    kx, ky, cosd = [dirs[4 * half + k][:, 0:1] for k in range(3)]
    before, after = shift_x(near, not transpose), shift_x(near, transpose)
    moved = jnp.where(cosd >= 0, before, after)
    return near + rj * (kx * (moved - near) + ky * (far - near))


def grown_kernel(tab, dirs, s_ref, mask, coef_in, speed, al_ref, lo, hi, u_ref, sum_ref, ul_ref, uh_ref, sy_ref, edge, work):
    nf, _, rows, nc = s_ref.shape
    ocean = mask[...].astype(F32)

    @pl.loop(0, nf)
    def _(j):
        fr, rj = coef(tab, j, nf, 0), coef(tab, j, nf, 1)
        for half, (blk, near, far, out) in enumerate(((lo, 1, 0, ul_ref), (hi, 0, 1, uh_ref))):
            x = [misc_row(blk, r, 3) * halo_rows(blk, j, r) for r in range(2)]
            edge[half] = rj * x[near]
            u = halo_growth(fr, dirs, half, blk, near) * halo_adv(rj, dirs, half, x[near], x[far], False)
            out[j] = u
            sy_ref[half, pl.ds(j, 1), :] = jnp.sum(dirs[4 * half + 1][:, 0:1] * u, axis=0, keepdims=True)
        tiles = range(rows // 8)
        work[...] = (fr * (time_step * LOG2E / HIGHEST)) * (coef_in[...] * speed[...])
        oj = [rj * ocean[8 * t : 8 * t + 8] for t in tiles]
        seen = set()
        for quad in QUADS:
            acc = [[None] * 3 for _ in tiles]
            for d in quad:
                kx, ky = float(KX[d]), float(KY[d])
                x = [o * v for o, v in zip(oj, slab(s_ref, j, d))]
                row = edge[0, d : d + 1, :] if YP[d] else edge[1, d - NL : d - NL + 1, :]
                y = rows_from(x, YP[d], row)
                for t in tiles:
                    u = jnp.exp2(work[8 * t : 8 * t + 8] * al_ref[d, 8 * t : 8 * t + 8]) * (
                        (fr - (kx + ky)) * x[t] + kx * shift_x(x[t], XP[d]) + ky * y[t]
                    )
                    u_ref[j, d, 8 * t : 8 * t + 8, :] = u
                    for k, v in enumerate((u, kx * u, ky * u)):
                        acc[t][k] = v if acc[t][k] is None else acc[t][k] + v
            for k, key in enumerate((0, 1 if XP[quad[0]] else 2, 3 if YP[quad[0]] else 4)):
                for t in tiles:
                    at = (key, j, slice(8 * t, 8 * t + 8))
                    sum_ref[at] = sum_ref[at] + acc[t][k] if key in seen else acc[t][k]
                seen.add(key)
        for t in tiles:
            a, b, c, d, e = [sum_ref[k, j, 8 * t : 8 * t + 8, :] for k in range(5)]
            sum_ref[0, j, 8 * t : 8 * t + 8, :] = a - rj * (b + c + d + e)


def product_kernel(tab, u_ref, p_ref, al_ref, ul_ref, uh_ref, r_ref, t_ref):
    nf, _, rows, nc = u_ref.shape

    @pl.loop(0, nf)
    def _(j):
        rj = coef(tab, j, nf, 1)
        for t in range(0, rows, 8):
            seen = set()
            for quad in QUADS:
                acc = [None] * 6
                for d in quad:
                    kx, ky = float(KX[d]), float(KY[d])
                    u, p, al = u_ref[j, d, t : t + 8, :], p_ref[j, d, t : t + 8, :], al_ref[d, t : t + 8, :]
                    if YP[d]:
                        row = ul_ref[j, d : d + 1, :] if t == 0 else u_ref[j, d, t - 1 : t, :]
                        y = jnp.where(first_row(u), row, pltpu.roll(u, 1, 0))
                    else:
                        row = uh_ref[j, d - NL : d - NL + 1, :] if t + 8 == rows else u_ref[j, d, t + 8 : t + 9, :]
                        y = jnp.where(last_row(u), row, pltpu.roll(u, 7, 0))
                    cu = (1.0 - rj * (kx + ky)) * (p * u)
                    px, py = kx * (p * shift_x(u, XP[d])), ky * (p * y)
                    for k, v in enumerate((cu, px, py, al * cu, al * px, al * py)):
                        acc[k] = v if acc[k] is None else acc[k] + v
                xk, yk = (1 if XP[quad[0]] else 2), (3 if YP[quad[0]] else 4)
                for k, ref in enumerate((r_ref, t_ref)):
                    for key, v in zip((0, xk, yk), acc[3 * k : 3 * k + 3]):
                        at = (key, j, slice(t, t + 8))
                        ref[at] = ref[at] + v if (k, key) in seen else v
                        seen.add((k, key))


def total_kernel(rows, *refs):
    parts, (tot, up, dn) = refs[:-3], refs[-3:]
    total = parts[0][...]
    for part in parts[1:]:
        total = total + part[...]
    tot[...] = total
    up[...] = jnp.zeros_like(up)
    dn[...] = jnp.zeros_like(dn)
    for k, row in enumerate((rows - 1, 2 * rows - 1, 2 * rows, 2 * rows + 1)):
        up[k : k + 1, :] = total[row : row + 1]
    for k, row in enumerate((0, rows, 2 * rows + 2, 2 * rows + 3)):
        dn[k : k + 1, :] = total[row : row + 1]


def advected_sum(rj, h, above, below, s):
    return h * s[0], rj * (
        shift_x(h * s[1], True) + shift_x(h * s[2], False) + from_before(h * s[3], above) + from_after(h * s[4], below)
    )


def first_kernel(nf, tab, tot, lo, hi, lo_misc, hi_misc, mask, white, sum_ref, sy_ref, t0_ref, t0h_ref, h0_ref, h0h_ref, t1_ref):
    rows, nc = mask.shape
    ocean = mask[...].astype(F32)
    row = lax.broadcasted_iota(jnp.int32, (rows, nc), 0)
    total = tot[...]
    field = []
    halo = []
    t0h_ref[...] = jnp.zeros_like(t0h_ref)
    for k in range(2):
        v = total[k * rows : (k + 1) * rows]
        v = v + jnp.where(row == 0, lo[2 + k : 3 + k, :], 0.0) + jnp.where(row == rows - 1, hi[2 + k : 3 + k, :], 0.0)
        field.append(ocean * v)
        t0_ref[k] = field[k]
        above = misc_row(lo_misc, 1, 3) * (lo[k : k + 1, :] + total[2 * rows + 2 + k : 2 * rows + 3 + k])
        below = misc_row(hi_misc, 0, 3) * (hi[k : k + 1, :] + total[2 * rows + k : 2 * rows + 1 + k])
        halo.append((above, below))
        t0h_ref[k : k + 1, :] = above
        t0h_ref[2 + k : 3 + k, :] = below
    damping = damping_of(*field)[3]
    damp_lo = damping_of(halo[0][0], halo[1][0])[3]
    damp_hi = damping_of(halo[0][1], halo[1][1])[3]
    energy, moment = jnp.zeros((rows, nc), F32), jnp.zeros((rows, nc), F32)
    for j in range(nf):
        rj, w, q, wf = [coef(tab, j, nf, k) for k in (1, 2, 3, 4)]
        h = gate(q, white[...], damping, ocean)
        h_lo = gate(q, misc_row(lo_misc, 1, 4), damp_lo, misc_row(lo_misc, 1, 3))
        h_hi = gate(q, misc_row(hi_misc, 0, 4), damp_hi, misc_row(hi_misc, 0, 3))
        h0_ref[j] = h
        h0h_ref[0, j : j + 1, :] = h_lo
        h0h_ref[1, j : j + 1, :] = h_hi
        centre, around = advected_sum(
            rj, h, h_lo * sy_ref[0, j : j + 1, :], h_hi * sy_ref[1, j : j + 1, :], [sum_ref[k, j] for k in range(5)]
        )
        adv = centre + around
        energy, moment = energy + w * adv, moment + wf * adv
    t1_ref[0:rows, :] = energy
    t1_ref[rows : 2 * rows, :] = moment


def gathered(rj, h, h_lo, h_hi, r):
    return h * r[0] + rj * (
        shift_x(h, True) * r[1] + shift_x(h, False) * r[2] + from_before(h, h_lo) * r[3] + from_after(h, h_hi) * r[4]
    )


def second_kernel(nf, n, tab, *refs):
    parts, (mask, white, h0_ref, h0h_ref, r_ref, t1_ref, h1_ref, d1_ref) = refs[:n], refs[n:]
    rows, nc = mask.shape
    ocean = mask[...].astype(F32)
    total = parts[0][...]
    for part in parts[1:]:
        total = total + part[...]
    energy, moment = ocean * total[:rows], ocean * total[rows:]
    t1_ref[0] = energy
    t1_ref[1] = moment
    damping = damping_of(energy, moment)[3]
    acc = jnp.zeros((rows, nc), F32)
    for j in range(nf):
        rj, q = coef(tab, j, nf, 1), coef(tab, j, nf, 3)
        h1 = gate(q, white[...], damping, ocean)
        h1_ref[j] = h1
        part = gathered(rj, h0_ref[j], h0h_ref[0, j : j + 1, :], h0h_ref[1, j : j + 1, :], [r_ref[k, j] for k in range(5)])
        acc = acc + q * (h1 * part)
    d1_ref[...] = acc


def third_kernel(nf, n, tab, *refs):
    parts = refs[:n]
    mask, white, speed, t1, h0_ref, h0h_ref, h1_ref, sum_ref, sy_ref, r_ref, t_ref = refs[n : n + 11]
    d1_ref, v1_ref, d0_ref, f1_ref, up, dn = refs[n + 11 :]
    rows, nc = mask.shape
    ocean = mask[...].astype(F32)
    damp = parts[0][...]
    for part in parts[1:]:
        damp = damp + part[...]
    d1_ref[...] = damp
    up[...] = jnp.zeros_like(up)
    dn[...] = jnp.zeros_like(dn)
    for k, v in enumerate((t1[0], t1[1], damp)):
        up[2 * k : 2 * k + 2, :] = v[rows - 2 : rows]
        dn[2 * k : 2 * k + 2, :] = v[0:2]
    grad_e, grad_m, _ = grads_of(t1[0], t1[1], white[...], damp)
    acc, force = jnp.zeros((rows, nc), F32), jnp.zeros((rows, nc), F32)
    push_lo, push_hi = jnp.zeros((1, nc), F32), jnp.zeros((1, nc), F32)
    for j in range(nf):
        fr, rj, w, q = [coef(tab, j, nf, k) for k in range(4)]
        h0, h1 = h0_ref[j], h1_ref[j]
        h_lo, h_hi = h0h_ref[0, j : j + 1, :], h0h_ref[1, j : j + 1, :]
        v1 = ocean * (w * (grad_e + fr * grad_m))
        v1_ref[j] = v1
        s, r = [sum_ref[k, j] for k in range(5)], [r_ref[k, j] for k in range(5)]
        inner = (
            shift_x(h1 * r[1], False)
            + shift_x(h1 * r[2], True)
            + from_after(h1 * r[3], 0.0)
            + from_before(h1 * r[4], 0.0)
            + s[1] * shift_x(v1, False)
            + s[2] * shift_x(v1, True)
            + s[3] * from_after(v1, 0.0)
            + s[4] * from_before(v1, 0.0)
        )
        acc = acc + q * (h0 * (h1 * r[0] + v1 * s[0] + rj * inner))
        push_lo = push_lo + (q * rj) * (h_lo * (h1[0:1] * r[3][0:1] + v1[0:1] * sy_ref[0, j : j + 1, :]))
        e = rows - 1
        push_hi = push_hi + (q * rj) * (
            h_hi * (h1[e : e + 1] * r[4][e : e + 1] + v1[e : e + 1] * sy_ref[1, j : j + 1, :])
        )
        part = gathered(rj, h0, h_lo, h_hi, [t_ref[k, j] for k in range(5)])
        force = force + fr * (h1 * part)
    up[6:7, :] = acc[rows - 1 : rows]
    up[7:8, :] = push_hi
    dn[6:7, :] = acc[0:1]
    dn[7:8, :] = push_lo
    d0_ref[0:rows, :] = acc
    d0_ref[rows:, :] = jnp.zeros_like(d0_ref[rows:, :])
    d0_ref[rows : rows + 1, :] = push_lo
    d0_ref[rows + 1 : rows + 2, :] = push_hi
    f1_ref[...] = (speed[...] / HIGHEST) * force


def back_kernel(tab, dirs, p_ref, u_ref, coef_in, al_ref, h0_ref, h0h_ref, h1_ref, v1_ref, pl_ref, ph_ref, lo_misc, hi_misc, lo, hi, f1_ref, speed, z_ref, zl_ref, zh_ref, f_ref, edge, halo, scaled, work):
    nf, _, rows, nc = p_ref.shape
    sides = ((0, ph_ref, hi_misc, hi, 0, 1, 1, zh_ref), (1, pl_ref, lo_misc, lo, 1, 0, 0, zl_ref))
    for side, (_, _, misc, got, *_) in enumerate(sides):
        for r in range(2):
            energy, moment, damp = [got[2 * k + r : 2 * k + r + 1, :] for k in range(3)]
            white = misc_row(misc, r, 4)
            grad_e, grad_m, damping = grads_of(energy, moment, white, damp)
            for k, v in enumerate((grad_e, grad_m, white * damping)):
                halo[side, r, k : k + 1, :] = v
    f_ref[...] = jnp.zeros_like(f_ref)

    @pl.loop(0, nf)
    def _(j):
        fr, rj = coef(tab, j, nf, 0), coef(tab, j, nf, 1)
        w, q = coef(tab, j, nf, 2), coef(tab, j, nf, 3)
        for side, (half, blk, misc, _, near, far, which, out) in enumerate(sides):
            x = []
            for r in range(2):
                ocean = misc_row(misc, r, 3)
                h = gate(q, halo[side, r, 2:3, :], 1.0, ocean)
                v = ocean * (w * (halo[side, r, 0:1, :] + fr * halo[side, r, 1:2, :]))
                x.append(halo_rows(blk, j, r) * h + v)
            edge[side] = x[near]
            moved = halo_adv(rj, dirs, half, x[near], x[far], True) * halo_growth(fr, dirs, half, misc, near)
            out[j] = moved * h0h_ref[which, pl.ds(j, 1), :]
        tiles = range(rows // 8)
        at8 = [slice(8 * t, 8 * t + 8) for t in tiles]
        work[...] = (fr * (time_step * LOG2E / HIGHEST)) * (coef_in[...] * speed[...])
        for t in tiles:
            scaled[at8[t]] = rj * h0_ref[j, at8[t]]
        force = [None for _ in tiles]
        for d in range(ND):
            kx, ky = float(KX[d]), float(KY[d])
            x = [p_ref[j, d, at8[t]] * h1_ref[j, at8[t]] + v1_ref[j, at8[t]] for t in tiles]
            row = edge[0, d : d + 1, :] if YP[d] else edge[1, d - NL : d - NL + 1, :]
            y = rows_from(x, not YP[d], row)
            for t in tiles:
                back = (fr - (kx + ky)) * x[t] + kx * shift_x(x[t], not XP[d]) + ky * y[t]
                al = al_ref[d, at8[t]]
                v = al * (back * u_ref[j, d, at8[t]])
                force[t] = v if force[t] is None else force[t] + v
                z_ref[j, d, at8[t]] = back * (jnp.exp2(work[at8[t]] * al) * scaled[at8[t]])
        for t in tiles:
            f_ref[at8[t]] += fr * (scaled[at8[t]] * force[t])

    f_ref[...] = (speed[...] / HIGHEST) * f_ref[...] + f1_ref[...]


def fourth_kernel(rows, part, lo, hi, out):
    row = lax.broadcasted_iota(jnp.int32, (rows, out.shape[1]), 0)
    v = part[0:rows, :]
    v = v + jnp.where(row == 0, lo[7:8, :], 0.0) + jnp.where(row == rows - 1, hi[7:8, :], 0.0)
    out[0:rows, :] = v
    out[rows:, :] = jnp.zeros_like(out[rows:, :])
    out[rows : rows + 1, :] = part[rows : rows + 1, :] + lo[6:7, :]
    out[rows + 1 : rows + 2, :] = part[rows + 1 : rows + 2, :] + hi[6:7, :]


def out_kernel(n, tab, *refs):
    parts, refs = refs[:n], refs[n:]
    z_ref, zl_ref, zh_ref, t0, t0h, t1, d1, mask, white, lo_misc, hi_misc = refs[:11]
    out_hbm, gw_ref, own, halo, edge, work, buf, sems = refs[11:]
    nf, _, rows, nc = z_ref.shape
    ocean = mask[...].astype(F32)
    total = parts[0][...]
    for part in parts[1:]:
        total = total + part[...]
    damp = total[0:rows]
    grad_e, grad_m, damping = grads_of(t0[0], t0[1], white[...], damp)
    own[0] = grad_e
    own[1] = grad_m
    gw_ref[...] = -time_step * (damping * damp + damping_of(t1[0], t1[1])[3] * d1[...])
    above, below = total[rows : rows + 1], total[rows + 1 : rows + 2]
    sides = ((hi_misc, 0, 2, below, zh_ref), (lo_misc, 1, 0, above, zl_ref))
    for side, (misc, r, k, damp, _) in enumerate(sides):
        e, m, _ = grads_of(t0h[k : k + 1, :], t0h[k + 1 : k + 2, :], misc_row(misc, r, 4), damp)
        halo[side, 0:1, :] = e
        halo[side, 1:2, :] = m

    def put(j):
        return pltpu.make_async_copy(buf.at[j % NBUF], out_hbm.at[j], sems.at[j % NBUF])

    @pl.loop(0, nf)
    def _(j):
        slot = j % NBUF
        fr, rj, w = [coef(tab, j, nf, k) for k in range(3)]
        for side, (misc, r, _, _, z) in enumerate(sides):
            edge[side] = z[j] + misc_row(misc, r, 3) * (w * (halo[side, 0:1, :] + fr * halo[side, 1:2, :]))
        tiles = range(rows // 8)
        o = [ocean[8 * t : 8 * t + 8] for t in tiles]
        v = [o[t] * (w * (own[0, 8 * t : 8 * t + 8] + fr * own[1, 8 * t : 8 * t + 8])) for t in tiles]
        for t in tiles:
            work[0, 8 * t : 8 * t + 8] = v[t]
            work[1, 8 * t : 8 * t + 8] = rj * o[t]

        @pl.when(j >= NBUF)
        def _():
            put(j - NBUF).wait()

        for d in range(ND):
            kx, ky = float(KX[d]), float(KY[d])
            x = [z + work[0, 8 * t : 8 * t + 8] for t, z in enumerate(slab(z_ref, j, d))]
            row = edge[0, d : d + 1, :] if YP[d] else edge[1, d - NL : d - NL + 1, :]
            y = rows_from(x, not YP[d], row)
            for t in tiles:
                back = (fr - (kx + ky)) * x[t] + kx * shift_x(x[t], not XP[d]) + ky * y[t]
                buf[slot, d, 8 * t : 8 * t + 8, :] = work[1, 8 * t : 8 * t + 8] * back
        put(j).start()

    for j in range(max(0, nf - NBUF), nf):
        put(j).wait()


VMEM = pl.BlockSpec(memory_space=pltpu.VMEM)
SMEM = pl.BlockSpec(memory_space=pltpu.SMEM)
HBM = pl.BlockSpec(memory_space=pltpu.HBM)


def f32(*shape):
    return jax.ShapeDtypeStruct(shape, F32)


def vmem(*shape):
    return pltpu.VMEM(shape, F32)


def call(kernel, name, outs, args, scratch=(), hbm=(), held=(), out_hbm=(), limit=6, alias=None):
    put = {**dict.fromkeys(hbm, pltpu.HBM), **dict.fromkeys(held, pltpu.VMEM)}
    args = [pltpu.with_memory_space_constraint(a, put[k]) if k in put else a for k, a in enumerate(args)]
    return pl.pallas_call(
        kernel,
        name=name,
        out_shape=outs,
        in_specs=[HBM if k in hbm else SMEM if a.ndim == 1 else VMEM for k, a in enumerate(args)],
        out_specs=[HBM if k in out_hbm else VMEM for k in range(len(outs))],
        scratch_shapes=list(scratch),
        input_output_aliases=alias or {},
        compiler_params=pltpu.CompilerParams(vmem_limit_bytes=limit * MIB),
        cost_estimate=pl.CostEstimate(flops=1, bytes_accessed=1, transcendentals=0),
    )(*args)


def peers(x):
    n = lax.axis_size("spec")
    if n & (n - 1) == 0:
        return [lax.ppermute(x, "spec", [(i, i ^ k) for i in range(n)]) for k in range(1, n)]
    return [lax.ppermute(x, "spec", [(i, (i + k) % n) for i in range(n)]) for k in range(1, n)]


def exchange(up, dn):
    n = lax.axis_size("cells")
    lo = lax.ppermute(up, "cells", [(i, i + 1) for i in range(n - 1)])
    hi = lax.ppermute(dn, "cells", [(i + 1, i) for i in range(n - 1)])
    return lo, hi


def after(first, *later):
    return lax.optimization_barrier((first, *later))[1:]


def shards(spectrum_start, input_coef, white_coef, wind_speed, wind_angle, sea_mask, cotangent):
    nf, _, rows, nc = spectrum_start.shape
    n = lax.axis_size("spec")
    tab, dirs = jnp.asarray(TABLE), jnp.asarray(DIRS)
    big = vmem(nf, ND, rows, nc)
    band = f32(nf, MISC + MROWS, nc)
    line, duo, hs, sums = f32(nf, NL, nc), f32(2, nf, nc), f32(nf, rows, nc), f32(5, nf, rows, nc)
    flat, two, push = f32(rows, nc), f32(2, rows, nc), f32(8, nc)
    stream = [vmem(NBUF, ND, rows, nc), pltpu.SemaphoreType.DMA((NBUF,))]
    heavy = dict(limit=8)

    s_up, s_dn = call(
        edge_kernel, "edge", [band, band], [spectrum_start, sea_mask, input_coef, white_coef, wind_speed, wind_angle],
        [
            vmem(nf, NL, 8, nc), vmem(nf, NL, 8, nc), pltpu.SemaphoreType.DMA((2, nf)), vmem(4, rows, nc),
            pltpu.VMEM((rows, nc), jnp.int32), pltpu.SemaphoreType.DMA((5,)),
        ],
        hbm=range(6), **heavy,
    )
    s_lo, s_hi = exchange(s_up, s_dn)
    (mask,) = after(s_up, sea_mask)
    start, t0_part = call(
        start_kernel, "start", [big, f32(2 * rows + 8, nc)], [spectrum_start, tab, mask],
        [pltpu.SemaphoreType.DMA((nf,)), pltpu.SMEM(tab.shape, F32), pltpu.SemaphoreType.DMA(()), vmem(2, 5, rows, nc)],
        hbm=range(2), **heavy,
    )
    t0_parts = peers(t0_part)
    (speed,) = after(t0_part, wind_speed)
    p, al, p_up, p_dn = call(
        wind_kernel, "wind", [big, vmem(ND, rows, nc), band, band], [tab, cotangent, input_coef, speed, wind_angle],
        [pltpu.SemaphoreType.DMA((nf,)), vmem(ND, rows, nc)], hbm=(1,), **heavy,
    )
    (t0_own,) = after(p_up, t0_part)
    tot0, e_up, e_dn = call(functools.partial(total_kernel, rows), "total", [f32(2 * rows + 8, nc), push, push], [t0_own, *t0_parts])
    e_lo, e_hi = exchange(e_up, e_dn)
    (mask,) = after(tot0, sea_mask)
    u, s5, u_lo, u_hi, sy = call(
        grown_kernel, "grown", [big, sums, line, line, duo], [tab, dirs, start, mask, input_coef, wind_speed, al, s_lo, s_hi],
        [vmem(2, NL, nc), vmem(rows, nc)], held=(2, 6), **heavy,
    )
    t0, t0h, h0, h0h, t1_part = call(
        functools.partial(first_kernel, nf), "first", [two, push, hs, duo, f32(2 * rows, nc)],
        [tab, tot0, e_lo, e_hi, s_lo, s_hi, sea_mask, white_coef, s5, sy],
    )
    t1_parts = peers(t1_part)
    p_up, p_dn = after(t1_part, p_up, p_dn)
    p_lo, p_hi = exchange(p_up, p_dn)
    r5, t5 = call(product_kernel, "product", [sums, sums], [tab, u, p, al, u_lo, u_hi], held=(1, 2, 3), **heavy)
    (t1_own,) = after(r5, t1_part)
    t1, h1, d1_part = call(
        functools.partial(second_kernel, nf, n), "second", [two, hs, flat],
        [tab, t1_own, *t1_parts, sea_mask, white_coef, h0, h0h, r5],
    )
    d1_parts = [d1_part] + peers(d1_part)
    d1, v1, d0_part, f1, b_up, b_dn = call(
        functools.partial(third_kernel, nf, n), "third", [flat, hs, f32(rows + 8, nc), flat, push, push],
        [tab, *d1_parts, sea_mask, white_coef, wind_speed, t1, h0, h0h, h1, s5, sy, r5, t5],
    )
    b_lo, b_hi = exchange(b_up, b_dn)
    (d0_part,) = call(functools.partial(fourth_kernel, rows), "fourth", [f32(rows + 8, nc)], [d0_part, b_lo, b_hi])
    d0_parts = peers(d0_part)
    z, z_lo, z_hi, f_part = call(
        back_kernel, "back", [big, line, line, flat],
        [tab, dirs, p, u, input_coef, al, h0, h0h, h1, v1, p_lo, p_hi, s_lo, s_hi, b_lo, b_hi, f1, wind_speed],
        [vmem(2, NL, nc), vmem(2, 2, 8, nc), vmem(rows, nc), vmem(rows, nc)], held=(2, 3, 5), **heavy,
    )
    (d0_own,) = after(f_part, d0_part)
    f_parts = peers(f_part)
    out, grad_white = call(
        functools.partial(out_kernel, n), "out", [f32(nf, ND, rows, nc), flat],
        [tab, d0_own, *d0_parts, z, z_lo, z_hi, t0, t0h, t1, d1, sea_mask, white_coef, s_lo, s_hi],
        [vmem(2, rows, nc), vmem(2, 8, nc), vmem(2, NL, nc), vmem(2, rows, nc)] + stream, held=(1 + n,), out_hbm=(0,), **heavy,
    )
    grad_input = f_part
    for other in f_parts:
        grad_input = grad_input + other
    return out, time_step * grad_input, grad_white


def solution(mesh):
    return jax.shard_map(
        shards,
        mesh=mesh,
        in_specs=(
            P("spec", None, "cells", None),
            P("cells", None),
            P("cells", None),
            P("cells", None),
            P("cells", None),
            P("cells", None),
            P("spec", None, "cells", None),
        ),
        out_specs=(P("spec", None, "cells", None), P("cells", None), P("cells", None)),
        check_vma=False,
    )
```

```python
import functools
import math

import jax
import jax.numpy as jnp
import numpy as np
from jax import lax
from jax.experimental import pallas as pl
from jax.experimental.pallas import tpu as pltpu
from jax.sharding import PartitionSpec as P

NF = 32
ND = 36
STEPS = 2

epsilon = 1e-06
energy_ref = 0.5
time_step = 0.5
courant = 0.7
ratio_step = 1.1

F32 = jnp.float32
LOG2E = math.log2(math.e)

_every = np.exp(np.arange(NF, dtype=np.float32) * np.float32(math.log(ratio_step))).astype(np.float32)
_total = _every.sum(dtype=np.float32)
HIGHEST = float(_every[-1])
MEAN_RATIO = float((_every * _every).sum(dtype=np.float32) / _total)
_weights = _every / (np.float32(ND) * _total)
_q = (_every / _every[-1]) ** 2
NTAB = 5
TABLE = np.stack([_every, 1 / _every, _weights, _q, _weights * _every], axis=1).astype(np.float32).reshape(-1)

_angle = (np.float32(2.0 * math.pi) * np.arange(ND, dtype=np.float32) / np.float32(ND)).astype(np.float32)
COS, SIN = np.cos(_angle).astype(np.float32), np.sin(_angle).astype(np.float32)
KX, KY = np.float32(courant) * np.abs(COS), np.float32(courant) * np.abs(SIN)
XP, YP = [bool(c >= 0) for c in COS], [bool(s >= 0) for s in SIN]
NL = sum(YP)
NH = ND - NL
assert YP == [True] * NL + [False] * NH and NL == NH
QUADS = [[d for d in range(ND) if (XP[d], YP[d]) == quad] for quad in ((1, 1), (0, 1), (0, 0), (1, 0))]
DIRS = np.stack([v[a:b] for a, b in ((0, NL), (NL, ND)) for v in (KX, KY, COS, SIN)]).astype(np.float32)
DIRS = np.ascontiguousarray(np.broadcast_to(DIRS[:, :, None], DIRS.shape + (128,)))
MISC = 2 * NL
MROWS = 4
NMISC = 5

MIB = 1 << 20


def coef(tab, j, nf, which):
    return tab[(lax.axis_index("spec") * nf + j) * NTAB + which]


def shift_x(x, plus):
    return pltpu.roll(x, 1 if plus else x.shape[1] - 1, 1)


def first_row(x):
    return lax.broadcasted_iota(jnp.int32, x.shape, 0) == 0


def last_row(x):
    return lax.broadcasted_iota(jnp.int32, x.shape, 0) == x.shape[0] - 1


def from_before(x, above):
    return jnp.where(first_row(x), above, pltpu.roll(x, 1, 0))


def from_after(x, below):
    return jnp.where(last_row(x), below, pltpu.roll(x, x.shape[0] - 1, 0))


def shift_y(x, plus, outside):
    return from_before(x, outside) if plus else from_after(x, outside)


def damping_of(energy, moment):
    shifted = energy + epsilon
    ratio = moment / (shifted * MEAN_RATIO)
    r2 = ratio * ratio
    steep = energy * (r2 * r2) / energy_ref
    return shifted, ratio, steep, steep * steep * ratio


def grads_of(energy, moment, white, damp_total):
    shifted, ratio, steep, damping = damping_of(energy, moment)
    grad_damp = -time_step * white * damp_total
    grad_ratio = 9.0 * grad_damp * steep * steep
    r2 = ratio * ratio
    grad_energy = grad_damp * 2.0 * steep * (r2 * r2) * ratio / energy_ref - grad_ratio * ratio / shifted
    grad_moment = grad_ratio / (shifted * MEAN_RATIO)
    return grad_energy, grad_moment, damping


def gate(q, white, damping, ocean):
    return ocean * jnp.exp2((-time_step * LOG2E) * q * (white * damping))


def rows_from(tiles, plus, outside):
    moved = [pltpu.roll(x, 1 if plus else 7, 0) for x in tiles]
    mark = first_row(tiles[0]) if plus else last_row(tiles[0])
    feed = [outside] + moved[:-1] if plus else moved[1:] + [outside]
    return [jnp.where(mark, a, b) for a, b in zip(feed, moved)]


def slab(ref, *index):
    return [ref[(*index, slice(t, t + 8))] for t in range(0, ref.shape[-2], 8)]


def by_parity(write, first, second):
    odd = lax.rem(lax.axis_index("cells"), 2)

    @pl.when(odd == 0)
    def _():
        write(first, second)

    @pl.when(odd == 1)
    def _():
        write(second, first)


class Either:
    def __init__(self, even, odd):
        self.even, self.odd, self.shape = even, odd, even.shape

    def __getitem__(self, at):
        x, y = self.even[at], self.odd[at]
        return jnp.where(jnp.full(x.shape, lax.rem(lax.axis_index("cells"), 2), jnp.int32) == 0, x, y)


def beside(first, second):
    return Either(second, first), Either(first, second)


def misc_at(r, k):
    m = r * NMISC + k
    return m // MROWS, MISC + m % MROWS


def misc_row(ref, r, k):
    j, row = misc_at(r, k)
    return ref[j, row : row + 1, :]


def halo_rows(ref, j, r):
    return ref[j, r * NL : (r + 1) * NL, :]


def fetches(hbm, ref, sems):
    return lambda j: pltpu.make_async_copy(hbm.at[j], ref.at[j], sems.at[j])


NBUF = 3


def edge_kernel(s_hbm, mask_h, coef_h, white_h, speed_h, angle_h, a_ref, b_ref, low, high, sems, fields, ints, small_sems):
    nf, _, rows, nc = s_hbm.shape

    def fetch(j):
        return (
            pltpu.make_async_copy(s_hbm.at[j, 0:NL, rows - 8 : rows, :], low.at[j], sems.at[0, j]),
            pltpu.make_async_copy(s_hbm.at[j, NL:ND, 0:8, :], high.at[j], sems.at[1, j]),
        )

    smalls = [pltpu.make_async_copy(mask_h, ints, small_sems.at[0])]
    for k, f in enumerate((coef_h, white_h, speed_h, angle_h)):
        smalls.append(pltpu.make_async_copy(f, fields.at[k], small_sems.at[1 + k]))
    for c in smalls:
        c.start()
    for j in range(nf):
        for c in fetch(j):
            c.start()
    for c in smalls:
        c.wait()

    def write(up_ref, dn_ref):
        @pl.loop(0, nf)
        def _(j):
            up_ref[j, MISC:, :] = jnp.zeros_like(up_ref[j, MISC:, :])
            dn_ref[j, MISC:, :] = jnp.zeros_like(dn_ref[j, MISC:, :])

        for side, out in ((slice(rows - 2, rows), up_ref), (slice(0, 2), dn_ref)):
            kappa = (time_step * LOG2E / HIGHEST) * (fields[0, side] * fields[2, side])
            angle = fields[3, side]
            for k, v in enumerate((kappa, jnp.cos(angle), jnp.sin(angle), ints[side].astype(F32), fields[1, side])):
                for r in range(2):
                    a, b = misc_at(r, k)
                    out[a, b : b + 1, :] = v[r : r + 1]

        @pl.loop(0, nf)
        def _(j):
            for c in fetch(j):
                c.wait()
            for r in range(2):
                for d in range(NL):
                    up_ref[j, r * NL + d : r * NL + d + 1, :] = low[j, d, 6 + r : 7 + r, :]
                    dn_ref[j, r * NL + d : r * NL + d + 1, :] = high[j, d, r : r + 1, :]

    by_parity(write, a_ref, b_ref)


def start_kernel(s_hbm, tab_h, mask, s_ref, t0_ref, sems, tab, small_sem, sums):
    nf = s_hbm.shape[0]
    rows, nc = mask.shape
    fetch = fetches(s_hbm, s_ref, sems)
    get_tab = pltpu.make_async_copy(tab_h, tab, small_sem)
    get_tab.start()
    for j in range(nf):
        fetch(j).start()
    sums[...] = jnp.zeros_like(sums)
    get_tab.wait()

    @pl.loop(0, nf)
    def _(j):
        rj, w, wf = [coef(tab, j, nf, k) for k in (1, 2, 4)]
        fetch(j).wait()
        for t in range(0, rows, 8):
            acc = [None] * 5

            def add(k, v):
                acc[k] = v if acc[k] is None else acc[k] + v

            for d in range(ND):
                x = s_ref[j, d, t : t + 8, :]
                add(0, x)
                add(1 if XP[d] else 2, float(KX[d]) * x)
                add(3 if YP[d] else 4, float(KY[d]) * x)
            for k in range(5):
                sums[0, k, t : t + 8, :] += (w if k == 0 else w * rj) * acc[k]
                sums[1, k, t : t + 8, :] += (wf if k == 0 else wf * rj) * acc[k]

    ocean = mask[...].astype(F32)
    t0_ref[2 * rows :, :] = jnp.zeros_like(t0_ref[2 * rows :, :])
    for e in range(2):
        total, xp, xm, yp, ym = [ocean * sums[e, k] for k in range(5)]
        t0_ref[e * rows : (e + 1) * rows, :] = total + (
            shift_x(xp, True) + shift_x(xm, False) + from_before(yp, 0.0) + from_after(ym, 0.0) - (xp + xm + yp + ym)
        )
        t0_ref[2 * rows + e : 2 * rows + e + 1, :] = yp[rows - 1 : rows]
        t0_ref[2 * rows + 2 + e : 2 * rows + 3 + e, :] = ym[0:1]


def wind_kernel(tab, lam_hbm, coef_in, speed, angle, p_ref, al_ref, a_ref, b_ref, sems, expo):
    nf = lam_hbm.shape[0]
    rows, nc = angle.shape
    fetch = fetches(lam_hbm, p_ref, sems)
    for j in range(nf):
        fetch(j).start()
    for ref in (a_ref, b_ref):
        ref[:, MISC:, :] = jnp.zeros_like(ref[:, MISC:, :])
    kappa = (time_step * LOG2E / HIGHEST) * (coef_in[...] * speed[...])
    ca, sa = jnp.cos(angle[...]), jnp.sin(angle[...])
    for d in range(ND):
        align = jnp.maximum(float(COS[d]) * ca + float(SIN[d]) * sa, 0.0)
        al = align * align
        al_ref[d] = al
        expo[d] = kappa * al

    def write(up_ref, dn_ref):
        @pl.loop(0, nf)
        def _(j):
            fr = coef(tab, j, nf, 0)
            fetch(j).wait()
            for d in range(ND):
                p = jnp.exp2(fr * expo[d]) * p_ref[j, d]
                p_ref[j, d] = p
                for r in range(2):
                    at = slice(r * NL + d % NL, r * NL + d % NL + 1)
                    if d < NL:
                        dn_ref[j, at, :] = p[r : r + 1]
                    else:
                        up_ref[j, at, :] = p[rows - 2 + r : rows - 1 + r]

    by_parity(write, a_ref, b_ref)


def halo_growth(fr, dirs, half, misc, r):
    cosd, sind = dirs[4 * half + 2][:, 0:1], dirs[4 * half + 3][:, 0:1]
    align = jnp.maximum(cosd * misc_row(misc, r, 1) + sind * misc_row(misc, r, 2), 0.0)
    return jnp.exp2(fr * (misc_row(misc, r, 0) * (align * align)))


def halo_adv(rj, dirs, half, near, far, transpose):
    kx, ky, cosd = [dirs[4 * half + k][:, 0:1] for k in range(3)]
    before, after = shift_x(near, not transpose), shift_x(near, transpose)
    moved = jnp.where(cosd >= 0, before, after)
    return near + rj * (kx * (moved - near) + ky * (far - near))


def grown_kernel(tab, dirs, s_ref, mask, coef_in, speed, al_ref, s_first, s_second, u_ref, sum_ref, ul_ref, uh_ref, sy_ref, edge, work):
    nf, _, rows, nc = s_ref.shape
    lo, hi = beside(s_first, s_second)
    ocean = mask[...].astype(F32)

    @pl.loop(0, nf)
    def _(j):
        fr, rj = coef(tab, j, nf, 0), coef(tab, j, nf, 1)
        for half, (blk, near, far, out) in enumerate(((lo, 1, 0, ul_ref), (hi, 0, 1, uh_ref))):
            x = [misc_row(blk, r, 3) * halo_rows(blk, j, r) for r in range(2)]
            edge[half] = rj * x[near]
            u = halo_growth(fr, dirs, half, blk, near) * halo_adv(rj, dirs, half, x[near], x[far], False)
            out[j] = u
            sy_ref[half, pl.ds(j, 1), :] = jnp.sum(dirs[4 * half + 1][:, 0:1] * u, axis=0, keepdims=True)
        tiles = range(rows // 8)
        work[...] = (fr * (time_step * LOG2E / HIGHEST)) * (coef_in[...] * speed[...])
        oj = [rj * ocean[8 * t : 8 * t + 8] for t in tiles]
        seen = set()
        for quad in QUADS:
            acc = [[None] * 3 for _ in tiles]
            for d in quad:
                kx, ky = float(KX[d]), float(KY[d])
                x = [o * v for o, v in zip(oj, slab(s_ref, j, d))]
                row = edge[0, d : d + 1, :] if YP[d] else edge[1, d - NL : d - NL + 1, :]
                y = rows_from(x, YP[d], row)
                for t in tiles:
                    u = jnp.exp2(work[8 * t : 8 * t + 8] * al_ref[d, 8 * t : 8 * t + 8]) * (
                        (fr - (kx + ky)) * x[t] + kx * shift_x(x[t], XP[d]) + ky * y[t]
                    )
                    u_ref[j, d, 8 * t : 8 * t + 8, :] = u
                    for k, v in enumerate((u, kx * u, ky * u)):
                        acc[t][k] = v if acc[t][k] is None else acc[t][k] + v
            for k, key in enumerate((0, 1 if XP[quad[0]] else 2, 3 if YP[quad[0]] else 4)):
                for t in tiles:
                    at = (key, j, slice(8 * t, 8 * t + 8))
                    sum_ref[at] = sum_ref[at] + acc[t][k] if key in seen else acc[t][k]
                seen.add(key)
        for t in tiles:
            a, b, c, d, e = [sum_ref[k, j, 8 * t : 8 * t + 8, :] for k in range(5)]
            sum_ref[0, j, 8 * t : 8 * t + 8, :] = a - rj * (b + c + d + e)


def product_kernel(tab, u_ref, p_ref, al_ref, ul_ref, uh_ref, r_ref, t_ref):
    nf, _, rows, nc = u_ref.shape

    @pl.loop(0, nf)
    def _(j):
        rj = coef(tab, j, nf, 1)
        for t in range(0, rows, 8):
            seen = set()
            for quad in QUADS:
                acc = [None] * 6
                for d in quad:
                    kx, ky = float(KX[d]), float(KY[d])
                    u, p, al = u_ref[j, d, t : t + 8, :], p_ref[j, d, t : t + 8, :], al_ref[d, t : t + 8, :]
                    if YP[d]:
                        row = ul_ref[j, d : d + 1, :] if t == 0 else u_ref[j, d, t - 1 : t, :]
                        y = jnp.where(first_row(u), row, pltpu.roll(u, 1, 0))
                    else:
                        row = uh_ref[j, d - NL : d - NL + 1, :] if t + 8 == rows else u_ref[j, d, t + 8 : t + 9, :]
                        y = jnp.where(last_row(u), row, pltpu.roll(u, 7, 0))
                    cu = (1.0 - rj * (kx + ky)) * (p * u)
                    px, py = kx * (p * shift_x(u, XP[d])), ky * (p * y)
                    for k, v in enumerate((cu, px, py, al * cu, al * px, al * py)):
                        acc[k] = v if acc[k] is None else acc[k] + v
                xk, yk = (1 if XP[quad[0]] else 2), (3 if YP[quad[0]] else 4)
                for k, ref in enumerate((r_ref, t_ref)):
                    for key, v in zip((0, xk, yk), acc[3 * k : 3 * k + 3]):
                        at = (key, j, slice(t, t + 8))
                        ref[at] = ref[at] + v if (k, key) in seen else v
                        seen.add((k, key))


def total_kernel(rows, *refs):
    parts, (tot, first, second) = refs[:-3], refs[-3:]
    total = parts[0][...]
    for part in parts[1:]:
        total = total + part[...]
    tot[...] = total

    def write(up, dn):
        up[...] = jnp.zeros_like(up)
        dn[...] = jnp.zeros_like(dn)
        for k, row in enumerate((rows - 1, 2 * rows - 1, 2 * rows, 2 * rows + 1)):
            up[k : k + 1, :] = total[row : row + 1]
        for k, row in enumerate((0, rows, 2 * rows + 2, 2 * rows + 3)):
            dn[k : k + 1, :] = total[row : row + 1]

    by_parity(write, first, second)


def advected_sum(rj, h, above, below, s):
    return h * s[0], rj * (
        shift_x(h * s[1], True) + shift_x(h * s[2], False) + from_before(h * s[3], above) + from_after(h * s[4], below)
    )


def first_kernel(nf, tab, tot, e_first, e_second, s_first, s_second, mask, white, sum_ref, sy_ref, t0_ref, t0h_ref, h0_ref, h0h_ref, t1_ref):
    rows, nc = mask.shape
    lo, hi = beside(e_first, e_second)
    lo_misc, hi_misc = beside(s_first, s_second)
    ocean = mask[...].astype(F32)
    row = lax.broadcasted_iota(jnp.int32, (rows, nc), 0)
    total = tot[...]
    field = []
    halo = []
    t0h_ref[...] = jnp.zeros_like(t0h_ref)
    for k in range(2):
        v = total[k * rows : (k + 1) * rows]
        v = v + jnp.where(row == 0, lo[2 + k : 3 + k, :], 0.0) + jnp.where(row == rows - 1, hi[2 + k : 3 + k, :], 0.0)
        field.append(ocean * v)
        t0_ref[k] = field[k]
        above = misc_row(lo_misc, 1, 3) * (lo[k : k + 1, :] + total[2 * rows + 2 + k : 2 * rows + 3 + k])
        below = misc_row(hi_misc, 0, 3) * (hi[k : k + 1, :] + total[2 * rows + k : 2 * rows + 1 + k])
        halo.append((above, below))
        t0h_ref[k : k + 1, :] = above
        t0h_ref[2 + k : 3 + k, :] = below
    damping = damping_of(*field)[3]
    damp_lo = damping_of(halo[0][0], halo[1][0])[3]
    damp_hi = damping_of(halo[0][1], halo[1][1])[3]
    energy, moment = jnp.zeros((rows, nc), F32), jnp.zeros((rows, nc), F32)
    for j in range(nf):
        rj, w, q, wf = [coef(tab, j, nf, k) for k in (1, 2, 3, 4)]
        h = gate(q, white[...], damping, ocean)
        h_lo = gate(q, misc_row(lo_misc, 1, 4), damp_lo, misc_row(lo_misc, 1, 3))
        h_hi = gate(q, misc_row(hi_misc, 0, 4), damp_hi, misc_row(hi_misc, 0, 3))
        h0_ref[j] = h
        h0h_ref[0, j : j + 1, :] = h_lo
        h0h_ref[1, j : j + 1, :] = h_hi
        centre, around = advected_sum(
            rj, h, h_lo * sy_ref[0, j : j + 1, :], h_hi * sy_ref[1, j : j + 1, :], [sum_ref[k, j] for k in range(5)]
        )
        adv = centre + around
        energy, moment = energy + w * adv, moment + wf * adv
    t1_ref[0:rows, :] = energy
    t1_ref[rows : 2 * rows, :] = moment


def gathered(rj, h, h_lo, h_hi, r):
    return h * r[0] + rj * (
        shift_x(h, True) * r[1] + shift_x(h, False) * r[2] + from_before(h, h_lo) * r[3] + from_after(h, h_hi) * r[4]
    )


def second_kernel(nf, n, tab, *refs):
    parts, (mask, white, h0_ref, h0h_ref, r_ref, t1_ref, h1_ref, d1_ref) = refs[:n], refs[n:]
    rows, nc = mask.shape
    ocean = mask[...].astype(F32)
    total = parts[0][...]
    for part in parts[1:]:
        total = total + part[...]
    energy, moment = ocean * total[:rows], ocean * total[rows:]
    t1_ref[0] = energy
    t1_ref[1] = moment
    damping = damping_of(energy, moment)[3]
    acc = jnp.zeros((rows, nc), F32)
    for j in range(nf):
        rj, q = coef(tab, j, nf, 1), coef(tab, j, nf, 3)
        h1 = gate(q, white[...], damping, ocean)
        h1_ref[j] = h1
        part = gathered(rj, h0_ref[j], h0h_ref[0, j : j + 1, :], h0h_ref[1, j : j + 1, :], [r_ref[k, j] for k in range(5)])
        acc = acc + q * (h1 * part)
    d1_ref[...] = acc


def third_kernel(nf, n, tab, *refs):
    parts = refs[:n]
    mask, white, speed, t1, h0_ref, h0h_ref, h1_ref, sum_ref, sy_ref, r_ref, t_ref = refs[n : n + 11]
    d1_ref, v1_ref, d0_ref, f1_ref, first, second = refs[n + 11 :]
    rows, nc = mask.shape
    ocean = mask[...].astype(F32)
    damp = parts[0][...]
    for part in parts[1:]:
        damp = damp + part[...]
    d1_ref[...] = damp
    grad_e, grad_m, _ = grads_of(t1[0], t1[1], white[...], damp)
    acc, force = jnp.zeros((rows, nc), F32), jnp.zeros((rows, nc), F32)
    push_lo, push_hi = jnp.zeros((1, nc), F32), jnp.zeros((1, nc), F32)
    for j in range(nf):
        fr, rj, w, q = [coef(tab, j, nf, k) for k in range(4)]
        h0, h1 = h0_ref[j], h1_ref[j]
        h_lo, h_hi = h0h_ref[0, j : j + 1, :], h0h_ref[1, j : j + 1, :]
        v1 = ocean * (w * (grad_e + fr * grad_m))
        v1_ref[j] = v1
        s, r = [sum_ref[k, j] for k in range(5)], [r_ref[k, j] for k in range(5)]
        inner = (
            shift_x(h1 * r[1], False)
            + shift_x(h1 * r[2], True)
            + from_after(h1 * r[3], 0.0)
            + from_before(h1 * r[4], 0.0)
            + s[1] * shift_x(v1, False)
            + s[2] * shift_x(v1, True)
            + s[3] * from_after(v1, 0.0)
            + s[4] * from_before(v1, 0.0)
        )
        acc = acc + q * (h0 * (h1 * r[0] + v1 * s[0] + rj * inner))
        push_lo = push_lo + (q * rj) * (h_lo * (h1[0:1] * r[3][0:1] + v1[0:1] * sy_ref[0, j : j + 1, :]))
        e = rows - 1
        push_hi = push_hi + (q * rj) * (
            h_hi * (h1[e : e + 1] * r[4][e : e + 1] + v1[e : e + 1] * sy_ref[1, j : j + 1, :])
        )
        part = gathered(rj, h0, h_lo, h_hi, [t_ref[k, j] for k in range(5)])
        force = force + fr * (h1 * part)
    def write(up, dn):
        for k, v in enumerate((t1[0], t1[1], damp)):
            up[2 * k : 2 * k + 2, :] = v[rows - 2 : rows]
            dn[2 * k : 2 * k + 2, :] = v[0:2]
        up[6:7, :] = acc[rows - 1 : rows]
        up[7:8, :] = push_hi
        dn[6:7, :] = acc[0:1]
        dn[7:8, :] = push_lo

    by_parity(write, first, second)
    d0_ref[0:rows, :] = acc
    d0_ref[rows:, :] = jnp.zeros_like(d0_ref[rows:, :])
    d0_ref[rows : rows + 1, :] = push_lo
    d0_ref[rows + 1 : rows + 2, :] = push_hi
    f1_ref[...] = (speed[...] / HIGHEST) * force


def back_kernel(tab, dirs, p_ref, u_ref, coef_in, al_ref, h0_ref, h0h_ref, h1_ref, v1_ref, p_first, p_second, s_first, s_second, b_first, b_second, f1_ref, speed, z_ref, zl_ref, zh_ref, f_ref, edge, halo, scaled, work):
    nf, _, rows, nc = p_ref.shape
    pl_ref, ph_ref = beside(p_first, p_second)
    lo_misc, hi_misc = beside(s_first, s_second)
    lo, hi = beside(b_first, b_second)
    sides = ((0, ph_ref, hi_misc, hi, 0, 1, 1, zh_ref), (1, pl_ref, lo_misc, lo, 1, 0, 0, zl_ref))
    for side, (_, _, misc, got, *_) in enumerate(sides):
        for r in range(2):
            energy, moment, damp = [got[2 * k + r : 2 * k + r + 1, :] for k in range(3)]
            white = misc_row(misc, r, 4)
            grad_e, grad_m, damping = grads_of(energy, moment, white, damp)
            for k, v in enumerate((grad_e, grad_m, white * damping)):
                halo[side, r, k : k + 1, :] = v
    f_ref[...] = jnp.zeros_like(f_ref)

    @pl.loop(0, nf)
    def _(j):
        fr, rj = coef(tab, j, nf, 0), coef(tab, j, nf, 1)
        w, q = coef(tab, j, nf, 2), coef(tab, j, nf, 3)
        for side, (half, blk, misc, _, near, far, which, out) in enumerate(sides):
            x = []
            for r in range(2):
                ocean = misc_row(misc, r, 3)
                h = gate(q, halo[side, r, 2:3, :], 1.0, ocean)
                v = ocean * (w * (halo[side, r, 0:1, :] + fr * halo[side, r, 1:2, :]))
                x.append(halo_rows(blk, j, r) * h + v)
            edge[side] = x[near]
            moved = halo_adv(rj, dirs, half, x[near], x[far], True) * halo_growth(fr, dirs, half, misc, near)
            out[j] = moved * h0h_ref[which, pl.ds(j, 1), :]
        tiles = range(rows // 8)
        at8 = [slice(8 * t, 8 * t + 8) for t in tiles]
        work[...] = (fr * (time_step * LOG2E / HIGHEST)) * (coef_in[...] * speed[...])
        for t in tiles:
            scaled[at8[t]] = rj * h0_ref[j, at8[t]]
        force = [None for _ in tiles]
        for d in range(ND):
            kx, ky = float(KX[d]), float(KY[d])
            x = [p_ref[j, d, at8[t]] * h1_ref[j, at8[t]] + v1_ref[j, at8[t]] for t in tiles]
            row = edge[0, d : d + 1, :] if YP[d] else edge[1, d - NL : d - NL + 1, :]
            y = rows_from(x, not YP[d], row)
            for t in tiles:
                back = (fr - (kx + ky)) * x[t] + kx * shift_x(x[t], not XP[d]) + ky * y[t]
                al = al_ref[d, at8[t]]
                v = al * (back * u_ref[j, d, at8[t]])
                force[t] = v if force[t] is None else force[t] + v
                z_ref[j, d, at8[t]] = back * (jnp.exp2(work[at8[t]] * al) * scaled[at8[t]])
        for t in tiles:
            f_ref[at8[t]] += fr * (scaled[at8[t]] * force[t])

    f_ref[...] = (speed[...] / HIGHEST) * f_ref[...] + f1_ref[...]


def fourth_kernel(rows, part, first, second, out):
    lo, hi = beside(first, second)
    row = lax.broadcasted_iota(jnp.int32, (rows, out.shape[1]), 0)
    v = part[0:rows, :]
    v = v + jnp.where(row == 0, lo[7:8, :], 0.0) + jnp.where(row == rows - 1, hi[7:8, :], 0.0)
    out[0:rows, :] = v
    out[rows:, :] = jnp.zeros_like(out[rows:, :])
    out[rows : rows + 1, :] = part[rows : rows + 1, :] + lo[6:7, :]
    out[rows + 1 : rows + 2, :] = part[rows + 1 : rows + 2, :] + hi[6:7, :]


def out_kernel(n, tab, *refs):
    parts, refs = refs[:n], refs[n:]
    z_ref, zl_ref, zh_ref, t0, t0h, t1, d1, mask, white, s_first, s_second = refs[:11]
    lo_misc, hi_misc = beside(s_first, s_second)
    out_hbm, gw_ref, own, halo, edge, work, buf, sems = refs[11:]
    nf, _, rows, nc = z_ref.shape
    ocean = mask[...].astype(F32)
    total = parts[0][...]
    for part in parts[1:]:
        total = total + part[...]
    damp = total[0:rows]
    grad_e, grad_m, damping = grads_of(t0[0], t0[1], white[...], damp)
    own[0] = grad_e
    own[1] = grad_m
    gw_ref[...] = -time_step * (damping * damp + damping_of(t1[0], t1[1])[3] * d1[...])
    above, below = total[rows : rows + 1], total[rows + 1 : rows + 2]
    sides = ((hi_misc, 0, 2, below, zh_ref), (lo_misc, 1, 0, above, zl_ref))
    for side, (misc, r, k, damp, _) in enumerate(sides):
        e, m, _ = grads_of(t0h[k : k + 1, :], t0h[k + 1 : k + 2, :], misc_row(misc, r, 4), damp)
        halo[side, 0:1, :] = e
        halo[side, 1:2, :] = m

    def put(j):
        return pltpu.make_async_copy(buf.at[j % NBUF], out_hbm.at[j], sems.at[j % NBUF])

    @pl.loop(0, nf)
    def _(j):
        slot = j % NBUF
        fr, rj, w = [coef(tab, j, nf, k) for k in range(3)]
        for side, (misc, r, _, _, z) in enumerate(sides):
            edge[side] = z[j] + misc_row(misc, r, 3) * (w * (halo[side, 0:1, :] + fr * halo[side, 1:2, :]))
        tiles = range(rows // 8)
        o = [ocean[8 * t : 8 * t + 8] for t in tiles]
        v = [o[t] * (w * (own[0, 8 * t : 8 * t + 8] + fr * own[1, 8 * t : 8 * t + 8])) for t in tiles]
        for t in tiles:
            work[0, 8 * t : 8 * t + 8] = v[t]
            work[1, 8 * t : 8 * t + 8] = rj * o[t]

        @pl.when(j >= NBUF)
        def _():
            put(j - NBUF).wait()

        for d in range(ND):
            kx, ky = float(KX[d]), float(KY[d])
            x = [z + work[0, 8 * t : 8 * t + 8] for t, z in enumerate(slab(z_ref, j, d))]
            row = edge[0, d : d + 1, :] if YP[d] else edge[1, d - NL : d - NL + 1, :]
            y = rows_from(x, not YP[d], row)
            for t in tiles:
                back = (fr - (kx + ky)) * x[t] + kx * shift_x(x[t], not XP[d]) + ky * y[t]
                buf[slot, d, 8 * t : 8 * t + 8, :] = work[1, 8 * t : 8 * t + 8] * back
        put(j).start()

    for j in range(max(0, nf - NBUF), nf):
        put(j).wait()


VMEM = pl.BlockSpec(memory_space=pltpu.VMEM)
SMEM = pl.BlockSpec(memory_space=pltpu.SMEM)
HBM = pl.BlockSpec(memory_space=pltpu.HBM)


def f32(*shape):
    return jax.ShapeDtypeStruct(shape, F32)


def vmem(*shape):
    return pltpu.VMEM(shape, F32)


def call(kernel, name, outs, args, scratch=(), hbm=(), held=(), out_hbm=(), limit=6, alias=None):
    put = {**dict.fromkeys(hbm, pltpu.HBM), **dict.fromkeys(held, pltpu.VMEM)}
    args = [pltpu.with_memory_space_constraint(a, put[k]) if k in put else a for k, a in enumerate(args)]
    return pl.pallas_call(
        kernel,
        name=name,
        out_shape=outs,
        in_specs=[HBM if k in hbm else SMEM if a.ndim == 1 else VMEM for k, a in enumerate(args)],
        out_specs=[HBM if k in out_hbm else VMEM for k in range(len(outs))],
        scratch_shapes=list(scratch),
        input_output_aliases=alias or {},
        compiler_params=pltpu.CompilerParams(vmem_limit_bytes=limit * MIB),
        cost_estimate=pl.CostEstimate(flops=1, bytes_accessed=1, transcendentals=0),
    )(*args)


def peers(x):
    n = lax.axis_size("spec")
    if n & (n - 1) == 0:
        return [lax.ppermute(x, "spec", [(i, i ^ k) for i in range(n)]) for k in range(1, n)]
    return [lax.ppermute(x, "spec", [(i, (i + k) % n) for i in range(n)]) for k in range(1, n)]


def exchange(first, second):
    n = lax.axis_size("cells")
    swaps = [[(i, i + 1) for i in range(odd, n - 1, 2)] for odd in range(2)]
    return [lax.ppermute(x, "cells", pairs + [(b, a) for a, b in pairs]) for x, pairs in zip((first, second), swaps)]


def after(first, *later):
    return lax.optimization_barrier((first, *later))[1:]


def shards(spectrum_start, input_coef, white_coef, wind_speed, wind_angle, sea_mask, cotangent):
    nf, _, rows, nc = spectrum_start.shape
    n = lax.axis_size("spec")
    tab, dirs = jnp.asarray(TABLE), jnp.asarray(DIRS)
    big = vmem(nf, ND, rows, nc)
    band = f32(nf, MISC + MROWS, nc)
    line, duo, hs, sums = f32(nf, NL, nc), f32(2, nf, nc), f32(nf, rows, nc), f32(5, nf, rows, nc)
    flat, two, push = f32(rows, nc), f32(2, rows, nc), f32(8, nc)
    stream = [vmem(NBUF, ND, rows, nc), pltpu.SemaphoreType.DMA((NBUF,))]
    heavy = dict(limit=8)

    s_up, s_dn = call(
        edge_kernel, "edge", [band, band], [spectrum_start, sea_mask, input_coef, white_coef, wind_speed, wind_angle],
        [
            vmem(nf, NL, 8, nc), vmem(nf, NL, 8, nc), pltpu.SemaphoreType.DMA((2, nf)), vmem(4, rows, nc),
            pltpu.VMEM((rows, nc), jnp.int32), pltpu.SemaphoreType.DMA((5,)),
        ],
        hbm=range(6), **heavy,
    )
    s_lo, s_hi = exchange(s_up, s_dn)
    (mask,) = after(s_up, sea_mask)
    start, t0_part = call(
        start_kernel, "start", [big, f32(2 * rows + 8, nc)], [spectrum_start, tab, mask],
        [pltpu.SemaphoreType.DMA((nf,)), pltpu.SMEM(tab.shape, F32), pltpu.SemaphoreType.DMA(()), vmem(2, 5, rows, nc)],
        hbm=range(2), **heavy,
    )
    t0_parts = peers(t0_part)
    (speed,) = after(t0_part, wind_speed)
    p, al, p_up, p_dn = call(
        wind_kernel, "wind", [big, vmem(ND, rows, nc), band, band], [tab, cotangent, input_coef, speed, wind_angle],
        [pltpu.SemaphoreType.DMA((nf,)), vmem(ND, rows, nc)], hbm=(1,), **heavy,
    )
    (t0_own,) = after(p_up, t0_part)
    tot0, e_up, e_dn = call(functools.partial(total_kernel, rows), "total", [f32(2 * rows + 8, nc), push, push], [t0_own, *t0_parts])
    e_lo, e_hi = exchange(e_up, e_dn)
    (mask,) = after(tot0, sea_mask)
    u, s5, u_lo, u_hi, sy = call(
        grown_kernel, "grown", [big, sums, line, line, duo], [tab, dirs, start, mask, input_coef, wind_speed, al, s_lo, s_hi],
        [vmem(2, NL, nc), vmem(rows, nc)], held=(2, 6), **heavy,
    )
    t0, t0h, h0, h0h, t1_part = call(
        functools.partial(first_kernel, nf), "first", [two, push, hs, duo, f32(2 * rows, nc)],
        [tab, tot0, e_lo, e_hi, s_lo, s_hi, sea_mask, white_coef, s5, sy],
    )
    t1_parts = peers(t1_part)
    p_up, p_dn = after(t1_part, p_up, p_dn)
    p_lo, p_hi = exchange(p_up, p_dn)
    r5, t5 = call(product_kernel, "product", [sums, sums], [tab, u, p, al, u_lo, u_hi], held=(1, 2, 3), **heavy)
    (t1_own,) = after(r5, t1_part)
    t1, h1, d1_part = call(
        functools.partial(second_kernel, nf, n), "second", [two, hs, flat],
        [tab, t1_own, *t1_parts, sea_mask, white_coef, h0, h0h, r5],
    )
    d1_parts = [d1_part] + peers(d1_part)
    d1, v1, d0_part, f1, b_up, b_dn = call(
        functools.partial(third_kernel, nf, n), "third", [flat, hs, f32(rows + 8, nc), flat, push, push],
        [tab, *d1_parts, sea_mask, white_coef, wind_speed, t1, h0, h0h, h1, s5, sy, r5, t5],
    )
    b_lo, b_hi = exchange(b_up, b_dn)
    (d0_part,) = call(functools.partial(fourth_kernel, rows), "fourth", [f32(rows + 8, nc)], [d0_part, b_lo, b_hi])
    d0_parts = peers(d0_part)
    z, z_lo, z_hi, f_part = call(
        back_kernel, "back", [big, line, line, flat],
        [tab, dirs, p, u, input_coef, al, h0, h0h, h1, v1, p_lo, p_hi, s_lo, s_hi, b_lo, b_hi, f1, wind_speed],
        [vmem(2, NL, nc), vmem(2, 2, 8, nc), vmem(rows, nc), vmem(rows, nc)], held=(2, 3, 5), **heavy,
    )
    (d0_own,) = after(f_part, d0_part)
    f_parts = peers(f_part)
    out, grad_white = call(
        functools.partial(out_kernel, n), "out", [f32(nf, ND, rows, nc), flat],
        [tab, d0_own, *d0_parts, z, z_lo, z_hi, t0, t0h, t1, d1, sea_mask, white_coef, s_lo, s_hi],
        [vmem(2, rows, nc), vmem(2, 8, nc), vmem(2, NL, nc), vmem(2, rows, nc)] + stream, held=(1 + n,), out_hbm=(0,), **heavy,
    )
    grad_input = f_part
    for other in f_parts:
        grad_input = grad_input + other
    return out, time_step * grad_input, grad_white


def solution(mesh):
    return jax.shard_map(
        shards,
        mesh=mesh,
        in_specs=(
            P("spec", None, "cells", None),
            P("cells", None),
            P("cells", None),
            P("cells", None),
            P("cells", None),
            P("cells", None),
            P("spec", None, "cells", None),
        ),
        out_specs=(P("spec", None, "cells", None), P("cells", None), P("cells", None)),
        check_vma=False,
    )
```

```python
import functools
import math

import jax
import jax.numpy as jnp
import numpy as np
from jax import lax
from jax.experimental import pallas as pl
from jax.experimental.pallas import tpu as pltpu
from jax.sharding import PartitionSpec as P

NF = 32
ND = 36
STEPS = 2

epsilon = 1e-06
energy_ref = 0.5
time_step = 0.5
courant = 0.7
ratio_step = 1.1

F32 = jnp.float32
LOG2E = math.log2(math.e)

_every = np.exp(np.arange(NF, dtype=np.float32) * np.float32(math.log(ratio_step))).astype(np.float32)
_total = _every.sum(dtype=np.float32)
HIGHEST = float(_every[-1])
MEAN_RATIO = float((_every * _every).sum(dtype=np.float32) / _total)
_weights = _every / (np.float32(ND) * _total)
_q = (_every / _every[-1]) ** 2
NTAB = 5
TABLE = np.stack([_every, 1 / _every, _weights, _q, _weights * _every], axis=1).astype(np.float32).reshape(-1)

_angle = (np.float32(2.0 * math.pi) * np.arange(ND, dtype=np.float32) / np.float32(ND)).astype(np.float32)
COS, SIN = np.cos(_angle).astype(np.float32), np.sin(_angle).astype(np.float32)
KX, KY = np.float32(courant) * np.abs(COS), np.float32(courant) * np.abs(SIN)
XP, YP = [bool(c >= 0) for c in COS], [bool(s >= 0) for s in SIN]
NL = sum(YP)
NH = ND - NL
assert YP == [True] * NL + [False] * NH and NL == NH
QUADS = [[d for d in range(ND) if (XP[d], YP[d]) == quad] for quad in ((1, 1), (0, 1), (0, 0), (1, 0))]
DIRS = np.stack([v[a:b] for a, b in ((0, NL), (NL, ND)) for v in (KX, KY, COS, SIN)]).astype(np.float32)
DIRS = np.ascontiguousarray(np.broadcast_to(DIRS[:, :, None], DIRS.shape + (128,)))
MISC = 2 * NL
MROWS = 4
NMISC = 5

MIB = 1 << 20


def coef(tab, j, nf, which):
    return tab[(lax.axis_index("spec") * nf + j) * NTAB + which]


def shift_x(x, plus):
    return pltpu.roll(x, 1 if plus else x.shape[1] - 1, 1)


def first_row(x):
    return lax.broadcasted_iota(jnp.int32, x.shape, 0) == 0


def last_row(x):
    return lax.broadcasted_iota(jnp.int32, x.shape, 0) == x.shape[0] - 1


def from_before(x, above):
    return jnp.where(first_row(x), above, pltpu.roll(x, 1, 0))


def from_after(x, below):
    return jnp.where(last_row(x), below, pltpu.roll(x, x.shape[0] - 1, 0))


def shift_y(x, plus, outside):
    return from_before(x, outside) if plus else from_after(x, outside)


def damping_of(energy, moment):
    shifted = energy + epsilon
    ratio = moment / (shifted * MEAN_RATIO)
    r2 = ratio * ratio
    steep = energy * (r2 * r2) / energy_ref
    return shifted, ratio, steep, steep * steep * ratio


def grads_of(energy, moment, white, damp_total):
    shifted, ratio, steep, damping = damping_of(energy, moment)
    grad_damp = -time_step * white * damp_total
    grad_ratio = 9.0 * grad_damp * steep * steep
    r2 = ratio * ratio
    grad_energy = grad_damp * 2.0 * steep * (r2 * r2) * ratio / energy_ref - grad_ratio * ratio / shifted
    grad_moment = grad_ratio / (shifted * MEAN_RATIO)
    return grad_energy, grad_moment, damping


def gate(q, white, damping, ocean):
    return ocean * jnp.exp2((-time_step * LOG2E) * q * (white * damping))


def rows_from(tiles, plus, outside):
    moved = [pltpu.roll(x, 1 if plus else 7, 0) for x in tiles]
    mark = first_row(tiles[0]) if plus else last_row(tiles[0])
    feed = [outside] + moved[:-1] if plus else moved[1:] + [outside]
    return [jnp.where(mark, a, b) for a, b in zip(feed, moved)]


def slab(ref, *index):
    return [ref[(*index, slice(t, t + 8))] for t in range(0, ref.shape[-2], 8)]


def by_parity(write, first, second):
    odd = lax.rem(lax.axis_index("cells"), 2)

    @pl.when(odd == 0)
    def _():
        write(first, second)

    @pl.when(odd == 1)
    def _():
        write(second, first)


class Either:
    def __init__(self, even, odd):
        self.even, self.odd, self.shape = even, odd, even.shape

    def __getitem__(self, at):
        x, y = self.even[at], self.odd[at]
        return jnp.where(jnp.full(x.shape, lax.rem(lax.axis_index("cells"), 2), jnp.int32) == 0, x, y)


def beside(first, second):
    return Either(second, first), Either(first, second)


def misc_at(r, k):
    m = r * NMISC + k
    return m // MROWS, MISC + m % MROWS


def misc_row(ref, r, k):
    j, row = misc_at(r, k)
    return ref[j, row : row + 1, :]


def halo_rows(ref, j, r):
    return ref[j, r * NL : (r + 1) * NL, :]


def fetches(hbm, ref, sems):
    return lambda j: pltpu.make_async_copy(hbm.at[j], ref.at[j], sems.at[j])


NBUF = 3


def edge_kernel(s_hbm, mask_h, coef_h, white_h, speed_h, angle_h, a_ref, b_ref, low, high, sems, fields, ints, small_sems):
    nf, _, rows, nc = s_hbm.shape

    def fetch(j):
        return (
            pltpu.make_async_copy(s_hbm.at[j, 0:NL, rows - 8 : rows, :], low.at[j], sems.at[0, j]),
            pltpu.make_async_copy(s_hbm.at[j, NL:ND, 0:8, :], high.at[j], sems.at[1, j]),
        )

    smalls = [pltpu.make_async_copy(mask_h, ints, small_sems.at[0])]
    for k, f in enumerate((coef_h, white_h, speed_h, angle_h)):
        smalls.append(pltpu.make_async_copy(f, fields.at[k], small_sems.at[1 + k]))
    for c in smalls:
        c.start()
    for j in range(nf):
        for c in fetch(j):
            c.start()
    for c in smalls:
        c.wait()

    def write(up_ref, dn_ref):
        @pl.loop(0, nf)
        def _(j):
            up_ref[j, MISC:, :] = jnp.zeros_like(up_ref[j, MISC:, :])
            dn_ref[j, MISC:, :] = jnp.zeros_like(dn_ref[j, MISC:, :])

        for side, out in ((slice(rows - 2, rows), up_ref), (slice(0, 2), dn_ref)):
            kappa = (time_step * LOG2E / HIGHEST) * (fields[0, side] * fields[2, side])
            angle = fields[3, side]
            for k, v in enumerate((kappa, jnp.cos(angle), jnp.sin(angle), ints[side].astype(F32), fields[1, side])):
                for r in range(2):
                    a, b = misc_at(r, k)
                    out[a, b : b + 1, :] = v[r : r + 1]

        @pl.loop(0, nf)
        def _(j):
            for c in fetch(j):
                c.wait()
            for r in range(2):
                for d in range(NL):
                    up_ref[j, r * NL + d : r * NL + d + 1, :] = low[j, d, 6 + r : 7 + r, :]
                    dn_ref[j, r * NL + d : r * NL + d + 1, :] = high[j, d, r : r + 1, :]

    by_parity(write, a_ref, b_ref)


def start_kernel(s_hbm, tab_h, mask, s_ref, t0_ref, sems, tab, small_sem, sums):
    nf = s_hbm.shape[0]
    rows, nc = mask.shape
    fetch = fetches(s_hbm, s_ref, sems)
    get_tab = pltpu.make_async_copy(tab_h, tab, small_sem)
    get_tab.start()
    for j in range(nf):
        fetch(j).start()
    sums[...] = jnp.zeros_like(sums)
    get_tab.wait()

    @pl.loop(0, nf)
    def _(j):
        rj, w, wf = [coef(tab, j, nf, k) for k in (1, 2, 4)]
        fetch(j).wait()
        for t in range(0, rows, 8):
            acc = [None] * 5

            def add(k, v):
                acc[k] = v if acc[k] is None else acc[k] + v

            for d in range(ND):
                x = s_ref[j, d, t : t + 8, :]
                add(0, x)
                add(1 if XP[d] else 2, float(KX[d]) * x)
                add(3 if YP[d] else 4, float(KY[d]) * x)
            for k in range(5):
                sums[0, k, t : t + 8, :] += (w if k == 0 else w * rj) * acc[k]
                sums[1, k, t : t + 8, :] += (wf if k == 0 else wf * rj) * acc[k]

    ocean = mask[...].astype(F32)
    t0_ref[2 * rows :, :] = jnp.zeros_like(t0_ref[2 * rows :, :])
    for e in range(2):
        total, xp, xm, yp, ym = [ocean * sums[e, k] for k in range(5)]
        t0_ref[e * rows : (e + 1) * rows, :] = total + (
            shift_x(xp, True) + shift_x(xm, False) + from_before(yp, 0.0) + from_after(ym, 0.0) - (xp + xm + yp + ym)
        )
        t0_ref[2 * rows + e : 2 * rows + e + 1, :] = yp[rows - 1 : rows]
        t0_ref[2 * rows + 2 + e : 2 * rows + 3 + e, :] = ym[0:1]


def wind_kernel(tab, lam_hbm, coef_in, speed, angle, p_ref, al_ref, a_ref, b_ref, sems, expo):
    nf = lam_hbm.shape[0]
    rows, nc = angle.shape
    fetch = fetches(lam_hbm, p_ref, sems)
    for j in range(nf):
        fetch(j).start()
    for ref in (a_ref, b_ref):
        ref[:, MISC:, :] = jnp.zeros_like(ref[:, MISC:, :])
    kappa = (time_step * LOG2E / HIGHEST) * (coef_in[...] * speed[...])
    ca, sa = jnp.cos(angle[...]), jnp.sin(angle[...])
    for d in range(ND):
        align = jnp.maximum(float(COS[d]) * ca + float(SIN[d]) * sa, 0.0)
        al = align * align
        al_ref[d] = al
        expo[d] = kappa * al

    def write(up_ref, dn_ref):
        @pl.loop(0, nf)
        def _(j):
            fr = coef(tab, j, nf, 0)
            fetch(j).wait()
            for d in range(ND):
                p = jnp.exp2(fr * expo[d]) * p_ref[j, d]
                p_ref[j, d] = p
                for r in range(2):
                    at = slice(r * NL + d % NL, r * NL + d % NL + 1)
                    if d < NL:
                        dn_ref[j, at, :] = p[r : r + 1]
                    else:
                        up_ref[j, at, :] = p[rows - 2 + r : rows - 1 + r]

    by_parity(write, a_ref, b_ref)


def halo_growth(fr, dirs, half, misc, r):
    cosd, sind = dirs[4 * half + 2][:, 0:1], dirs[4 * half + 3][:, 0:1]
    align = jnp.maximum(cosd * misc_row(misc, r, 1) + sind * misc_row(misc, r, 2), 0.0)
    return jnp.exp2(fr * (misc_row(misc, r, 0) * (align * align)))


def halo_adv(rj, dirs, half, near, far, transpose):
    kx, ky, cosd = [dirs[4 * half + k][:, 0:1] for k in range(3)]
    before, after = shift_x(near, not transpose), shift_x(near, transpose)
    moved = jnp.where(cosd >= 0, before, after)
    return near + rj * (kx * (moved - near) + ky * (far - near))


def grown_kernel(tab, dirs, s_ref, mask, coef_in, speed, al_ref, s_first, s_second, u_ref, sum_ref, ul_ref, uh_ref, sy_ref, edge, work):
    nf, _, rows, nc = s_ref.shape
    lo, hi = beside(s_first, s_second)
    ocean = mask[...].astype(F32)

    @pl.loop(0, nf)
    def _(j):
        fr, rj = coef(tab, j, nf, 0), coef(tab, j, nf, 1)
        for half, (blk, near, far, out) in enumerate(((lo, 1, 0, ul_ref), (hi, 0, 1, uh_ref))):
            x = [misc_row(blk, r, 3) * halo_rows(blk, j, r) for r in range(2)]
            edge[half] = rj * x[near]
            u = halo_growth(fr, dirs, half, blk, near) * halo_adv(rj, dirs, half, x[near], x[far], False)
            out[j] = u
            sy_ref[half, pl.ds(j, 1), :] = jnp.sum(dirs[4 * half + 1][:, 0:1] * u, axis=0, keepdims=True)
        tiles = range(rows // 8)
        work[...] = (fr * (time_step * LOG2E / HIGHEST)) * (coef_in[...] * speed[...])
        oj = [rj * ocean[8 * t : 8 * t + 8] for t in tiles]
        seen = set()
        for quad in QUADS:
            acc = [[None] * 3 for _ in tiles]
            for d in quad:
                kx, ky = float(KX[d]), float(KY[d])
                x = [o * v for o, v in zip(oj, slab(s_ref, j, d))]
                row = edge[0, d : d + 1, :] if YP[d] else edge[1, d - NL : d - NL + 1, :]
                y = rows_from(x, YP[d], row)
                for t in tiles:
                    u = jnp.exp2(work[8 * t : 8 * t + 8] * al_ref[d, 8 * t : 8 * t + 8]) * (
                        (fr - (kx + ky)) * x[t] + kx * shift_x(x[t], XP[d]) + ky * y[t]
                    )
                    u_ref[j, d, 8 * t : 8 * t + 8, :] = u
                    for k, v in enumerate((u, kx * u, ky * u)):
                        acc[t][k] = v if acc[t][k] is None else acc[t][k] + v
            for k, key in enumerate((0, 1 if XP[quad[0]] else 2, 3 if YP[quad[0]] else 4)):
                for t in tiles:
                    at = (key, j, slice(8 * t, 8 * t + 8))
                    sum_ref[at] = sum_ref[at] + acc[t][k] if key in seen else acc[t][k]
                seen.add(key)
        for t in tiles:
            a, b, c, d, e = [sum_ref[k, j, 8 * t : 8 * t + 8, :] for k in range(5)]
            sum_ref[0, j, 8 * t : 8 * t + 8, :] = a - rj * (b + c + d + e)


def product_kernel(tab, u_ref, p_ref, al_ref, ul_ref, uh_ref, r_ref, t_ref):
    nf, _, rows, nc = u_ref.shape

    @pl.loop(0, nf)
    def _(j):
        rj = coef(tab, j, nf, 1)
        for t in range(0, rows, 8):
            seen = set()
            for quad in QUADS:
                acc = [None] * 6
                for d in quad:
                    kx, ky = float(KX[d]), float(KY[d])
                    u, p, al = u_ref[j, d, t : t + 8, :], p_ref[j, d, t : t + 8, :], al_ref[d, t : t + 8, :]
                    if YP[d]:
                        row = ul_ref[j, d : d + 1, :] if t == 0 else u_ref[j, d, t - 1 : t, :]
                        y = jnp.where(first_row(u), row, pltpu.roll(u, 1, 0))
                    else:
                        row = uh_ref[j, d - NL : d - NL + 1, :] if t + 8 == rows else u_ref[j, d, t + 8 : t + 9, :]
                        y = jnp.where(last_row(u), row, pltpu.roll(u, 7, 0))
                    cu = (1.0 - rj * (kx + ky)) * (p * u)
                    px, py = kx * (p * shift_x(u, XP[d])), ky * (p * y)
                    for k, v in enumerate((cu, px, py, al * cu, al * px, al * py)):
                        acc[k] = v if acc[k] is None else acc[k] + v
                xk, yk = (1 if XP[quad[0]] else 2), (3 if YP[quad[0]] else 4)
                for k, ref in enumerate((r_ref, t_ref)):
                    for key, v in zip((0, xk, yk), acc[3 * k : 3 * k + 3]):
                        at = (key, j, slice(t, t + 8))
                        ref[at] = ref[at] + v if (k, key) in seen else v
                        seen.add((k, key))


def total_kernel(rows, *refs):
    parts, (tot, first, second) = refs[:-3], refs[-3:]
    total = parts[0][...]
    for part in parts[1:]:
        total = total + part[...]
    tot[...] = total

    def write(up, dn):
        up[...] = jnp.zeros_like(up)
        dn[...] = jnp.zeros_like(dn)
        for k, row in enumerate((rows - 1, 2 * rows - 1, 2 * rows, 2 * rows + 1)):
            up[k : k + 1, :] = total[row : row + 1]
        for k, row in enumerate((0, rows, 2 * rows + 2, 2 * rows + 3)):
            dn[k : k + 1, :] = total[row : row + 1]

    by_parity(write, first, second)


def advected_sum(rj, h, above, below, s):
    return h * s[0], rj * (
        shift_x(h * s[1], True) + shift_x(h * s[2], False) + from_before(h * s[3], above) + from_after(h * s[4], below)
    )


def first_kernel(nf, tab, tot, e_first, e_second, s_first, s_second, mask, white, sum_ref, sy_ref, t0_ref, t0h_ref, h0_ref, h0h_ref, t1_ref):
    rows, nc = mask.shape
    lo, hi = beside(e_first, e_second)
    lo_misc, hi_misc = beside(s_first, s_second)
    ocean = mask[...].astype(F32)
    row = lax.broadcasted_iota(jnp.int32, (rows, nc), 0)
    total = tot[...]
    field = []
    halo = []
    t0h_ref[...] = jnp.zeros_like(t0h_ref)
    for k in range(2):
        v = total[k * rows : (k + 1) * rows]
        v = v + jnp.where(row == 0, lo[2 + k : 3 + k, :], 0.0) + jnp.where(row == rows - 1, hi[2 + k : 3 + k, :], 0.0)
        field.append(ocean * v)
        t0_ref[k] = field[k]
        above = misc_row(lo_misc, 1, 3) * (lo[k : k + 1, :] + total[2 * rows + 2 + k : 2 * rows + 3 + k])
        below = misc_row(hi_misc, 0, 3) * (hi[k : k + 1, :] + total[2 * rows + k : 2 * rows + 1 + k])
        halo.append((above, below))
        t0h_ref[k : k + 1, :] = above
        t0h_ref[2 + k : 3 + k, :] = below
    damping = damping_of(*field)[3]
    damp_lo = damping_of(halo[0][0], halo[1][0])[3]
    damp_hi = damping_of(halo[0][1], halo[1][1])[3]
    energy, moment = jnp.zeros((rows, nc), F32), jnp.zeros((rows, nc), F32)
    for j in range(nf):
        rj, w, q, wf = [coef(tab, j, nf, k) for k in (1, 2, 3, 4)]
        h = gate(q, white[...], damping, ocean)
        h_lo = gate(q, misc_row(lo_misc, 1, 4), damp_lo, misc_row(lo_misc, 1, 3))
        h_hi = gate(q, misc_row(hi_misc, 0, 4), damp_hi, misc_row(hi_misc, 0, 3))
        h0_ref[j] = h
        h0h_ref[0, j : j + 1, :] = h_lo
        h0h_ref[1, j : j + 1, :] = h_hi
        centre, around = advected_sum(
            rj, h, h_lo * sy_ref[0, j : j + 1, :], h_hi * sy_ref[1, j : j + 1, :], [sum_ref[k, j] for k in range(5)]
        )
        adv = centre + around
        energy, moment = energy + w * adv, moment + wf * adv
    t1_ref[0:rows, :] = energy
    t1_ref[rows : 2 * rows, :] = moment


def gathered(rj, h, h_lo, h_hi, r):
    return h * r[0] + rj * (
        shift_x(h, True) * r[1] + shift_x(h, False) * r[2] + from_before(h, h_lo) * r[3] + from_after(h, h_hi) * r[4]
    )


def second_kernel(nf, n, tab, *refs):
    parts, (mask, white, h0_ref, h0h_ref, r_ref, t1_ref, h1_ref, d1_ref) = refs[:n], refs[n:]
    rows, nc = mask.shape
    ocean = mask[...].astype(F32)
    total = parts[0][...]
    for part in parts[1:]:
        total = total + part[...]
    energy, moment = ocean * total[:rows], ocean * total[rows:]
    t1_ref[0] = energy
    t1_ref[1] = moment
    damping = damping_of(energy, moment)[3]
    acc = jnp.zeros((rows, nc), F32)
    for j in range(nf):
        rj, q = coef(tab, j, nf, 1), coef(tab, j, nf, 3)
        h1 = gate(q, white[...], damping, ocean)
        h1_ref[j] = h1
        part = gathered(rj, h0_ref[j], h0h_ref[0, j : j + 1, :], h0h_ref[1, j : j + 1, :], [r_ref[k, j] for k in range(5)])
        acc = acc + q * (h1 * part)
    d1_ref[...] = acc


def third_kernel(nf, n, tab, *refs):
    parts = refs[:n]
    mask, white, speed, t1, h0_ref, h0h_ref, h1_ref, sum_ref, sy_ref, r_ref, t_ref = refs[n : n + 11]
    d1_ref, v1_ref, d0_ref, f1_ref, first, second = refs[n + 11 :]
    rows, nc = mask.shape
    ocean = mask[...].astype(F32)
    damp = parts[0][...]
    for part in parts[1:]:
        damp = damp + part[...]
    d1_ref[...] = damp
    grad_e, grad_m, _ = grads_of(t1[0], t1[1], white[...], damp)
    acc, force = jnp.zeros((rows, nc), F32), jnp.zeros((rows, nc), F32)
    push_lo, push_hi = jnp.zeros((1, nc), F32), jnp.zeros((1, nc), F32)
    for j in range(nf):
        fr, rj, w, q = [coef(tab, j, nf, k) for k in range(4)]
        h0, h1 = h0_ref[j], h1_ref[j]
        h_lo, h_hi = h0h_ref[0, j : j + 1, :], h0h_ref[1, j : j + 1, :]
        v1 = ocean * (w * (grad_e + fr * grad_m))
        v1_ref[j] = v1
        s, r = [sum_ref[k, j] for k in range(5)], [r_ref[k, j] for k in range(5)]
        inner = (
            shift_x(h1 * r[1], False)
            + shift_x(h1 * r[2], True)
            + from_after(h1 * r[3], 0.0)
            + from_before(h1 * r[4], 0.0)
            + s[1] * shift_x(v1, False)
            + s[2] * shift_x(v1, True)
            + s[3] * from_after(v1, 0.0)
            + s[4] * from_before(v1, 0.0)
        )
        acc = acc + q * (h0 * (h1 * r[0] + v1 * s[0] + rj * inner))
        push_lo = push_lo + (q * rj) * (h_lo * (h1[0:1] * r[3][0:1] + v1[0:1] * sy_ref[0, j : j + 1, :]))
        e = rows - 1
        push_hi = push_hi + (q * rj) * (
            h_hi * (h1[e : e + 1] * r[4][e : e + 1] + v1[e : e + 1] * sy_ref[1, j : j + 1, :])
        )
        part = gathered(rj, h0, h_lo, h_hi, [t_ref[k, j] for k in range(5)])
        force = force + fr * (h1 * part)
    def write(up, dn):
        for k, v in enumerate((t1[0], t1[1], damp)):
            up[2 * k : 2 * k + 2, :] = v[rows - 2 : rows]
            dn[2 * k : 2 * k + 2, :] = v[0:2]
        up[6:7, :] = acc[rows - 1 : rows]
        up[7:8, :] = push_hi
        dn[6:7, :] = acc[0:1]
        dn[7:8, :] = push_lo

    by_parity(write, first, second)
    d0_ref[0:rows, :] = acc
    d0_ref[rows:, :] = jnp.zeros_like(d0_ref[rows:, :])
    d0_ref[rows : rows + 1, :] = push_lo
    d0_ref[rows + 1 : rows + 2, :] = push_hi
    f1_ref[...] = (speed[...] / HIGHEST) * force


def fourth_kernel(nf, tab, part, b_first, b_second, s_first, s_second, a_low, a_high, t_ref, h0_ref, h1_ref, v1_ref, f1_ref, speed, out):
    rows, nc = speed.shape
    lo, hi = beside(b_first, b_second)
    lo_misc, hi_misc = beside(s_first, s_second)
    row = lax.broadcasted_iota(jnp.int32, (rows, nc), 0)
    v = part[0:rows, :]
    v = v + jnp.where(row == 0, lo[7:8, :], 0.0) + jnp.where(row == rows - 1, hi[7:8, :], 0.0)
    out[0:rows, :] = v
    out[rows : rows + 8, :] = jnp.zeros((8, nc), F32)
    out[rows : rows + 1, :] = part[rows : rows + 1, :] + lo[6:7, :]
    out[rows + 1 : rows + 2, :] = part[rows + 1 : rows + 2, :] + hi[6:7, :]
    outside = []
    for got, misc, r in ((lo, lo_misc, 1), (hi, hi_misc, 0)):
        energy, moment, damp = [got[2 * k + r : 2 * k + r + 1, :] for k in range(3)]
        white = misc_row(misc, r, 4)
        grad_e, grad_m, damping = grads_of(energy, moment, white, damp)
        outside.append((white, damping, misc_row(misc, r, 3), grad_e, grad_m))
    force = jnp.zeros((rows, nc), F32)
    low = a_low.shape[1]
    for j in range(nf):
        fr, w, q = [coef(tab, j, nf, k) for k in (0, 2, 3)]
        a = [a_low[k, j] if j < low else a_high[k, j - low] for k in range(9)]
        h1, v1 = h1_ref[j], v1_ref[j]
        edges = [(gate(q, white, damping, o), o * (w * (ge + fr * gm))) for white, damping, o, ge, gm in outside]
        force = force + (fr * h0_ref[j]) * (h1 * t_ref[0, j]) + v1 * a[0]
        for x, k, b in ((v1, 0, 1), (h1, 4, 0)):
            force = force + (
                shift_x(x, False) * a[k + 1]
                + shift_x(x, True) * a[k + 2]
                + from_after(x, edges[1][b]) * a[k + 3]
                + from_before(x, edges[0][b]) * a[k + 4]
            )
    out[rows + 8 :, :] = (speed[...] / HIGHEST) * force + f1_ref[...]


def force_kernel(first, tab, u_ref, p_ref, al_ref, h0_ref, p_first, p_second, a_ref):
    nf, _, rows, nc = u_ref.shape
    pl_ref, ph_ref = beside(p_first, p_second)

    @pl.loop(0, a_ref.shape[1])
    def _(i):
        j = first + i
        fr, rj = coef(tab, j, nf, 0), coef(tab, j, nf, 1)
        for t in range(0, rows, 8):
            seen = set()
            for quad in QUADS:
                acc = [None] * 5
                for d in quad:
                    kx, ky = float(KX[d]), float(KY[d])
                    u, p, al = u_ref[j, d, t : t + 8, :], p_ref[j, d, t : t + 8, :], al_ref[d, t : t + 8, :]
                    if YP[d]:
                        row = ph_ref[j, d : d + 1, :] if t + 8 == rows else p_ref[j, d, t + 8 : t + 9, :]
                        y = from_after(p, row)
                    else:
                        row = pl_ref[j, d : d + 1, :] if t == 0 else p_ref[j, d, t - 1 : t, :]
                        y = from_before(p, row)
                    au = al * u
                    xau, yau = kx * au, ky * au
                    for k, v in enumerate(((1.0 - rj * (kx + ky)) * au, xau, yau, xau * shift_x(p, not XP[d]), yau * y)):
                        acc[k] = v if acc[k] is None else acc[k] + v
                xk, yk = (1 if XP[quad[0]] else 2), (3 if YP[quad[0]] else 4)
                for key, v in zip((0, xk, yk, 4 + xk, 4 + yk), acc):
                    at = (key, i, slice(t, t + 8))
                    a_ref[at] = a_ref[at] + v if key in seen else v
                    seen.add(key)
        h0 = h0_ref[j]
        for k in range(9):
            a_ref[k, i] = (fr * h0 if k == 0 else h0) * a_ref[k, i]


def back_kernel(tab, dirs, p_ref, coef_in, al_ref, h0_ref, h0h_ref, h1_ref, v1_ref, p_first, p_second, s_first, s_second, b_first, b_second, speed, z_ref, zl_ref, zh_ref, edge, halo, scaled, work):
    nf, _, rows, nc = p_ref.shape
    pl_ref, ph_ref = beside(p_first, p_second)
    lo_misc, hi_misc = beside(s_first, s_second)
    lo, hi = beside(b_first, b_second)
    sides = ((0, ph_ref, hi_misc, hi, 0, 1, 1, zh_ref), (1, pl_ref, lo_misc, lo, 1, 0, 0, zl_ref))
    for side, (_, _, misc, got, *_) in enumerate(sides):
        for r in range(2):
            energy, moment, damp = [got[2 * k + r : 2 * k + r + 1, :] for k in range(3)]
            white = misc_row(misc, r, 4)
            grad_e, grad_m, damping = grads_of(energy, moment, white, damp)
            for k, v in enumerate((grad_e, grad_m, white * damping)):
                halo[side, r, k : k + 1, :] = v

    @pl.loop(0, nf)
    def _(j):
        fr, rj = coef(tab, j, nf, 0), coef(tab, j, nf, 1)
        w, q = coef(tab, j, nf, 2), coef(tab, j, nf, 3)
        for side, (half, blk, misc, _, near, far, which, out) in enumerate(sides):
            x = []
            for r in range(2):
                ocean = misc_row(misc, r, 3)
                h = gate(q, halo[side, r, 2:3, :], 1.0, ocean)
                v = ocean * (w * (halo[side, r, 0:1, :] + fr * halo[side, r, 1:2, :]))
                x.append(halo_rows(blk, j, r) * h + v)
            edge[side] = x[near]
            moved = halo_adv(rj, dirs, half, x[near], x[far], True) * halo_growth(fr, dirs, half, misc, near)
            out[j] = moved * h0h_ref[which, pl.ds(j, 1), :]
        tiles = range(rows // 8)
        at8 = [slice(8 * t, 8 * t + 8) for t in tiles]
        work[...] = (fr * (time_step * LOG2E / HIGHEST)) * (coef_in[...] * speed[...])
        for t in tiles:
            scaled[at8[t]] = rj * h0_ref[j, at8[t]]
        for d in range(ND):
            kx, ky = float(KX[d]), float(KY[d])
            x = [p_ref[j, d, at8[t]] * h1_ref[j, at8[t]] + v1_ref[j, at8[t]] for t in tiles]
            row = edge[0, d : d + 1, :] if YP[d] else edge[1, d - NL : d - NL + 1, :]
            y = rows_from(x, not YP[d], row)
            for t in tiles:
                back = (fr - (kx + ky)) * x[t] + kx * shift_x(x[t], not XP[d]) + ky * y[t]
                z_ref[j, d, at8[t]] = back * (jnp.exp2(work[at8[t]] * al_ref[d, at8[t]]) * scaled[at8[t]])


def out_kernel(n, tab, *refs):
    parts, refs = refs[:n], refs[n:]
    z_ref, zl_ref, zh_ref, t0, t0h, t1, d1, mask, white, s_first, s_second = refs[:11]
    lo_misc, hi_misc = beside(s_first, s_second)
    out_hbm, gi_ref, gw_ref, own, halo, edge, work, buf, sems = refs[11:]
    nf, _, rows, nc = z_ref.shape
    ocean = mask[...].astype(F32)
    total = parts[0][...]
    for part in parts[1:]:
        total = total + part[...]
    damp = total[0:rows]
    gi_ref[...] = time_step * total[rows + 8 :]
    grad_e, grad_m, damping = grads_of(t0[0], t0[1], white[...], damp)
    own[0] = grad_e
    own[1] = grad_m
    gw_ref[...] = -time_step * (damping * damp + damping_of(t1[0], t1[1])[3] * d1[...])
    above, below = total[rows : rows + 1], total[rows + 1 : rows + 2]
    sides = ((hi_misc, 0, 2, below, zh_ref), (lo_misc, 1, 0, above, zl_ref))
    for side, (misc, r, k, damp, _) in enumerate(sides):
        e, m, _ = grads_of(t0h[k : k + 1, :], t0h[k + 1 : k + 2, :], misc_row(misc, r, 4), damp)
        halo[side, 0:1, :] = e
        halo[side, 1:2, :] = m

    def put(j):
        return pltpu.make_async_copy(buf.at[j % NBUF], out_hbm.at[j], sems.at[j % NBUF])

    @pl.loop(0, nf)
    def _(j):
        slot = j % NBUF
        fr, rj, w = [coef(tab, j, nf, k) for k in range(3)]
        for side, (misc, r, _, _, z) in enumerate(sides):
            edge[side] = z[j] + misc_row(misc, r, 3) * (w * (halo[side, 0:1, :] + fr * halo[side, 1:2, :]))
        tiles = range(rows // 8)
        o = [ocean[8 * t : 8 * t + 8] for t in tiles]
        v = [o[t] * (w * (own[0, 8 * t : 8 * t + 8] + fr * own[1, 8 * t : 8 * t + 8])) for t in tiles]
        for t in tiles:
            work[0, 8 * t : 8 * t + 8] = v[t]
            work[1, 8 * t : 8 * t + 8] = rj * o[t]

        @pl.when(j >= NBUF)
        def _():
            put(j - NBUF).wait()

        for d in range(ND):
            kx, ky = float(KX[d]), float(KY[d])
            x = [z + work[0, 8 * t : 8 * t + 8] for t, z in enumerate(slab(z_ref, j, d))]
            row = edge[0, d : d + 1, :] if YP[d] else edge[1, d - NL : d - NL + 1, :]
            y = rows_from(x, not YP[d], row)
            for t in tiles:
                back = (fr - (kx + ky)) * x[t] + kx * shift_x(x[t], not XP[d]) + ky * y[t]
                buf[slot, d, 8 * t : 8 * t + 8, :] = work[1, 8 * t : 8 * t + 8] * back
        put(j).start()

    for j in range(max(0, nf - NBUF), nf):
        put(j).wait()


VMEM = pl.BlockSpec(memory_space=pltpu.VMEM)
SMEM = pl.BlockSpec(memory_space=pltpu.SMEM)
HBM = pl.BlockSpec(memory_space=pltpu.HBM)


def f32(*shape):
    return jax.ShapeDtypeStruct(shape, F32)


def vmem(*shape):
    return pltpu.VMEM(shape, F32)


def call(kernel, name, outs, args, scratch=(), hbm=(), held=(), out_hbm=(), limit=6, alias=None):
    put = {**dict.fromkeys(hbm, pltpu.HBM), **dict.fromkeys(held, pltpu.VMEM)}
    args = [pltpu.with_memory_space_constraint(a, put[k]) if k in put else a for k, a in enumerate(args)]
    return pl.pallas_call(
        kernel,
        name=name,
        out_shape=outs,
        in_specs=[HBM if k in hbm else SMEM if a.ndim == 1 else VMEM for k, a in enumerate(args)],
        out_specs=[HBM if k in out_hbm else VMEM for k in range(len(outs))],
        scratch_shapes=list(scratch),
        input_output_aliases=alias or {},
        compiler_params=pltpu.CompilerParams(vmem_limit_bytes=limit * MIB),
        cost_estimate=pl.CostEstimate(flops=1, bytes_accessed=1, transcendentals=0),
    )(*args)


def peers(x):
    n = lax.axis_size("spec")
    if n & (n - 1) == 0:
        return [lax.ppermute(x, "spec", [(i, i ^ k) for i in range(n)]) for k in range(1, n)]
    return [lax.ppermute(x, "spec", [(i, (i + k) % n) for i in range(n)]) for k in range(1, n)]


def exchange(first, second):
    n = lax.axis_size("cells")
    swaps = [[(i, i + 1) for i in range(odd, n - 1, 2)] for odd in range(2)]
    return [lax.ppermute(x, "cells", pairs + [(b, a) for a, b in pairs]) for x, pairs in zip((first, second), swaps)]


def after(first, *later):
    return lax.optimization_barrier((first, *later))[1:]


def shards(spectrum_start, input_coef, white_coef, wind_speed, wind_angle, sea_mask, cotangent):
    nf, _, rows, nc = spectrum_start.shape
    n = lax.axis_size("spec")
    tab, dirs = jnp.asarray(TABLE), jnp.asarray(DIRS)
    big = vmem(nf, ND, rows, nc)
    band = f32(nf, MISC + MROWS, nc)
    line, duo, hs, sums = f32(nf, NL, nc), f32(2, nf, nc), f32(nf, rows, nc), f32(5, nf, rows, nc)
    flat, two, push = f32(rows, nc), f32(2, rows, nc), f32(8, nc)
    stream = [vmem(NBUF, ND, rows, nc), pltpu.SemaphoreType.DMA((NBUF,))]
    heavy = dict(limit=8)

    s_up, s_dn = call(
        edge_kernel, "edge", [band, band], [spectrum_start, sea_mask, input_coef, white_coef, wind_speed, wind_angle],
        [
            vmem(nf, NL, 8, nc), vmem(nf, NL, 8, nc), pltpu.SemaphoreType.DMA((2, nf)), vmem(4, rows, nc),
            pltpu.VMEM((rows, nc), jnp.int32), pltpu.SemaphoreType.DMA((5,)),
        ],
        hbm=range(6), **heavy,
    )
    s_lo, s_hi = exchange(s_up, s_dn)
    (mask,) = after(s_up, sea_mask)
    start, t0_part = call(
        start_kernel, "start", [big, f32(2 * rows + 8, nc)], [spectrum_start, tab, mask],
        [pltpu.SemaphoreType.DMA((nf,)), pltpu.SMEM(tab.shape, F32), pltpu.SemaphoreType.DMA(()), vmem(2, 5, rows, nc)],
        hbm=range(2), **heavy,
    )
    t0_parts = peers(t0_part)
    (speed,) = after(t0_part, wind_speed)
    p, al, p_up, p_dn = call(
        wind_kernel, "wind", [big, vmem(ND, rows, nc), band, band], [tab, cotangent, input_coef, speed, wind_angle],
        [pltpu.SemaphoreType.DMA((nf,)), vmem(ND, rows, nc)], hbm=(1,), **heavy,
    )
    (t0_own,) = after(p_up, t0_part)
    tot0, e_up, e_dn = call(functools.partial(total_kernel, rows), "total", [f32(2 * rows + 8, nc), push, push], [t0_own, *t0_parts])
    e_lo, e_hi = exchange(e_up, e_dn)
    (mask,) = after(tot0, sea_mask)
    u, s5, u_lo, u_hi, sy = call(
        grown_kernel, "grown", [big, sums, line, line, duo], [tab, dirs, start, mask, input_coef, wind_speed, al, s_lo, s_hi],
        [vmem(2, NL, nc), vmem(rows, nc)], held=(2, 6), **heavy,
    )
    t0, t0h, h0, h0h, t1_part = call(
        functools.partial(first_kernel, nf), "first", [two, push, hs, duo, f32(2 * rows, nc)],
        [tab, tot0, e_lo, e_hi, s_lo, s_hi, sea_mask, white_coef, s5, sy],
    )
    t1_parts = peers(t1_part)
    p_up, p_dn = after(t1_part, p_up, p_dn)
    p_lo, p_hi = exchange(p_up, p_dn)
    r5, t5 = call(product_kernel, "product", [sums, sums], [tab, u, p, al, u_lo, u_hi], held=(1, 2, 3), **heavy)
    (t1_own,) = after(r5, t1_part)
    t1, h1, d1_part = call(
        functools.partial(second_kernel, nf, n), "second", [two, hs, flat],
        [tab, t1_own, *t1_parts, sea_mask, white_coef, h0, h0h, r5],
    )
    d1_parts = peers(d1_part)
    half = max(1, nf // 2)
    forces = lambda first, count, h0: call(
        functools.partial(force_kernel, first), "force", [f32(9, count, rows, nc)], [tab, u, p, al, h0, p_lo, p_hi], held=(1, 2, 3), **heavy
    )[0]
    (h0_late,) = after(d1_part, h0)
    a_low = forces(0, half, h0_late)
    a_low, d1_own = lax.optimization_barrier((a_low, d1_part))
    d1_parts = [d1_own] + d1_parts
    d1, v1, d0_part, f1, b_up, b_dn = call(
        functools.partial(third_kernel, nf, n), "third", [flat, hs, f32(rows + 8, nc), flat, push, push],
        [tab, *d1_parts, sea_mask, white_coef, wind_speed, t1, h0, h0h, h1, s5, sy, r5, t5],
    )
    b_lo, b_hi = exchange(b_up, b_dn)
    (h0_late,) = after(b_up, h0)
    a_high = forces(half, nf - half, h0_late)
    (red,) = call(
        functools.partial(fourth_kernel, nf), "fourth", [f32(2 * rows + 8, nc)],
        [tab, d0_part, b_lo, b_hi, s_lo, s_hi, a_low, a_high, t5, h0, h1, v1, f1, wind_speed],
    )
    reds = peers(red)
    (late_speed,) = after(red, wind_speed)
    z, z_lo, z_hi = call(
        back_kernel, "back", [big, line, line],
        [tab, dirs, p, input_coef, al, h0, h0h, h1, v1, p_lo, p_hi, s_lo, s_hi, b_lo, b_hi, late_speed],
        [vmem(2, NL, nc), vmem(2, 2, 8, nc), vmem(rows, nc), vmem(rows, nc)], held=(2, 4), **heavy,
    )
    (red_own,) = after(z_lo, red)
    reds = [red_own] + reds
    out, grad_input, grad_white = call(
        functools.partial(out_kernel, n), "out", [f32(nf, ND, rows, nc), flat, flat],
        [tab, *reds, z, z_lo, z_hi, t0, t0h, t1, d1, sea_mask, white_coef, s_lo, s_hi],
        [vmem(2, rows, nc), vmem(2, 8, nc), vmem(2, NL, nc), vmem(2, rows, nc)] + stream, held=(1 + n,), out_hbm=(0,), **heavy,
    )
    return out, grad_input, grad_white


def solution(mesh):
    return jax.shard_map(
        shards,
        mesh=mesh,
        in_specs=(
            P("spec", None, "cells", None),
            P("cells", None),
            P("cells", None),
            P("cells", None),
            P("cells", None),
            P("cells", None),
            P("spec", None, "cells", None),
        ),
        out_specs=(P("spec", None, "cells", None), P("cells", None), P("cells", None)),
        check_vma=False,
    )
```

```python
import functools
import math

import jax
import jax.numpy as jnp
import numpy as np
from jax import lax
from jax.experimental import pallas as pl
from jax.experimental.pallas import tpu as pltpu
from jax.sharding import PartitionSpec as P

NF = 32
ND = 36
STEPS = 2

epsilon = 1e-06
energy_ref = 0.5
time_step = 0.5
courant = 0.7
ratio_step = 1.1

F32 = jnp.float32
LOG2E = math.log2(math.e)

_every = np.exp(np.arange(NF, dtype=np.float32) * np.float32(math.log(ratio_step))).astype(np.float32)
_total = _every.sum(dtype=np.float32)
HIGHEST = float(_every[-1])
MEAN_RATIO = float((_every * _every).sum(dtype=np.float32) / _total)
_weights = _every / (np.float32(ND) * _total)
_q = (_every / _every[-1]) ** 2
NTAB = 5
TABLE = np.stack([_every, 1 / _every, _weights, _q, _weights * _every], axis=1).astype(np.float32).reshape(-1)

_angle = (np.float32(2.0 * math.pi) * np.arange(ND, dtype=np.float32) / np.float32(ND)).astype(np.float32)
COS, SIN = np.cos(_angle).astype(np.float32), np.sin(_angle).astype(np.float32)
KX, KY = np.float32(courant) * np.abs(COS), np.float32(courant) * np.abs(SIN)
XP, YP = [bool(c >= 0) for c in COS], [bool(s >= 0) for s in SIN]
NL = sum(YP)
NH = ND - NL
assert YP == [True] * NL + [False] * NH and NL == NH
QUADS = [[d for d in range(ND) if (XP[d], YP[d]) == quad] for quad in ((1, 1), (0, 1), (0, 0), (1, 0))]
DIRS = np.stack([v[a:b] for a, b in ((0, NL), (NL, ND)) for v in (KX, KY, COS, SIN)]).astype(np.float32)
DIRS = np.ascontiguousarray(np.broadcast_to(DIRS[:, :, None], DIRS.shape + (128,)))
MISC = 2 * NL
MROWS = 4
NMISC = 5

MIB = 1 << 20


def coef(tab, j, nf, which):
    return tab[(lax.axis_index("spec") * nf + j) * NTAB + which]


def shift_x(x, plus):
    return pltpu.roll(x, 1 if plus else x.shape[1] - 1, 1)


def first_row(x):
    return lax.broadcasted_iota(jnp.int32, x.shape, 0) == 0


def last_row(x):
    return lax.broadcasted_iota(jnp.int32, x.shape, 0) == x.shape[0] - 1


def from_before(x, above):
    return jnp.where(first_row(x), above, pltpu.roll(x, 1, 0))


def from_after(x, below):
    return jnp.where(last_row(x), below, pltpu.roll(x, x.shape[0] - 1, 0))


def shift_y(x, plus, outside):
    return from_before(x, outside) if plus else from_after(x, outside)


def damping_of(energy, moment):
    shifted = energy + epsilon
    ratio = moment / (shifted * MEAN_RATIO)
    r2 = ratio * ratio
    steep = energy * (r2 * r2) / energy_ref
    return shifted, ratio, steep, steep * steep * ratio


def grads_of(energy, moment, white, damp_total):
    shifted, ratio, steep, damping = damping_of(energy, moment)
    grad_damp = -time_step * white * damp_total
    grad_ratio = 9.0 * grad_damp * steep * steep
    r2 = ratio * ratio
    grad_energy = grad_damp * 2.0 * steep * (r2 * r2) * ratio / energy_ref - grad_ratio * ratio / shifted
    grad_moment = grad_ratio / (shifted * MEAN_RATIO)
    return grad_energy, grad_moment, damping


def gate(q, white, damping, ocean):
    return ocean * jnp.exp2((-time_step * LOG2E) * q * (white * damping))


def rows_from(tiles, plus, outside):
    moved = [pltpu.roll(x, 1 if plus else 7, 0) for x in tiles]
    mark = first_row(tiles[0]) if plus else last_row(tiles[0])
    feed = [outside] + moved[:-1] if plus else moved[1:] + [outside]
    return [jnp.where(mark, a, b) for a, b in zip(feed, moved)]


def slab(ref, *index):
    return [ref[(*index, slice(t, t + 8))] for t in range(0, ref.shape[-2], 8)]


def by_parity(write, first, second):
    odd = lax.rem(lax.axis_index("cells"), 2)

    @pl.when(odd == 0)
    def _():
        write(first, second)

    @pl.when(odd == 1)
    def _():
        write(second, first)


class Either:
    def __init__(self, even, odd):
        self.even, self.odd, self.shape = even, odd, even.shape

    def __getitem__(self, at):
        x, y = self.even[at], self.odd[at]
        return jnp.where(jnp.full(x.shape, lax.rem(lax.axis_index("cells"), 2), jnp.int32) == 0, x, y)


def beside(first, second):
    return Either(second, first), Either(first, second)


def misc_at(r, k):
    m = r * NMISC + k
    return m // MROWS, MISC + m % MROWS


def misc_row(ref, r, k):
    j, row = misc_at(r, k)
    return ref[j, row : row + 1, :]


def halo_rows(ref, j, r):
    return ref[j, r * NL : (r + 1) * NL, :]


def fetches(hbm, ref, sems):
    return lambda j: pltpu.make_async_copy(hbm.at[j], ref.at[j], sems.at[j])


NBUF = 3


def edge_kernel(s_hbm, mask_h, coef_h, white_h, speed_h, angle_h, a_ref, b_ref, low, high, sems, fields, ints, small_sems):
    nf, _, rows, nc = s_hbm.shape

    def fetch(j):
        return (
            pltpu.make_async_copy(s_hbm.at[j, 0:NL, rows - 8 : rows, :], low.at[j], sems.at[0, j]),
            pltpu.make_async_copy(s_hbm.at[j, NL:ND, 0:8, :], high.at[j], sems.at[1, j]),
        )

    smalls = [pltpu.make_async_copy(mask_h, ints, small_sems.at[0])]
    for k, f in enumerate((coef_h, white_h, speed_h, angle_h)):
        smalls.append(pltpu.make_async_copy(f, fields.at[k], small_sems.at[1 + k]))
    for c in smalls:
        c.start()
    for j in range(nf):
        for c in fetch(j):
            c.start()
    for c in smalls:
        c.wait()

    def write(up_ref, dn_ref):
        @pl.loop(0, nf)
        def _(j):
            up_ref[j, MISC:, :] = jnp.zeros_like(up_ref[j, MISC:, :])
            dn_ref[j, MISC:, :] = jnp.zeros_like(dn_ref[j, MISC:, :])

        for side, out in ((slice(rows - 2, rows), up_ref), (slice(0, 2), dn_ref)):
            kappa = (time_step * LOG2E / HIGHEST) * (fields[0, side] * fields[2, side])
            angle = fields[3, side]
            for k, v in enumerate((kappa, jnp.cos(angle), jnp.sin(angle), ints[side].astype(F32), fields[1, side])):
                for r in range(2):
                    a, b = misc_at(r, k)
                    out[a, b : b + 1, :] = v[r : r + 1]

        @pl.loop(0, nf)
        def _(j):
            for c in fetch(j):
                c.wait()
            for r in range(2):
                for d in range(NL):
                    up_ref[j, r * NL + d : r * NL + d + 1, :] = low[j, d, 6 + r : 7 + r, :]
                    dn_ref[j, r * NL + d : r * NL + d + 1, :] = high[j, d, r : r + 1, :]

    by_parity(write, a_ref, b_ref)


def start_kernel(tab, s_ref, mask, t0_ref, sums):
    nf = s_ref.shape[0]
    rows, nc = mask.shape
    sums[...] = jnp.zeros_like(sums)

    @pl.loop(0, nf)
    def _(j):
        rj, w, wf = [coef(tab, j, nf, k) for k in (1, 2, 4)]
        for t in range(0, rows, 8):
            acc = [None] * 5

            def add(k, v):
                acc[k] = v if acc[k] is None else acc[k] + v

            for d in range(ND):
                x = s_ref[j, d, t : t + 8, :]
                add(0, x)
                add(1 if XP[d] else 2, float(KX[d]) * x)
                add(3 if YP[d] else 4, float(KY[d]) * x)
            for k in range(5):
                sums[0, k, t : t + 8, :] += (w if k == 0 else w * rj) * acc[k]
                sums[1, k, t : t + 8, :] += (wf if k == 0 else wf * rj) * acc[k]

    ocean = mask[...].astype(F32)
    t0_ref[2 * rows :, :] = jnp.zeros_like(t0_ref[2 * rows :, :])
    for e in range(2):
        total, xp, xm, yp, ym = [ocean * sums[e, k] for k in range(5)]
        t0_ref[e * rows : (e + 1) * rows, :] = total + (
            shift_x(xp, True) + shift_x(xm, False) + from_before(yp, 0.0) + from_after(ym, 0.0) - (xp + xm + yp + ym)
        )
        t0_ref[2 * rows + e : 2 * rows + e + 1, :] = yp[rows - 1 : rows]
        t0_ref[2 * rows + 2 + e : 2 * rows + 3 + e, :] = ym[0:1]


def wind_kernel(tab, lam_ref, coef_in, speed, angle, p_ref, al_ref, a_ref, b_ref, expo):
    nf = lam_ref.shape[0]
    rows, nc = angle.shape
    for ref in (a_ref, b_ref):
        ref[:, MISC:, :] = jnp.zeros_like(ref[:, MISC:, :])
    kappa = (time_step * LOG2E / HIGHEST) * (coef_in[...] * speed[...])
    ca, sa = jnp.cos(angle[...]), jnp.sin(angle[...])
    for d in range(ND):
        align = jnp.maximum(float(COS[d]) * ca + float(SIN[d]) * sa, 0.0)
        al = align * align
        al_ref[d] = al
        expo[d] = kappa * al

    def write(up_ref, dn_ref):
        @pl.loop(0, nf)
        def _(j):
            fr = coef(tab, j, nf, 0)
            for d in range(ND):
                p = jnp.exp2(fr * expo[d]) * lam_ref[j, d]
                p_ref[j, d] = p
                for r in range(2):
                    at = slice(r * NL + d % NL, r * NL + d % NL + 1)
                    if d < NL:
                        dn_ref[j, at, :] = p[r : r + 1]
                    else:
                        up_ref[j, at, :] = p[rows - 2 + r : rows - 1 + r]

    by_parity(write, a_ref, b_ref)


def halo_growth(fr, dirs, half, misc, r):
    cosd, sind = dirs[4 * half + 2][:, 0:1], dirs[4 * half + 3][:, 0:1]
    align = jnp.maximum(cosd * misc_row(misc, r, 1) + sind * misc_row(misc, r, 2), 0.0)
    return jnp.exp2(fr * (misc_row(misc, r, 0) * (align * align)))


def halo_adv(rj, dirs, half, near, far, transpose):
    kx, ky, cosd = [dirs[4 * half + k][:, 0:1] for k in range(3)]
    before, after = shift_x(near, not transpose), shift_x(near, transpose)
    moved = jnp.where(cosd >= 0, before, after)
    return near + rj * (kx * (moved - near) + ky * (far - near))


def grown_kernel(tab, dirs, s_ref, mask, coef_in, speed, al_ref, s_first, s_second, u_ref, sum_ref, ul_ref, uh_ref, sy_ref, edge, work):
    nf, _, rows, nc = s_ref.shape
    lo, hi = beside(s_first, s_second)
    ocean = mask[...].astype(F32)

    @pl.loop(0, nf)
    def _(j):
        fr, rj = coef(tab, j, nf, 0), coef(tab, j, nf, 1)
        for half, (blk, near, far, out) in enumerate(((lo, 1, 0, ul_ref), (hi, 0, 1, uh_ref))):
            x = [misc_row(blk, r, 3) * halo_rows(blk, j, r) for r in range(2)]
            edge[half] = rj * x[near]
            u = halo_growth(fr, dirs, half, blk, near) * halo_adv(rj, dirs, half, x[near], x[far], False)
            out[j] = u
            sy_ref[half, pl.ds(j, 1), :] = jnp.sum(dirs[4 * half + 1][:, 0:1] * u, axis=0, keepdims=True)
        tiles = range(rows // 8)
        work[...] = (fr * (time_step * LOG2E / HIGHEST)) * (coef_in[...] * speed[...])
        oj = [rj * ocean[8 * t : 8 * t + 8] for t in tiles]
        seen = set()
        for quad in QUADS:
            acc = [[None] * 3 for _ in tiles]
            for d in quad:
                kx, ky = float(KX[d]), float(KY[d])
                x = [o * v for o, v in zip(oj, slab(s_ref, j, d))]
                row = edge[0, d : d + 1, :] if YP[d] else edge[1, d - NL : d - NL + 1, :]
                y = rows_from(x, YP[d], row)
                for t in tiles:
                    u = jnp.exp2(work[8 * t : 8 * t + 8] * al_ref[d, 8 * t : 8 * t + 8]) * (
                        (fr - (kx + ky)) * x[t] + kx * shift_x(x[t], XP[d]) + ky * y[t]
                    )
                    u_ref[j, d, 8 * t : 8 * t + 8, :] = u
                    for k, v in enumerate((u, kx * u, ky * u)):
                        acc[t][k] = v if acc[t][k] is None else acc[t][k] + v
            for k, key in enumerate((0, 1 if XP[quad[0]] else 2, 3 if YP[quad[0]] else 4)):
                for t in tiles:
                    at = (key, j, slice(8 * t, 8 * t + 8))
                    sum_ref[at] = sum_ref[at] + acc[t][k] if key in seen else acc[t][k]
                seen.add(key)
        for t in tiles:
            a, b, c, d, e = [sum_ref[k, j, 8 * t : 8 * t + 8, :] for k in range(5)]
            sum_ref[0, j, 8 * t : 8 * t + 8, :] = a - rj * (b + c + d + e)


def product_kernel(tab, u_ref, p_ref, al_ref, ul_ref, uh_ref, r_ref, t_ref):
    nf, _, rows, nc = u_ref.shape

    @pl.loop(0, nf)
    def _(j):
        rj = coef(tab, j, nf, 1)
        for t in range(0, rows, 8):
            seen = set()
            for quad in QUADS:
                acc = [None] * 6
                for d in quad:
                    kx, ky = float(KX[d]), float(KY[d])
                    u, p, al = u_ref[j, d, t : t + 8, :], p_ref[j, d, t : t + 8, :], al_ref[d, t : t + 8, :]
                    if YP[d]:
                        row = ul_ref[j, d : d + 1, :] if t == 0 else u_ref[j, d, t - 1 : t, :]
                        y = jnp.where(first_row(u), row, pltpu.roll(u, 1, 0))
                    else:
                        row = uh_ref[j, d - NL : d - NL + 1, :] if t + 8 == rows else u_ref[j, d, t + 8 : t + 9, :]
                        y = jnp.where(last_row(u), row, pltpu.roll(u, 7, 0))
                    cu = (1.0 - rj * (kx + ky)) * (p * u)
                    px, py = kx * (p * shift_x(u, XP[d])), ky * (p * y)
                    for k, v in enumerate((cu, px, py, al * cu, al * px, al * py)):
                        acc[k] = v if acc[k] is None else acc[k] + v
                xk, yk = (1 if XP[quad[0]] else 2), (3 if YP[quad[0]] else 4)
                for k, ref in enumerate((r_ref, t_ref)):
                    for key, v in zip((0, xk, yk), acc[3 * k : 3 * k + 3]):
                        at = (key, j, slice(t, t + 8))
                        ref[at] = ref[at] + v if (k, key) in seen else v
                        seen.add((k, key))


def total_kernel(rows, *refs):
    parts, (tot, first, second) = refs[:-3], refs[-3:]
    total = parts[0][...]
    for part in parts[1:]:
        total = total + part[...]
    tot[...] = total

    def write(up, dn):
        up[...] = jnp.zeros_like(up)
        dn[...] = jnp.zeros_like(dn)
        for k, row in enumerate((rows - 1, 2 * rows - 1, 2 * rows, 2 * rows + 1)):
            up[k : k + 1, :] = total[row : row + 1]
        for k, row in enumerate((0, rows, 2 * rows + 2, 2 * rows + 3)):
            dn[k : k + 1, :] = total[row : row + 1]

    by_parity(write, first, second)


def advected_sum(rj, h, above, below, s):
    return h * s[0], rj * (
        shift_x(h * s[1], True) + shift_x(h * s[2], False) + from_before(h * s[3], above) + from_after(h * s[4], below)
    )


def first_kernel(nf, tab, tot, e_first, e_second, s_first, s_second, mask, white, sum_ref, sy_ref, t0_ref, t0h_ref, h0_ref, h0h_ref, t1_ref):
    rows, nc = mask.shape
    lo, hi = beside(e_first, e_second)
    lo_misc, hi_misc = beside(s_first, s_second)
    ocean = mask[...].astype(F32)
    row = lax.broadcasted_iota(jnp.int32, (rows, nc), 0)
    total = tot[...]
    field = []
    halo = []
    t0h_ref[...] = jnp.zeros_like(t0h_ref)
    for k in range(2):
        v = total[k * rows : (k + 1) * rows]
        v = v + jnp.where(row == 0, lo[2 + k : 3 + k, :], 0.0) + jnp.where(row == rows - 1, hi[2 + k : 3 + k, :], 0.0)
        field.append(ocean * v)
        t0_ref[k] = field[k]
        above = misc_row(lo_misc, 1, 3) * (lo[k : k + 1, :] + total[2 * rows + 2 + k : 2 * rows + 3 + k])
        below = misc_row(hi_misc, 0, 3) * (hi[k : k + 1, :] + total[2 * rows + k : 2 * rows + 1 + k])
        halo.append((above, below))
        t0h_ref[k : k + 1, :] = above
        t0h_ref[2 + k : 3 + k, :] = below
    damping = damping_of(*field)[3]
    damp_lo = damping_of(halo[0][0], halo[1][0])[3]
    damp_hi = damping_of(halo[0][1], halo[1][1])[3]
    energy, moment = jnp.zeros((rows, nc), F32), jnp.zeros((rows, nc), F32)
    for j in range(nf):
        rj, w, q, wf = [coef(tab, j, nf, k) for k in (1, 2, 3, 4)]
        h = gate(q, white[...], damping, ocean)
        h_lo = gate(q, misc_row(lo_misc, 1, 4), damp_lo, misc_row(lo_misc, 1, 3))
        h_hi = gate(q, misc_row(hi_misc, 0, 4), damp_hi, misc_row(hi_misc, 0, 3))
        h0_ref[j] = h
        h0h_ref[0, j : j + 1, :] = h_lo
        h0h_ref[1, j : j + 1, :] = h_hi
        centre, around = advected_sum(
            rj, h, h_lo * sy_ref[0, j : j + 1, :], h_hi * sy_ref[1, j : j + 1, :], [sum_ref[k, j] for k in range(5)]
        )
        adv = centre + around
        energy, moment = energy + w * adv, moment + wf * adv
    t1_ref[0:rows, :] = energy
    t1_ref[rows : 2 * rows, :] = moment


def gathered(rj, h, h_lo, h_hi, r):
    return h * r[0] + rj * (
        shift_x(h, True) * r[1] + shift_x(h, False) * r[2] + from_before(h, h_lo) * r[3] + from_after(h, h_hi) * r[4]
    )


def second_kernel(nf, n, tab, *refs):
    parts, (mask, white, h0_ref, h0h_ref, r_ref, t1_ref, h1_ref, d1_ref) = refs[:n], refs[n:]
    rows, nc = mask.shape
    ocean = mask[...].astype(F32)
    total = parts[0][...]
    for part in parts[1:]:
        total = total + part[...]
    energy, moment = ocean * total[:rows], ocean * total[rows:]
    t1_ref[0] = energy
    t1_ref[1] = moment
    damping = damping_of(energy, moment)[3]
    acc = jnp.zeros((rows, nc), F32)
    for j in range(nf):
        rj, q = coef(tab, j, nf, 1), coef(tab, j, nf, 3)
        h1 = gate(q, white[...], damping, ocean)
        h1_ref[j] = h1
        part = gathered(rj, h0_ref[j], h0h_ref[0, j : j + 1, :], h0h_ref[1, j : j + 1, :], [r_ref[k, j] for k in range(5)])
        acc = acc + q * (h1 * part)
    d1_ref[...] = acc


def third_kernel(nf, n, tab, *refs):
    parts = refs[:n]
    mask, white, speed, t1, h0_ref, h0h_ref, h1_ref, sum_ref, sy_ref, r_ref, t_ref = refs[n : n + 11]
    d1_ref, v1_ref, d0_ref, f1_ref, first, second = refs[n + 11 :]
    rows, nc = mask.shape
    ocean = mask[...].astype(F32)
    damp = parts[0][...]
    for part in parts[1:]:
        damp = damp + part[...]
    d1_ref[...] = damp
    grad_e, grad_m, _ = grads_of(t1[0], t1[1], white[...], damp)
    acc, force = jnp.zeros((rows, nc), F32), jnp.zeros((rows, nc), F32)
    push_lo, push_hi = jnp.zeros((1, nc), F32), jnp.zeros((1, nc), F32)
    for j in range(nf):
        fr, rj, w, q = [coef(tab, j, nf, k) for k in range(4)]
        h0, h1 = h0_ref[j], h1_ref[j]
        h_lo, h_hi = h0h_ref[0, j : j + 1, :], h0h_ref[1, j : j + 1, :]
        v1 = ocean * (w * (grad_e + fr * grad_m))
        v1_ref[j] = v1
        s, r = [sum_ref[k, j] for k in range(5)], [r_ref[k, j] for k in range(5)]
        inner = (
            shift_x(h1 * r[1], False)
            + shift_x(h1 * r[2], True)
            + from_after(h1 * r[3], 0.0)
            + from_before(h1 * r[4], 0.0)
            + s[1] * shift_x(v1, False)
            + s[2] * shift_x(v1, True)
            + s[3] * from_after(v1, 0.0)
            + s[4] * from_before(v1, 0.0)
        )
        acc = acc + q * (h0 * (h1 * r[0] + v1 * s[0] + rj * inner))
        push_lo = push_lo + (q * rj) * (h_lo * (h1[0:1] * r[3][0:1] + v1[0:1] * sy_ref[0, j : j + 1, :]))
        e = rows - 1
        push_hi = push_hi + (q * rj) * (
            h_hi * (h1[e : e + 1] * r[4][e : e + 1] + v1[e : e + 1] * sy_ref[1, j : j + 1, :])
        )
        part = gathered(rj, h0, h_lo, h_hi, [t_ref[k, j] for k in range(5)])
        force = force + fr * (h1 * part)
    def write(up, dn):
        for k, v in enumerate((t1[0], t1[1], damp)):
            up[2 * k : 2 * k + 2, :] = v[rows - 2 : rows]
            dn[2 * k : 2 * k + 2, :] = v[0:2]
        up[6:7, :] = acc[rows - 1 : rows]
        up[7:8, :] = push_hi
        dn[6:7, :] = acc[0:1]
        dn[7:8, :] = push_lo

    by_parity(write, first, second)
    d0_ref[0:rows, :] = acc
    d0_ref[rows:, :] = jnp.zeros_like(d0_ref[rows:, :])
    d0_ref[rows : rows + 1, :] = push_lo
    d0_ref[rows + 1 : rows + 2, :] = push_hi
    f1_ref[...] = (speed[...] / HIGHEST) * force


def fourth_kernel(nf, tab, part, b_first, b_second, s_first, s_second, a_low, a_high, t_ref, h0_ref, h1_ref, v1_ref, f1_ref, speed, out):
    rows, nc = speed.shape
    lo, hi = beside(b_first, b_second)
    lo_misc, hi_misc = beside(s_first, s_second)
    row = lax.broadcasted_iota(jnp.int32, (rows, nc), 0)
    v = part[0:rows, :]
    v = v + jnp.where(row == 0, lo[7:8, :], 0.0) + jnp.where(row == rows - 1, hi[7:8, :], 0.0)
    out[0:rows, :] = v
    out[rows : rows + 8, :] = jnp.zeros((8, nc), F32)
    out[rows : rows + 1, :] = part[rows : rows + 1, :] + lo[6:7, :]
    out[rows + 1 : rows + 2, :] = part[rows + 1 : rows + 2, :] + hi[6:7, :]
    outside = []
    for got, misc, r in ((lo, lo_misc, 1), (hi, hi_misc, 0)):
        energy, moment, damp = [got[2 * k + r : 2 * k + r + 1, :] for k in range(3)]
        white = misc_row(misc, r, 4)
        grad_e, grad_m, damping = grads_of(energy, moment, white, damp)
        outside.append((white, damping, misc_row(misc, r, 3), grad_e, grad_m))
    force = jnp.zeros((rows, nc), F32)
    low = a_low.shape[1]
    for j in range(nf):
        fr, w, q = [coef(tab, j, nf, k) for k in (0, 2, 3)]
        a = [a_low[k, j] if j < low else a_high[k, j - low] for k in range(9)]
        h1, v1 = h1_ref[j], v1_ref[j]
        edges = [(gate(q, white, damping, o), o * (w * (ge + fr * gm))) for white, damping, o, ge, gm in outside]
        force = force + (fr * h0_ref[j]) * (h1 * t_ref[0, j]) + v1 * a[0]
        for x, k, b in ((v1, 0, 1), (h1, 4, 0)):
            force = force + (
                shift_x(x, False) * a[k + 1]
                + shift_x(x, True) * a[k + 2]
                + from_after(x, edges[1][b]) * a[k + 3]
                + from_before(x, edges[0][b]) * a[k + 4]
            )
    out[rows + 8 :, :] = (speed[...] / HIGHEST) * force + f1_ref[...]


def force_kernel(first, tab, u_ref, p_ref, al_ref, h0_ref, p_first, p_second, a_ref):
    nf, _, rows, nc = u_ref.shape
    pl_ref, ph_ref = beside(p_first, p_second)

    @pl.loop(0, a_ref.shape[1])
    def _(i):
        j = first + i
        fr, rj = coef(tab, j, nf, 0), coef(tab, j, nf, 1)
        for t in range(0, rows, 8):
            seen = set()
            for quad in QUADS:
                acc = [None] * 5
                for d in quad:
                    kx, ky = float(KX[d]), float(KY[d])
                    u, p, al = u_ref[j, d, t : t + 8, :], p_ref[j, d, t : t + 8, :], al_ref[d, t : t + 8, :]
                    if YP[d]:
                        row = ph_ref[j, d : d + 1, :] if t + 8 == rows else p_ref[j, d, t + 8 : t + 9, :]
                        y = from_after(p, row)
                    else:
                        row = pl_ref[j, d : d + 1, :] if t == 0 else p_ref[j, d, t - 1 : t, :]
                        y = from_before(p, row)
                    au = al * u
                    xau, yau = kx * au, ky * au
                    for k, v in enumerate(((1.0 - rj * (kx + ky)) * au, xau, yau, xau * shift_x(p, not XP[d]), yau * y)):
                        acc[k] = v if acc[k] is None else acc[k] + v
                xk, yk = (1 if XP[quad[0]] else 2), (3 if YP[quad[0]] else 4)
                for key, v in zip((0, xk, yk, 4 + xk, 4 + yk), acc):
                    at = (key, i, slice(t, t + 8))
                    a_ref[at] = a_ref[at] + v if key in seen else v
                    seen.add(key)
        h0 = h0_ref[j]
        for k in range(9):
            a_ref[k, i] = (fr * h0 if k == 0 else h0) * a_ref[k, i]


def back_kernel(tab, dirs, p_ref, coef_in, al_ref, h0_ref, h0h_ref, h1_ref, v1_ref, p_first, p_second, s_first, s_second, b_first, b_second, speed, z_ref, zl_ref, zh_ref, edge, halo, scaled, work):
    nf, _, rows, nc = p_ref.shape
    pl_ref, ph_ref = beside(p_first, p_second)
    lo_misc, hi_misc = beside(s_first, s_second)
    lo, hi = beside(b_first, b_second)
    sides = ((0, ph_ref, hi_misc, hi, 0, 1, 1, zh_ref), (1, pl_ref, lo_misc, lo, 1, 0, 0, zl_ref))
    for side, (_, _, misc, got, *_) in enumerate(sides):
        for r in range(2):
            energy, moment, damp = [got[2 * k + r : 2 * k + r + 1, :] for k in range(3)]
            white = misc_row(misc, r, 4)
            grad_e, grad_m, damping = grads_of(energy, moment, white, damp)
            for k, v in enumerate((grad_e, grad_m, white * damping)):
                halo[side, r, k : k + 1, :] = v

    @pl.loop(0, nf)
    def _(j):
        fr, rj = coef(tab, j, nf, 0), coef(tab, j, nf, 1)
        w, q = coef(tab, j, nf, 2), coef(tab, j, nf, 3)
        for side, (half, blk, misc, _, near, far, which, out) in enumerate(sides):
            x = []
            for r in range(2):
                ocean = misc_row(misc, r, 3)
                h = gate(q, halo[side, r, 2:3, :], 1.0, ocean)
                v = ocean * (w * (halo[side, r, 0:1, :] + fr * halo[side, r, 1:2, :]))
                x.append(halo_rows(blk, j, r) * h + v)
            edge[side] = x[near]
            moved = halo_adv(rj, dirs, half, x[near], x[far], True) * halo_growth(fr, dirs, half, misc, near)
            out[j] = moved * h0h_ref[which, pl.ds(j, 1), :]
        tiles = range(rows // 8)
        at8 = [slice(8 * t, 8 * t + 8) for t in tiles]
        work[...] = (fr * (time_step * LOG2E / HIGHEST)) * (coef_in[...] * speed[...])
        for t in tiles:
            scaled[at8[t]] = rj * h0_ref[j, at8[t]]
        for d in range(ND):
            kx, ky = float(KX[d]), float(KY[d])
            x = [p_ref[j, d, at8[t]] * h1_ref[j, at8[t]] + v1_ref[j, at8[t]] for t in tiles]
            row = edge[0, d : d + 1, :] if YP[d] else edge[1, d - NL : d - NL + 1, :]
            y = rows_from(x, not YP[d], row)
            for t in tiles:
                back = (fr - (kx + ky)) * x[t] + kx * shift_x(x[t], not XP[d]) + ky * y[t]
                z_ref[j, d, at8[t]] = back * (jnp.exp2(work[at8[t]] * al_ref[d, at8[t]]) * scaled[at8[t]])


def out_kernel(n, tab, *refs):
    parts, refs = refs[:n], refs[n:]
    z_ref, zl_ref, zh_ref, t0, t0h, t1, d1, mask, white, s_first, s_second = refs[:11]
    lo_misc, hi_misc = beside(s_first, s_second)
    out_hbm, gi_ref, gw_ref, own, halo, edge, work, buf, sems = refs[11:]
    nf, _, rows, nc = z_ref.shape
    ocean = mask[...].astype(F32)
    total = parts[0][...]
    for part in parts[1:]:
        total = total + part[...]
    damp = total[0:rows]
    gi_ref[...] = time_step * total[rows + 8 :]
    grad_e, grad_m, damping = grads_of(t0[0], t0[1], white[...], damp)
    own[0] = grad_e
    own[1] = grad_m
    gw_ref[...] = -time_step * (damping * damp + damping_of(t1[0], t1[1])[3] * d1[...])
    above, below = total[rows : rows + 1], total[rows + 1 : rows + 2]
    sides = ((hi_misc, 0, 2, below, zh_ref), (lo_misc, 1, 0, above, zl_ref))
    for side, (misc, r, k, damp, _) in enumerate(sides):
        e, m, _ = grads_of(t0h[k : k + 1, :], t0h[k + 1 : k + 2, :], misc_row(misc, r, 4), damp)
        halo[side, 0:1, :] = e
        halo[side, 1:2, :] = m

    def put(j):
        return pltpu.make_async_copy(buf.at[j % NBUF], out_hbm.at[j], sems.at[j % NBUF])

    @pl.loop(0, nf)
    def _(j):
        slot = j % NBUF
        fr, rj, w = [coef(tab, j, nf, k) for k in range(3)]
        for side, (misc, r, _, _, z) in enumerate(sides):
            edge[side] = z[j] + misc_row(misc, r, 3) * (w * (halo[side, 0:1, :] + fr * halo[side, 1:2, :]))
        tiles = range(rows // 8)
        o = [ocean[8 * t : 8 * t + 8] for t in tiles]
        v = [o[t] * (w * (own[0, 8 * t : 8 * t + 8] + fr * own[1, 8 * t : 8 * t + 8])) for t in tiles]
        for t in tiles:
            work[0, 8 * t : 8 * t + 8] = v[t]
            work[1, 8 * t : 8 * t + 8] = rj * o[t]

        @pl.when(j >= NBUF)
        def _():
            put(j - NBUF).wait()

        for d in range(ND):
            kx, ky = float(KX[d]), float(KY[d])
            x = [z + work[0, 8 * t : 8 * t + 8] for t, z in enumerate(slab(z_ref, j, d))]
            row = edge[0, d : d + 1, :] if YP[d] else edge[1, d - NL : d - NL + 1, :]
            y = rows_from(x, not YP[d], row)
            for t in tiles:
                back = (fr - (kx + ky)) * x[t] + kx * shift_x(x[t], not XP[d]) + ky * y[t]
                buf[slot, d, 8 * t : 8 * t + 8, :] = work[1, 8 * t : 8 * t + 8] * back
        put(j).start()

    for j in range(max(0, nf - NBUF), nf):
        put(j).wait()


VMEM = pl.BlockSpec(memory_space=pltpu.VMEM)
SMEM = pl.BlockSpec(memory_space=pltpu.SMEM)
HBM = pl.BlockSpec(memory_space=pltpu.HBM)


def f32(*shape):
    return jax.ShapeDtypeStruct(shape, F32)


def vmem(*shape):
    return pltpu.VMEM(shape, F32)


def call(kernel, name, outs, args, scratch=(), hbm=(), held=(), out_hbm=(), limit=6, alias=None):
    put = {**dict.fromkeys(hbm, pltpu.HBM), **dict.fromkeys(held, pltpu.VMEM)}
    args = [pltpu.with_memory_space_constraint(a, put[k]) if k in put else a for k, a in enumerate(args)]
    return pl.pallas_call(
        kernel,
        name=name,
        out_shape=outs,
        in_specs=[HBM if k in hbm else SMEM if a.ndim == 1 else VMEM for k, a in enumerate(args)],
        out_specs=[HBM if k in out_hbm else VMEM for k in range(len(outs))],
        scratch_shapes=list(scratch),
        input_output_aliases=alias or {},
        compiler_params=pltpu.CompilerParams(vmem_limit_bytes=limit * MIB),
        cost_estimate=pl.CostEstimate(flops=1, bytes_accessed=1, transcendentals=0),
    )(*args)


def peers(x):
    n = lax.axis_size("spec")
    if n & (n - 1) == 0:
        return [lax.ppermute(x, "spec", [(i, i ^ k) for i in range(n)]) for k in range(1, n)]
    return [lax.ppermute(x, "spec", [(i, (i + k) % n) for i in range(n)]) for k in range(1, n)]


def exchange(first, second):
    n = lax.axis_size("cells")
    swaps = [[(i, i + 1) for i in range(odd, n - 1, 2)] for odd in range(2)]
    return [lax.ppermute(x, "cells", pairs + [(b, a) for a, b in pairs]) for x, pairs in zip((first, second), swaps)]


def after(first, *later):
    return lax.optimization_barrier((first, *later))[1:]


def shards(spectrum_start, input_coef, white_coef, wind_speed, wind_angle, sea_mask, cotangent):
    nf, _, rows, nc = spectrum_start.shape
    n = lax.axis_size("spec")
    tab, dirs = jnp.asarray(TABLE), jnp.asarray(DIRS)
    big = vmem(nf, ND, rows, nc)
    band = f32(nf, MISC + MROWS, nc)
    line, duo, hs, sums = f32(nf, NL, nc), f32(2, nf, nc), f32(nf, rows, nc), f32(5, nf, rows, nc)
    flat, two, push = f32(rows, nc), f32(2, rows, nc), f32(8, nc)
    stream = [vmem(NBUF, ND, rows, nc), pltpu.SemaphoreType.DMA((NBUF,))]
    heavy = dict(limit=8)

    s_up, s_dn = call(
        edge_kernel, "edge", [band, band], [spectrum_start, sea_mask, input_coef, white_coef, wind_speed, wind_angle],
        [
            vmem(nf, NL, 8, nc), vmem(nf, NL, 8, nc), pltpu.SemaphoreType.DMA((2, nf)), vmem(4, rows, nc),
            pltpu.VMEM((rows, nc), jnp.int32), pltpu.SemaphoreType.DMA((5,)),
        ],
        hbm=range(6), **heavy,
    )
    s_lo, s_hi = exchange(s_up, s_dn)
    (mask,) = after(s_up, sea_mask)
    (t0_part,) = call(
        start_kernel, "start", [f32(2 * rows + 8, nc)], [tab, spectrum_start, mask], [vmem(2, 5, rows, nc)], held=(1,), **heavy
    )
    t0_parts = peers(t0_part)
    (speed,) = after(t0_part, wind_speed)
    p, al, p_up, p_dn = call(
        wind_kernel, "wind", [big, vmem(ND, rows, nc), band, band], [tab, cotangent, input_coef, speed, wind_angle],
        [vmem(ND, rows, nc)], held=(1,), **heavy,
    )
    (t0_own,) = after(p_up, t0_part)
    tot0, e_up, e_dn = call(functools.partial(total_kernel, rows), "total", [f32(2 * rows + 8, nc), push, push], [t0_own, *t0_parts])
    e_lo, e_hi = exchange(e_up, e_dn)
    (mask,) = after(tot0, sea_mask)
    u, s5, u_lo, u_hi, sy = call(
        grown_kernel, "grown", [big, sums, line, line, duo], [tab, dirs, spectrum_start, mask, input_coef, wind_speed, al, s_lo, s_hi],
        [vmem(2, NL, nc), vmem(rows, nc)], held=(2, 6), **heavy,
    )
    t0, t0h, h0, h0h, t1_part = call(
        functools.partial(first_kernel, nf), "first", [two, push, hs, duo, f32(2 * rows, nc)],
        [tab, tot0, e_lo, e_hi, s_lo, s_hi, sea_mask, white_coef, s5, sy],
    )
    t1_parts = peers(t1_part)
    p_up, p_dn = after(t1_part, p_up, p_dn)
    p_lo, p_hi = exchange(p_up, p_dn)
    r5, t5 = call(product_kernel, "product", [sums, sums], [tab, u, p, al, u_lo, u_hi], held=(1, 2, 3), **heavy)
    (t1_own,) = after(r5, t1_part)
    t1, h1, d1_part = call(
        functools.partial(second_kernel, nf, n), "second", [two, hs, flat],
        [tab, t1_own, *t1_parts, sea_mask, white_coef, h0, h0h, r5],
    )
    d1_parts = peers(d1_part)
    half = max(1, nf // 2)
    forces = lambda first, count, h0: call(
        functools.partial(force_kernel, first), "force", [f32(9, count, rows, nc)], [tab, u, p, al, h0, p_lo, p_hi], held=(1, 2, 3), **heavy
    )[0]
    (h0_late,) = after(d1_part, h0)
    a_low = forces(0, half, h0_late)
    a_low, d1_own = lax.optimization_barrier((a_low, d1_part))
    d1_parts = [d1_own] + d1_parts
    d1, v1, d0_part, f1, b_up, b_dn = call(
        functools.partial(third_kernel, nf, n), "third", [flat, hs, f32(rows + 8, nc), flat, push, push],
        [tab, *d1_parts, sea_mask, white_coef, wind_speed, t1, h0, h0h, h1, s5, sy, r5, t5],
    )
    b_lo, b_hi = exchange(b_up, b_dn)
    (h0_late,) = after(b_up, h0)
    a_high = forces(half, nf - half, h0_late)
    (red,) = call(
        functools.partial(fourth_kernel, nf), "fourth", [f32(2 * rows + 8, nc)],
        [tab, d0_part, b_lo, b_hi, s_lo, s_hi, a_low, a_high, t5, h0, h1, v1, f1, wind_speed],
    )
    reds = peers(red)
    (late_speed,) = after(red, wind_speed)
    z, z_lo, z_hi = call(
        back_kernel, "back", [big, line, line],
        [tab, dirs, p, input_coef, al, h0, h0h, h1, v1, p_lo, p_hi, s_lo, s_hi, b_lo, b_hi, late_speed],
        [vmem(2, NL, nc), vmem(2, 2, 8, nc), vmem(rows, nc), vmem(rows, nc)], held=(2, 4), **heavy,
    )
    (red_own,) = after(z_lo, red)
    reds = [red_own] + reds
    out, grad_input, grad_white = call(
        functools.partial(out_kernel, n), "out", [f32(nf, ND, rows, nc), flat, flat],
        [tab, *reds, z, z_lo, z_hi, t0, t0h, t1, d1, sea_mask, white_coef, s_lo, s_hi],
        [vmem(2, rows, nc), vmem(2, 8, nc), vmem(2, NL, nc), vmem(2, rows, nc)] + stream, held=(1 + n,), out_hbm=(0,), **heavy,
    )
    return out, grad_input, grad_white


def solution(mesh):
    return jax.shard_map(
        shards,
        mesh=mesh,
        in_specs=(
            P("spec", None, "cells", None),
            P("cells", None),
            P("cells", None),
            P("cells", None),
            P("cells", None),
            P("cells", None),
            P("spec", None, "cells", None),
        ),
        out_specs=(P("spec", None, "cells", None), P("cells", None), P("cells", None)),
        check_vma=False,
    )
```

```python
import functools
import math

import jax
import jax.numpy as jnp
import numpy as np
from jax import lax
from jax.experimental import pallas as pl
from jax.experimental.pallas import tpu as pltpu
from jax.sharding import PartitionSpec as P

NF = 32
ND = 36
STEPS = 2

epsilon = 1e-06
energy_ref = 0.5
time_step = 0.5
courant = 0.7
ratio_step = 1.1

F32 = jnp.float32
LOG2E = math.log2(math.e)

_every = np.exp(np.arange(NF, dtype=np.float32) * np.float32(math.log(ratio_step))).astype(np.float32)
_total = _every.sum(dtype=np.float32)
HIGHEST = float(_every[-1])
MEAN_RATIO = float((_every * _every).sum(dtype=np.float32) / _total)
_weights = _every / (np.float32(ND) * _total)
_q = (_every / _every[-1]) ** 2
NTAB = 5
TABLE = np.stack([_every, 1 / _every, _weights, _q, _weights * _every], axis=1).astype(np.float32).reshape(-1)

_angle = (np.float32(2.0 * math.pi) * np.arange(ND, dtype=np.float32) / np.float32(ND)).astype(np.float32)
COS, SIN = np.cos(_angle).astype(np.float32), np.sin(_angle).astype(np.float32)
KX, KY = np.float32(courant) * np.abs(COS), np.float32(courant) * np.abs(SIN)
XP, YP = [bool(c >= 0) for c in COS], [bool(s >= 0) for s in SIN]
NL = sum(YP)
NH = ND - NL
assert YP == [True] * NL + [False] * NH and NL == NH
QUADS = [[d for d in range(ND) if (XP[d], YP[d]) == quad] for quad in ((1, 1), (0, 1), (0, 0), (1, 0))]
DIRS = np.stack([v[a:b] for a, b in ((0, NL), (NL, ND)) for v in (KX, KY, COS, SIN)]).astype(np.float32)
DIRS = np.ascontiguousarray(np.broadcast_to(DIRS[:, :, None], DIRS.shape + (128,)))
MISC = 2 * NL
MROWS = 4
NMISC = 5

MIB = 1 << 20


def coef(tab, j, nf, which):
    return tab[(lax.axis_index("spec") * nf + j) * NTAB + which]


def shift_x(x, plus):
    return pltpu.roll(x, 1 if plus else x.shape[1] - 1, 1)


def first_row(x):
    return lax.broadcasted_iota(jnp.int32, x.shape, 0) == 0


def last_row(x):
    return lax.broadcasted_iota(jnp.int32, x.shape, 0) == x.shape[0] - 1


def from_before(x, above):
    return jnp.where(first_row(x), above, pltpu.roll(x, 1, 0))


def from_after(x, below):
    return jnp.where(last_row(x), below, pltpu.roll(x, x.shape[0] - 1, 0))


def shift_y(x, plus, outside):
    return from_before(x, outside) if plus else from_after(x, outside)


def damping_of(energy, moment):
    shifted = energy + epsilon
    ratio = moment / (shifted * MEAN_RATIO)
    r2 = ratio * ratio
    steep = energy * (r2 * r2) / energy_ref
    return shifted, ratio, steep, steep * steep * ratio


def grads_of(energy, moment, white, damp_total):
    shifted, ratio, steep, damping = damping_of(energy, moment)
    grad_damp = -time_step * white * damp_total
    grad_ratio = 9.0 * grad_damp * steep * steep
    r2 = ratio * ratio
    grad_energy = grad_damp * 2.0 * steep * (r2 * r2) * ratio / energy_ref - grad_ratio * ratio / shifted
    grad_moment = grad_ratio / (shifted * MEAN_RATIO)
    return grad_energy, grad_moment, damping


def gate(q, white, damping, ocean):
    return ocean * jnp.exp2((-time_step * LOG2E) * q * (white * damping))


def rows_from(tiles, plus, outside):
    moved = [pltpu.roll(x, 1 if plus else 7, 0) for x in tiles]
    mark = first_row(tiles[0]) if plus else last_row(tiles[0])
    feed = [outside] + moved[:-1] if plus else moved[1:] + [outside]
    return [jnp.where(mark, a, b) for a, b in zip(feed, moved)]


def slab(ref, *index):
    return [ref[(*index, slice(t, t + 8))] for t in range(0, ref.shape[-2], 8)]


def by_parity(write, first, second):
    odd = lax.rem(lax.axis_index("cells"), 2)

    @pl.when(odd == 0)
    def _():
        write(first, second)

    @pl.when(odd == 1)
    def _():
        write(second, first)


class Either:
    def __init__(self, even, odd):
        self.even, self.odd, self.shape = even, odd, even.shape

    def __getitem__(self, at):
        x, y = self.even[at], self.odd[at]
        return jnp.where(jnp.full(x.shape, lax.rem(lax.axis_index("cells"), 2), jnp.int32) == 0, x, y)


def beside(first, second):
    return Either(second, first), Either(first, second)


def misc_at(r, k):
    m = r * NMISC + k
    return m // MROWS, MISC + m % MROWS


def misc_row(ref, r, k):
    j, row = misc_at(r, k)
    return ref[j, row : row + 1, :]


def halo_rows(ref, j, r):
    return ref[j, r * NL : (r + 1) * NL, :]


def fetches(hbm, ref, sems):
    return lambda j: pltpu.make_async_copy(hbm.at[j], ref.at[j], sems.at[j])


NBUF = 3


def edge_kernel(s_hbm, mask_h, coef_h, white_h, speed_h, angle_h, a_ref, b_ref, low, high, sems, fields, ints, small_sems):
    nf, _, rows, nc = s_hbm.shape

    def fetch(j):
        return (
            pltpu.make_async_copy(s_hbm.at[j, 0:NL, rows - 8 : rows, :], low.at[j], sems.at[0, j]),
            pltpu.make_async_copy(s_hbm.at[j, NL:ND, 0:8, :], high.at[j], sems.at[1, j]),
        )

    smalls = [pltpu.make_async_copy(mask_h, ints, small_sems.at[0])]
    for k, f in enumerate((coef_h, white_h, speed_h, angle_h)):
        smalls.append(pltpu.make_async_copy(f, fields.at[k], small_sems.at[1 + k]))
    for c in smalls:
        c.start()
    for j in range(nf):
        for c in fetch(j):
            c.start()
    for c in smalls:
        c.wait()

    def write(up_ref, dn_ref):
        @pl.loop(0, nf)
        def _(j):
            up_ref[j, MISC:, :] = jnp.zeros_like(up_ref[j, MISC:, :])
            dn_ref[j, MISC:, :] = jnp.zeros_like(dn_ref[j, MISC:, :])

        for side, out in ((slice(rows - 2, rows), up_ref), (slice(0, 2), dn_ref)):
            kappa = (time_step * LOG2E / HIGHEST) * (fields[0, side] * fields[2, side])
            angle = fields[3, side]
            for k, v in enumerate((kappa, jnp.cos(angle), jnp.sin(angle), ints[side].astype(F32), fields[1, side])):
                for r in range(2):
                    a, b = misc_at(r, k)
                    out[a, b : b + 1, :] = v[r : r + 1]

        @pl.loop(0, nf)
        def _(j):
            for c in fetch(j):
                c.wait()
            for r in range(2):
                for d in range(NL):
                    up_ref[j, r * NL + d : r * NL + d + 1, :] = low[j, d, 6 + r : 7 + r, :]
                    dn_ref[j, r * NL + d : r * NL + d + 1, :] = high[j, d, r : r + 1, :]

    by_parity(write, a_ref, b_ref)


def start_kernel(tab, s_ref, mask, t0_ref, sums):
    nf = s_ref.shape[0]
    rows, nc = mask.shape
    sums[...] = jnp.zeros_like(sums)

    @pl.loop(0, nf)
    def _(j):
        rj, w, wf = [coef(tab, j, nf, k) for k in (1, 2, 4)]
        for t in range(0, rows, 8):
            acc = [None] * 5

            def add(k, v):
                acc[k] = v if acc[k] is None else acc[k] + v

            for d in range(ND):
                x = s_ref[j, d, t : t + 8, :]
                add(0, x)
                add(1 if XP[d] else 2, float(KX[d]) * x)
                add(3 if YP[d] else 4, float(KY[d]) * x)
            for k in range(5):
                sums[0, k, t : t + 8, :] += (w if k == 0 else w * rj) * acc[k]
                sums[1, k, t : t + 8, :] += (wf if k == 0 else wf * rj) * acc[k]

    ocean = mask[...].astype(F32)
    t0_ref[2 * rows :, :] = jnp.zeros_like(t0_ref[2 * rows :, :])
    for e in range(2):
        total, xp, xm, yp, ym = [ocean * sums[e, k] for k in range(5)]
        t0_ref[e * rows : (e + 1) * rows, :] = total + (
            shift_x(xp, True) + shift_x(xm, False) + from_before(yp, 0.0) + from_after(ym, 0.0) - (xp + xm + yp + ym)
        )
        t0_ref[2 * rows + e : 2 * rows + e + 1, :] = yp[rows - 1 : rows]
        t0_ref[2 * rows + 2 + e : 2 * rows + 3 + e, :] = ym[0:1]


def wind_kernel(tab, lam_ref, coef_in, speed, angle, p_ref, al_ref, a_ref, b_ref, expo):
    nf = lam_ref.shape[0]
    rows, nc = angle.shape
    for ref in (a_ref, b_ref):
        ref[:, MISC:, :] = jnp.zeros_like(ref[:, MISC:, :])
    kappa = (time_step * LOG2E / HIGHEST) * (coef_in[...] * speed[...])
    ca, sa = jnp.cos(angle[...]), jnp.sin(angle[...])
    for d in range(ND):
        align = jnp.maximum(float(COS[d]) * ca + float(SIN[d]) * sa, 0.0)
        al = align * align
        al_ref[d] = al
        expo[d] = kappa * al

    def write(up_ref, dn_ref):
        @pl.loop(0, nf)
        def _(j):
            fr = coef(tab, j, nf, 0)
            for d in range(ND):
                p = jnp.exp2(fr * expo[d]) * lam_ref[j, d]
                p_ref[j, d] = p
                for r in range(2):
                    at = slice(r * NL + d % NL, r * NL + d % NL + 1)
                    if d < NL:
                        dn_ref[j, at, :] = p[r : r + 1]
                    else:
                        up_ref[j, at, :] = p[rows - 2 + r : rows - 1 + r]

    by_parity(write, a_ref, b_ref)


def halo_growth(fr, dirs, half, misc, r):
    cosd, sind = dirs[4 * half + 2][:, 0:1], dirs[4 * half + 3][:, 0:1]
    align = jnp.maximum(cosd * misc_row(misc, r, 1) + sind * misc_row(misc, r, 2), 0.0)
    return jnp.exp2(fr * (misc_row(misc, r, 0) * (align * align)))


def halo_adv(rj, dirs, half, near, far, transpose):
    kx, ky, cosd = [dirs[4 * half + k][:, 0:1] for k in range(3)]
    before, after = shift_x(near, not transpose), shift_x(near, transpose)
    moved = jnp.where(cosd >= 0, before, after)
    return near + rj * (kx * (moved - near) + ky * (far - near))


def grow(outer, tab, j, s_ref, ocean, coef_in, speed, al_ref, u_ref, sum_ref, work, edge, before):
    nf, _, rows, nc = s_ref.shape
    fr, rj = coef(tab, j, nf, 0), coef(tab, j, nf, 1)
    work[...] = (fr * (time_step * LOG2E / HIGHEST)) * (coef_in[...] * speed[...])
    for t in range(0, rows, 8):
        at8 = slice(t, t + 8)
        o = rj * ocean[at8]
        seen = set()
        for quad in QUADS:
            plus = YP[quad[0]]
            end = t == 0 if plus else t + 8 == rows
            if end != outer:
                continue
            n = t - 1 if plus else t + 8
            acc = [None] * 3
            for d in quad:
                kx, ky = float(KX[d]), float(KY[d])
                x = o * s_ref[j, d, at8, :]
                if outer:
                    row = edge[0, d : d + 1, :] if plus else edge[1, d - NL : d - NL + 1, :]
                else:
                    row = (rj * ocean[n : n + 1]) * s_ref[j, d, n : n + 1, :]
                y = shift_y(x, plus, row)
                u = jnp.exp2(work[at8] * al_ref[d, at8]) * ((fr - (kx + ky)) * x + kx * shift_x(x, XP[d]) + ky * y)
                u_ref[j, d, at8, :] = u
                for k, v in enumerate((u, kx * u, ky * u)):
                    acc[k] = v if acc[k] is None else acc[k] + v
            for k, key in enumerate((0, 1 if XP[quad[0]] else 2, 3 if plus else 4)):
                at = (key, j, at8)
                if key in seen:
                    sum_ref[at] += acc[k]
                else:
                    sum_ref[at] = acc[k] if before is None else before[at] + acc[k]
                seen.add(key)
        for key in range(5):
            if key not in seen:
                at = (key, j, at8)
                sum_ref[at] = jnp.zeros((8, nc), F32) if before is None else before[at]


def inner_kernel(tab, s_ref, mask, coef_in, speed, al_ref, u_ref, sum_ref, work):
    ocean = mask[...].astype(F32)

    @pl.loop(0, s_ref.shape[0])
    def _(j):
        grow(False, tab, j, s_ref, ocean, coef_in, speed, al_ref, u_ref, sum_ref, work, None, None)


def grown_kernel(tab, dirs, s_ref, mask, coef_in, speed, al_ref, s_first, s_second, u_in, before, u_ref, sum_ref, ul_ref, uh_ref, sy_ref, edge, work):
    nf, _, rows, nc = s_ref.shape
    lo, hi = beside(s_first, s_second)
    ocean = mask[...].astype(F32)

    @pl.loop(0, nf)
    def _(j):
        fr, rj = coef(tab, j, nf, 0), coef(tab, j, nf, 1)
        for half, (blk, near, far, out) in enumerate(((lo, 1, 0, ul_ref), (hi, 0, 1, uh_ref))):
            x = [misc_row(blk, r, 3) * halo_rows(blk, j, r) for r in range(2)]
            edge[half] = rj * x[near]
            u = halo_growth(fr, dirs, half, blk, near) * halo_adv(rj, dirs, half, x[near], x[far], False)
            out[j] = u
            sy_ref[half, pl.ds(j, 1), :] = jnp.sum(dirs[4 * half + 1][:, 0:1] * u, axis=0, keepdims=True)
        grow(True, tab, j, s_ref, ocean, coef_in, speed, al_ref, u_ref, sum_ref, work, edge, before)
        for t in range(0, rows, 8):
            a, b, c, d, e = [sum_ref[k, j, t : t + 8, :] for k in range(5)]
            sum_ref[0, j, t : t + 8, :] = a - rj * (b + c + d + e)


def product_kernel(tab, u_ref, p_ref, al_ref, ul_ref, uh_ref, r_ref, t_ref):
    nf, _, rows, nc = u_ref.shape

    @pl.loop(0, nf)
    def _(j):
        rj = coef(tab, j, nf, 1)
        for t in range(0, rows, 8):
            seen = set()
            for quad in QUADS:
                acc = [None] * 6
                for d in quad:
                    kx, ky = float(KX[d]), float(KY[d])
                    u, p, al = u_ref[j, d, t : t + 8, :], p_ref[j, d, t : t + 8, :], al_ref[d, t : t + 8, :]
                    if YP[d]:
                        row = ul_ref[j, d : d + 1, :] if t == 0 else u_ref[j, d, t - 1 : t, :]
                        y = jnp.where(first_row(u), row, pltpu.roll(u, 1, 0))
                    else:
                        row = uh_ref[j, d - NL : d - NL + 1, :] if t + 8 == rows else u_ref[j, d, t + 8 : t + 9, :]
                        y = jnp.where(last_row(u), row, pltpu.roll(u, 7, 0))
                    cu = (1.0 - rj * (kx + ky)) * (p * u)
                    px, py = kx * (p * shift_x(u, XP[d])), ky * (p * y)
                    for k, v in enumerate((cu, px, py, al * cu, al * px, al * py)):
                        acc[k] = v if acc[k] is None else acc[k] + v
                xk, yk = (1 if XP[quad[0]] else 2), (3 if YP[quad[0]] else 4)
                for k, ref in enumerate((r_ref, t_ref)):
                    for key, v in zip((0, xk, yk), acc[3 * k : 3 * k + 3]):
                        at = (key, j, slice(t, t + 8))
                        ref[at] = ref[at] + v if (k, key) in seen else v
                        seen.add((k, key))


def total_kernel(rows, *refs):
    parts, (tot, first, second) = refs[:-3], refs[-3:]
    total = parts[0][...]
    for part in parts[1:]:
        total = total + part[...]
    tot[...] = total

    def write(up, dn):
        up[...] = jnp.zeros_like(up)
        dn[...] = jnp.zeros_like(dn)
        for k, row in enumerate((rows - 1, 2 * rows - 1, 2 * rows, 2 * rows + 1)):
            up[k : k + 1, :] = total[row : row + 1]
        for k, row in enumerate((0, rows, 2 * rows + 2, 2 * rows + 3)):
            dn[k : k + 1, :] = total[row : row + 1]

    by_parity(write, first, second)


def advected_sum(rj, h, above, below, s):
    return h * s[0], rj * (
        shift_x(h * s[1], True) + shift_x(h * s[2], False) + from_before(h * s[3], above) + from_after(h * s[4], below)
    )


def first_kernel(nf, tab, tot, e_first, e_second, s_first, s_second, mask, white, sum_ref, sy_ref, t0_ref, t0h_ref, h0_ref, h0h_ref, t1_ref):
    rows, nc = mask.shape
    lo, hi = beside(e_first, e_second)
    lo_misc, hi_misc = beside(s_first, s_second)
    ocean = mask[...].astype(F32)
    row = lax.broadcasted_iota(jnp.int32, (rows, nc), 0)
    total = tot[...]
    field = []
    halo = []
    t0h_ref[...] = jnp.zeros_like(t0h_ref)
    for k in range(2):
        v = total[k * rows : (k + 1) * rows]
        v = v + jnp.where(row == 0, lo[2 + k : 3 + k, :], 0.0) + jnp.where(row == rows - 1, hi[2 + k : 3 + k, :], 0.0)
        field.append(ocean * v)
        t0_ref[k] = field[k]
        above = misc_row(lo_misc, 1, 3) * (lo[k : k + 1, :] + total[2 * rows + 2 + k : 2 * rows + 3 + k])
        below = misc_row(hi_misc, 0, 3) * (hi[k : k + 1, :] + total[2 * rows + k : 2 * rows + 1 + k])
        halo.append((above, below))
        t0h_ref[k : k + 1, :] = above
        t0h_ref[2 + k : 3 + k, :] = below
    damping = damping_of(*field)[3]
    damp_lo = damping_of(halo[0][0], halo[1][0])[3]
    damp_hi = damping_of(halo[0][1], halo[1][1])[3]
    energy, moment = jnp.zeros((rows, nc), F32), jnp.zeros((rows, nc), F32)
    for j in range(nf):
        rj, w, q, wf = [coef(tab, j, nf, k) for k in (1, 2, 3, 4)]
        h = gate(q, white[...], damping, ocean)
        h_lo = gate(q, misc_row(lo_misc, 1, 4), damp_lo, misc_row(lo_misc, 1, 3))
        h_hi = gate(q, misc_row(hi_misc, 0, 4), damp_hi, misc_row(hi_misc, 0, 3))
        h0_ref[j] = h
        h0h_ref[0, j : j + 1, :] = h_lo
        h0h_ref[1, j : j + 1, :] = h_hi
        centre, around = advected_sum(
            rj, h, h_lo * sy_ref[0, j : j + 1, :], h_hi * sy_ref[1, j : j + 1, :], [sum_ref[k, j] for k in range(5)]
        )
        adv = centre + around
        energy, moment = energy + w * adv, moment + wf * adv
    t1_ref[0:rows, :] = energy
    t1_ref[rows : 2 * rows, :] = moment


def gathered(rj, h, h_lo, h_hi, r):
    return h * r[0] + rj * (
        shift_x(h, True) * r[1] + shift_x(h, False) * r[2] + from_before(h, h_lo) * r[3] + from_after(h, h_hi) * r[4]
    )


def second_kernel(nf, n, tab, *refs):
    parts, (mask, white, h0_ref, h0h_ref, r_ref, t1_ref, h1_ref, d1_ref) = refs[:n], refs[n:]
    rows, nc = mask.shape
    ocean = mask[...].astype(F32)
    total = parts[0][...]
    for part in parts[1:]:
        total = total + part[...]
    energy, moment = ocean * total[:rows], ocean * total[rows:]
    t1_ref[0] = energy
    t1_ref[1] = moment
    damping = damping_of(energy, moment)[3]
    acc = jnp.zeros((rows, nc), F32)
    for j in range(nf):
        rj, q = coef(tab, j, nf, 1), coef(tab, j, nf, 3)
        h1 = gate(q, white[...], damping, ocean)
        h1_ref[j] = h1
        part = gathered(rj, h0_ref[j], h0h_ref[0, j : j + 1, :], h0h_ref[1, j : j + 1, :], [r_ref[k, j] for k in range(5)])
        acc = acc + q * (h1 * part)
    d1_ref[...] = acc


def third_kernel(nf, n, tab, *refs):
    parts = refs[:n]
    mask, white, speed, t1, h0_ref, h0h_ref, h1_ref, sum_ref, sy_ref, r_ref, t_ref = refs[n : n + 11]
    d1_ref, v1_ref, d0_ref, f1_ref, first, second = refs[n + 11 :]
    rows, nc = mask.shape
    ocean = mask[...].astype(F32)
    damp = parts[0][...]
    for part in parts[1:]:
        damp = damp + part[...]
    d1_ref[...] = damp
    grad_e, grad_m, _ = grads_of(t1[0], t1[1], white[...], damp)
    acc, force = jnp.zeros((rows, nc), F32), jnp.zeros((rows, nc), F32)
    push_lo, push_hi = jnp.zeros((1, nc), F32), jnp.zeros((1, nc), F32)
    for j in range(nf):
        fr, rj, w, q = [coef(tab, j, nf, k) for k in range(4)]
        h0, h1 = h0_ref[j], h1_ref[j]
        h_lo, h_hi = h0h_ref[0, j : j + 1, :], h0h_ref[1, j : j + 1, :]
        v1 = ocean * (w * (grad_e + fr * grad_m))
        v1_ref[j] = v1
        s, r = [sum_ref[k, j] for k in range(5)], [r_ref[k, j] for k in range(5)]
        inner = (
            shift_x(h1 * r[1], False)
            + shift_x(h1 * r[2], True)
            + from_after(h1 * r[3], 0.0)
            + from_before(h1 * r[4], 0.0)
            + s[1] * shift_x(v1, False)
            + s[2] * shift_x(v1, True)
            + s[3] * from_after(v1, 0.0)
            + s[4] * from_before(v1, 0.0)
        )
        acc = acc + q * (h0 * (h1 * r[0] + v1 * s[0] + rj * inner))
        push_lo = push_lo + (q * rj) * (h_lo * (h1[0:1] * r[3][0:1] + v1[0:1] * sy_ref[0, j : j + 1, :]))
        e = rows - 1
        push_hi = push_hi + (q * rj) * (
            h_hi * (h1[e : e + 1] * r[4][e : e + 1] + v1[e : e + 1] * sy_ref[1, j : j + 1, :])
        )
        part = gathered(rj, h0, h_lo, h_hi, [t_ref[k, j] for k in range(5)])
        force = force + fr * (h1 * part)
    def write(up, dn):
        for k, v in enumerate((t1[0], t1[1], damp)):
            up[2 * k : 2 * k + 2, :] = v[rows - 2 : rows]
            dn[2 * k : 2 * k + 2, :] = v[0:2]
        up[6:7, :] = acc[rows - 1 : rows]
        up[7:8, :] = push_hi
        dn[6:7, :] = acc[0:1]
        dn[7:8, :] = push_lo

    by_parity(write, first, second)
    d0_ref[0:rows, :] = acc
    d0_ref[rows:, :] = jnp.zeros_like(d0_ref[rows:, :])
    d0_ref[rows : rows + 1, :] = push_lo
    d0_ref[rows + 1 : rows + 2, :] = push_hi
    f1_ref[...] = (speed[...] / HIGHEST) * force


def fourth_kernel(nf, tab, part, b_first, b_second, s_first, s_second, a_low, a_high, t_ref, h0_ref, h1_ref, v1_ref, f1_ref, speed, out):
    rows, nc = speed.shape
    lo, hi = beside(b_first, b_second)
    lo_misc, hi_misc = beside(s_first, s_second)
    row = lax.broadcasted_iota(jnp.int32, (rows, nc), 0)
    v = part[0:rows, :]
    v = v + jnp.where(row == 0, lo[7:8, :], 0.0) + jnp.where(row == rows - 1, hi[7:8, :], 0.0)
    out[0:rows, :] = v
    out[rows : rows + 8, :] = jnp.zeros((8, nc), F32)
    out[rows : rows + 1, :] = part[rows : rows + 1, :] + lo[6:7, :]
    out[rows + 1 : rows + 2, :] = part[rows + 1 : rows + 2, :] + hi[6:7, :]
    outside = []
    for got, misc, r in ((lo, lo_misc, 1), (hi, hi_misc, 0)):
        energy, moment, damp = [got[2 * k + r : 2 * k + r + 1, :] for k in range(3)]
        white = misc_row(misc, r, 4)
        grad_e, grad_m, damping = grads_of(energy, moment, white, damp)
        outside.append((white, damping, misc_row(misc, r, 3), grad_e, grad_m))
    force = jnp.zeros((rows, nc), F32)
    low = a_low.shape[1]
    for j in range(nf):
        fr, w, q = [coef(tab, j, nf, k) for k in (0, 2, 3)]
        a = [a_low[k, j] if j < low else a_high[k, j - low] for k in range(9)]
        h1, v1 = h1_ref[j], v1_ref[j]
        edges = [(gate(q, white, damping, o), o * (w * (ge + fr * gm))) for white, damping, o, ge, gm in outside]
        force = force + (fr * h0_ref[j]) * (h1 * t_ref[0, j]) + v1 * a[0]
        for x, k, b in ((v1, 0, 1), (h1, 4, 0)):
            force = force + (
                shift_x(x, False) * a[k + 1]
                + shift_x(x, True) * a[k + 2]
                + from_after(x, edges[1][b]) * a[k + 3]
                + from_before(x, edges[0][b]) * a[k + 4]
            )
    out[rows + 8 :, :] = (speed[...] / HIGHEST) * force + f1_ref[...]


def force_kernel(first, tab, u_ref, p_ref, al_ref, h0_ref, p_first, p_second, a_ref):
    nf, _, rows, nc = u_ref.shape
    pl_ref, ph_ref = beside(p_first, p_second)

    @pl.loop(0, a_ref.shape[1])
    def _(i):
        j = first + i
        fr, rj = coef(tab, j, nf, 0), coef(tab, j, nf, 1)
        for t in range(0, rows, 8):
            seen = set()
            for quad in QUADS:
                acc = [None] * 5
                for d in quad:
                    kx, ky = float(KX[d]), float(KY[d])
                    u, p, al = u_ref[j, d, t : t + 8, :], p_ref[j, d, t : t + 8, :], al_ref[d, t : t + 8, :]
                    if YP[d]:
                        row = ph_ref[j, d : d + 1, :] if t + 8 == rows else p_ref[j, d, t + 8 : t + 9, :]
                        y = from_after(p, row)
                    else:
                        row = pl_ref[j, d : d + 1, :] if t == 0 else p_ref[j, d, t - 1 : t, :]
                        y = from_before(p, row)
                    au = al * u
                    xau, yau = kx * au, ky * au
                    for k, v in enumerate(((1.0 - rj * (kx + ky)) * au, xau, yau, xau * shift_x(p, not XP[d]), yau * y)):
                        acc[k] = v if acc[k] is None else acc[k] + v
                xk, yk = (1 if XP[quad[0]] else 2), (3 if YP[quad[0]] else 4)
                for key, v in zip((0, xk, yk, 4 + xk, 4 + yk), acc):
                    at = (key, i, slice(t, t + 8))
                    a_ref[at] = a_ref[at] + v if key in seen else v
                    seen.add(key)
        h0 = h0_ref[j]
        for k in range(9):
            a_ref[k, i] = (fr * h0 if k == 0 else h0) * a_ref[k, i]


def back_kernel(tab, dirs, p_ref, coef_in, al_ref, h0_ref, h0h_ref, h1_ref, v1_ref, p_first, p_second, s_first, s_second, b_first, b_second, speed, z_ref, zl_ref, zh_ref, edge, halo, scaled, work):
    nf, _, rows, nc = p_ref.shape
    pl_ref, ph_ref = beside(p_first, p_second)
    lo_misc, hi_misc = beside(s_first, s_second)
    lo, hi = beside(b_first, b_second)
    sides = ((0, ph_ref, hi_misc, hi, 0, 1, 1, zh_ref), (1, pl_ref, lo_misc, lo, 1, 0, 0, zl_ref))
    for side, (_, _, misc, got, *_) in enumerate(sides):
        for r in range(2):
            energy, moment, damp = [got[2 * k + r : 2 * k + r + 1, :] for k in range(3)]
            white = misc_row(misc, r, 4)
            grad_e, grad_m, damping = grads_of(energy, moment, white, damp)
            for k, v in enumerate((grad_e, grad_m, white * damping)):
                halo[side, r, k : k + 1, :] = v

    @pl.loop(0, nf)
    def _(j):
        fr, rj = coef(tab, j, nf, 0), coef(tab, j, nf, 1)
        w, q = coef(tab, j, nf, 2), coef(tab, j, nf, 3)
        for side, (half, blk, misc, _, near, far, which, out) in enumerate(sides):
            x = []
            for r in range(2):
                ocean = misc_row(misc, r, 3)
                h = gate(q, halo[side, r, 2:3, :], 1.0, ocean)
                v = ocean * (w * (halo[side, r, 0:1, :] + fr * halo[side, r, 1:2, :]))
                x.append(halo_rows(blk, j, r) * h + v)
            edge[side] = x[near]
            moved = halo_adv(rj, dirs, half, x[near], x[far], True) * halo_growth(fr, dirs, half, misc, near)
            out[j] = moved * h0h_ref[which, pl.ds(j, 1), :]
        tiles = range(rows // 8)
        at8 = [slice(8 * t, 8 * t + 8) for t in tiles]
        work[...] = (fr * (time_step * LOG2E / HIGHEST)) * (coef_in[...] * speed[...])
        for t in tiles:
            scaled[at8[t]] = rj * h0_ref[j, at8[t]]
        for d in range(ND):
            kx, ky = float(KX[d]), float(KY[d])
            x = [p_ref[j, d, at8[t]] * h1_ref[j, at8[t]] + v1_ref[j, at8[t]] for t in tiles]
            row = edge[0, d : d + 1, :] if YP[d] else edge[1, d - NL : d - NL + 1, :]
            y = rows_from(x, not YP[d], row)
            for t in tiles:
                back = (fr - (kx + ky)) * x[t] + kx * shift_x(x[t], not XP[d]) + ky * y[t]
                z_ref[j, d, at8[t]] = back * (jnp.exp2(work[at8[t]] * al_ref[d, at8[t]]) * scaled[at8[t]])


def out_kernel(n, tab, *refs):
    parts, refs = refs[:n], refs[n:]
    z_ref, zl_ref, zh_ref, t0, t0h, t1, d1, mask, white, s_first, s_second = refs[:11]
    lo_misc, hi_misc = beside(s_first, s_second)
    out_hbm, gi_ref, gw_ref, own, halo, edge, work, buf, sems = refs[11:]
    nf, _, rows, nc = z_ref.shape
    ocean = mask[...].astype(F32)
    total = parts[0][...]
    for part in parts[1:]:
        total = total + part[...]
    damp = total[0:rows]
    gi_ref[...] = time_step * total[rows + 8 :]
    grad_e, grad_m, damping = grads_of(t0[0], t0[1], white[...], damp)
    own[0] = grad_e
    own[1] = grad_m
    gw_ref[...] = -time_step * (damping * damp + damping_of(t1[0], t1[1])[3] * d1[...])
    above, below = total[rows : rows + 1], total[rows + 1 : rows + 2]
    sides = ((hi_misc, 0, 2, below, zh_ref), (lo_misc, 1, 0, above, zl_ref))
    for side, (misc, r, k, damp, _) in enumerate(sides):
        e, m, _ = grads_of(t0h[k : k + 1, :], t0h[k + 1 : k + 2, :], misc_row(misc, r, 4), damp)
        halo[side, 0:1, :] = e
        halo[side, 1:2, :] = m

    def put(j):
        return pltpu.make_async_copy(buf.at[j % NBUF], out_hbm.at[j], sems.at[j % NBUF])

    @pl.loop(0, nf)
    def _(j):
        slot = j % NBUF
        fr, rj, w = [coef(tab, j, nf, k) for k in range(3)]
        for side, (misc, r, _, _, z) in enumerate(sides):
            edge[side] = z[j] + misc_row(misc, r, 3) * (w * (halo[side, 0:1, :] + fr * halo[side, 1:2, :]))
        tiles = range(rows // 8)
        o = [ocean[8 * t : 8 * t + 8] for t in tiles]
        v = [o[t] * (w * (own[0, 8 * t : 8 * t + 8] + fr * own[1, 8 * t : 8 * t + 8])) for t in tiles]
        for t in tiles:
            work[0, 8 * t : 8 * t + 8] = v[t]
            work[1, 8 * t : 8 * t + 8] = rj * o[t]

        @pl.when(j >= NBUF)
        def _():
            put(j - NBUF).wait()

        for d in range(ND):
            kx, ky = float(KX[d]), float(KY[d])
            x = [z + work[0, 8 * t : 8 * t + 8] for t, z in enumerate(slab(z_ref, j, d))]
            row = edge[0, d : d + 1, :] if YP[d] else edge[1, d - NL : d - NL + 1, :]
            y = rows_from(x, not YP[d], row)
            for t in tiles:
                back = (fr - (kx + ky)) * x[t] + kx * shift_x(x[t], not XP[d]) + ky * y[t]
                buf[slot, d, 8 * t : 8 * t + 8, :] = work[1, 8 * t : 8 * t + 8] * back
        put(j).start()

    for j in range(max(0, nf - NBUF), nf):
        put(j).wait()


VMEM = pl.BlockSpec(memory_space=pltpu.VMEM)
SMEM = pl.BlockSpec(memory_space=pltpu.SMEM)
HBM = pl.BlockSpec(memory_space=pltpu.HBM)


def f32(*shape):
    return jax.ShapeDtypeStruct(shape, F32)


def vmem(*shape):
    return pltpu.VMEM(shape, F32)


def call(kernel, name, outs, args, scratch=(), hbm=(), held=(), out_hbm=(), limit=6, alias=None):
    put = {**dict.fromkeys(hbm, pltpu.HBM), **dict.fromkeys(held, pltpu.VMEM)}
    args = [pltpu.with_memory_space_constraint(a, put[k]) if k in put else a for k, a in enumerate(args)]
    return pl.pallas_call(
        kernel,
        name=name,
        out_shape=outs,
        in_specs=[HBM if k in hbm else SMEM if a.ndim == 1 else VMEM for k, a in enumerate(args)],
        out_specs=[HBM if k in out_hbm else VMEM for k in range(len(outs))],
        scratch_shapes=list(scratch),
        input_output_aliases=alias or {},
        compiler_params=pltpu.CompilerParams(vmem_limit_bytes=limit * MIB),
        cost_estimate=pl.CostEstimate(flops=1, bytes_accessed=1, transcendentals=0),
    )(*args)


def peers(x):
    n = lax.axis_size("spec")
    if n & (n - 1) == 0:
        return [lax.ppermute(x, "spec", [(i, i ^ k) for i in range(n)]) for k in range(1, n)]
    return [lax.ppermute(x, "spec", [(i, (i + k) % n) for i in range(n)]) for k in range(1, n)]


def exchange(first, second):
    n = lax.axis_size("cells")
    swaps = [[(i, i + 1) for i in range(odd, n - 1, 2)] for odd in range(2)]
    return [lax.ppermute(x, "cells", pairs + [(b, a) for a, b in pairs]) for x, pairs in zip((first, second), swaps)]


def after(first, *later):
    return lax.optimization_barrier((first, *later))[1:]


def shards(spectrum_start, input_coef, white_coef, wind_speed, wind_angle, sea_mask, cotangent):
    nf, _, rows, nc = spectrum_start.shape
    n = lax.axis_size("spec")
    tab, dirs = jnp.asarray(TABLE), jnp.asarray(DIRS)
    big = vmem(nf, ND, rows, nc)
    band = f32(nf, MISC + MROWS, nc)
    line, duo, hs, sums = f32(nf, NL, nc), f32(2, nf, nc), f32(nf, rows, nc), f32(5, nf, rows, nc)
    flat, two, push = f32(rows, nc), f32(2, rows, nc), f32(8, nc)
    stream = [vmem(NBUF, ND, rows, nc), pltpu.SemaphoreType.DMA((NBUF,))]
    heavy = dict(limit=8)

    s_up, s_dn = call(
        edge_kernel, "edge", [band, band], [spectrum_start, sea_mask, input_coef, white_coef, wind_speed, wind_angle],
        [
            vmem(nf, NL, 8, nc), vmem(nf, NL, 8, nc), pltpu.SemaphoreType.DMA((2, nf)), vmem(4, rows, nc),
            pltpu.VMEM((rows, nc), jnp.int32), pltpu.SemaphoreType.DMA((5,)),
        ],
        hbm=range(6), **heavy,
    )
    s_lo, s_hi = exchange(s_up, s_dn)
    (mask,) = after(s_up, sea_mask)
    (t0_part,) = call(
        start_kernel, "start", [f32(2 * rows + 8, nc)], [tab, spectrum_start, mask], [vmem(2, 5, rows, nc)], held=(1,), **heavy
    )
    t0_parts = peers(t0_part)
    (speed,) = after(t0_part, wind_speed)
    p, al, p_up, p_dn = call(
        wind_kernel, "wind", [big, vmem(ND, rows, nc), band, band], [tab, cotangent, input_coef, speed, wind_angle],
        [vmem(ND, rows, nc)], held=(1,), **heavy,
    )
    u_inner, s5_inner = call(
        inner_kernel, "inner", [big, sums], [tab, spectrum_start, sea_mask, input_coef, wind_speed, al], [vmem(rows, nc)],
        held=(1, 5), **heavy,
    )
    (t0_own,) = after(s5_inner, t0_part)
    tot0, e_up, e_dn = call(functools.partial(total_kernel, rows), "total", [f32(2 * rows + 8, nc), push, push], [t0_own, *t0_parts])
    e_lo, e_hi = exchange(e_up, e_dn)
    (mask,) = after(tot0, sea_mask)
    u, s5, u_lo, u_hi, sy = call(
        grown_kernel, "grown", [big, sums, line, line, duo], [tab, dirs, spectrum_start, mask, input_coef, wind_speed, al, s_lo, s_hi, u_inner, s5_inner],
        [vmem(2, NL, nc), vmem(rows, nc)], held=(2, 6, 9), alias={9: 0}, **heavy,
    )
    t0, t0h, h0, h0h, t1_part = call(
        functools.partial(first_kernel, nf), "first", [two, push, hs, duo, f32(2 * rows, nc)],
        [tab, tot0, e_lo, e_hi, s_lo, s_hi, sea_mask, white_coef, s5, sy],
    )
    t1_parts = peers(t1_part)
    p_up, p_dn = after(t1_part, p_up, p_dn)
    p_lo, p_hi = exchange(p_up, p_dn)
    r5, t5 = call(product_kernel, "product", [sums, sums], [tab, u, p, al, u_lo, u_hi], held=(1, 2, 3), **heavy)
    (t1_own,) = after(r5, t1_part)
    t1, h1, d1_part = call(
        functools.partial(second_kernel, nf, n), "second", [two, hs, flat],
        [tab, t1_own, *t1_parts, sea_mask, white_coef, h0, h0h, r5],
    )
    d1_parts = peers(d1_part)
    half = max(1, nf // 2)
    forces = lambda first, count, h0: call(
        functools.partial(force_kernel, first), "force", [f32(9, count, rows, nc)], [tab, u, p, al, h0, p_lo, p_hi], held=(1, 2, 3), **heavy
    )[0]
    (h0_late,) = after(d1_part, h0)
    a_low = forces(0, half, h0_late)
    a_low, d1_own = lax.optimization_barrier((a_low, d1_part))
    d1_parts = [d1_own] + d1_parts
    d1, v1, d0_part, f1, b_up, b_dn = call(
        functools.partial(third_kernel, nf, n), "third", [flat, hs, f32(rows + 8, nc), flat, push, push],
        [tab, *d1_parts, sea_mask, white_coef, wind_speed, t1, h0, h0h, h1, s5, sy, r5, t5],
    )
    b_lo, b_hi = exchange(b_up, b_dn)
    (h0_late,) = after(b_up, h0)
    a_high = forces(half, nf - half, h0_late)
    (red,) = call(
        functools.partial(fourth_kernel, nf), "fourth", [f32(2 * rows + 8, nc)],
        [tab, d0_part, b_lo, b_hi, s_lo, s_hi, a_low, a_high, t5, h0, h1, v1, f1, wind_speed],
    )
    reds = peers(red)
    (late_speed,) = after(red, wind_speed)
    z, z_lo, z_hi = call(
        back_kernel, "back", [big, line, line],
        [tab, dirs, p, input_coef, al, h0, h0h, h1, v1, p_lo, p_hi, s_lo, s_hi, b_lo, b_hi, late_speed],
        [vmem(2, NL, nc), vmem(2, 2, 8, nc), vmem(rows, nc), vmem(rows, nc)], held=(2, 4), **heavy,
    )
    (red_own,) = after(z_lo, red)
    reds = [red_own] + reds
    out, grad_input, grad_white = call(
        functools.partial(out_kernel, n), "out", [f32(nf, ND, rows, nc), flat, flat],
        [tab, *reds, z, z_lo, z_hi, t0, t0h, t1, d1, sea_mask, white_coef, s_lo, s_hi],
        [vmem(2, rows, nc), vmem(2, 8, nc), vmem(2, NL, nc), vmem(2, rows, nc)] + stream, held=(1 + n,), out_hbm=(0,), **heavy,
    )
    return out, grad_input, grad_white


def solution(mesh):
    return jax.shard_map(
        shards,
        mesh=mesh,
        in_specs=(
            P("spec", None, "cells", None),
            P("cells", None),
            P("cells", None),
            P("cells", None),
            P("cells", None),
            P("cells", None),
            P("spec", None, "cells", None),
        ),
        out_specs=(P("spec", None, "cells", None), P("cells", None), P("cells", None)),
        check_vma=False,
    )
```

```python
import functools
import math

import jax
import jax.numpy as jnp
import numpy as np
from jax import lax
from jax.experimental import pallas as pl
from jax.experimental.pallas import tpu as pltpu
from jax.sharding import PartitionSpec as P

NF = 32
ND = 36
STEPS = 2

epsilon = 1e-06
energy_ref = 0.5
time_step = 0.5
courant = 0.7
ratio_step = 1.1

F32 = jnp.float32
LOG2E = math.log2(math.e)

_every = np.exp(np.arange(NF, dtype=np.float32) * np.float32(math.log(ratio_step))).astype(np.float32)
_total = _every.sum(dtype=np.float32)
HIGHEST = float(_every[-1])
MEAN_RATIO = float((_every * _every).sum(dtype=np.float32) / _total)
_weights = _every / (np.float32(ND) * _total)
_q = (_every / _every[-1]) ** 2
NTAB = 5
TABLE = np.stack([_every, 1 / _every, _weights, _q, _weights * _every], axis=1).astype(np.float32).reshape(-1)

_angle = (np.float32(2.0 * math.pi) * np.arange(ND, dtype=np.float32) / np.float32(ND)).astype(np.float32)
COS, SIN = np.cos(_angle).astype(np.float32), np.sin(_angle).astype(np.float32)
KX, KY = np.float32(courant) * np.abs(COS), np.float32(courant) * np.abs(SIN)
XP, YP = [bool(c >= 0) for c in COS], [bool(s >= 0) for s in SIN]
NL = sum(YP)
NH = ND - NL
assert YP == [True] * NL + [False] * NH and NL == NH
QUADS = [[d for d in range(ND) if (XP[d], YP[d]) == quad] for quad in ((1, 1), (0, 1), (0, 0), (1, 0))]
DIRS = np.stack([v[a:b] for a, b in ((0, NL), (NL, ND)) for v in (KX, KY, COS, SIN)]).astype(np.float32)
DIRS = np.ascontiguousarray(np.broadcast_to(DIRS[:, :, None], DIRS.shape + (128,)))
MISC = 2 * NL
MROWS = 4
NMISC = 5

MIB = 1 << 20


def coef(tab, j, nf, which):
    return tab[(lax.axis_index("spec") * nf + j) * NTAB + which]


def shift_x(x, plus):
    return pltpu.roll(x, 1 if plus else x.shape[1] - 1, 1)


def first_row(x):
    return lax.broadcasted_iota(jnp.int32, x.shape, 0) == 0


def last_row(x):
    return lax.broadcasted_iota(jnp.int32, x.shape, 0) == x.shape[0] - 1


def from_before(x, above):
    return jnp.where(first_row(x), above, pltpu.roll(x, 1, 0))


def from_after(x, below):
    return jnp.where(last_row(x), below, pltpu.roll(x, x.shape[0] - 1, 0))


def shift_y(x, plus, outside):
    return from_before(x, outside) if plus else from_after(x, outside)


def damping_of(energy, moment):
    shifted = energy + epsilon
    ratio = moment / (shifted * MEAN_RATIO)
    r2 = ratio * ratio
    steep = energy * (r2 * r2) / energy_ref
    return shifted, ratio, steep, steep * steep * ratio


def grads_of(energy, moment, white, damp_total):
    shifted, ratio, steep, damping = damping_of(energy, moment)
    grad_damp = -time_step * white * damp_total
    grad_ratio = 9.0 * grad_damp * steep * steep
    r2 = ratio * ratio
    grad_energy = grad_damp * 2.0 * steep * (r2 * r2) * ratio / energy_ref - grad_ratio * ratio / shifted
    grad_moment = grad_ratio / (shifted * MEAN_RATIO)
    return grad_energy, grad_moment, damping


def gate(q, white, damping, ocean):
    return ocean * jnp.exp2((-time_step * LOG2E) * q * (white * damping))


def rows_from(tiles, plus, outside):
    moved = [pltpu.roll(x, 1 if plus else 7, 0) for x in tiles]
    mark = first_row(tiles[0]) if plus else last_row(tiles[0])
    feed = [outside] + moved[:-1] if plus else moved[1:] + [outside]
    return [jnp.where(mark, a, b) for a, b in zip(feed, moved)]


def slab(ref, *index):
    return [ref[(*index, slice(t, t + 8))] for t in range(0, ref.shape[-2], 8)]


def by_parity(write, first, second):
    odd = lax.rem(lax.axis_index("cells"), 2)

    @pl.when(odd == 0)
    def _():
        write(first, second)

    @pl.when(odd == 1)
    def _():
        write(second, first)


class Either:
    def __init__(self, even, odd):
        self.even, self.odd, self.shape = even, odd, even.shape

    def __getitem__(self, at):
        x, y = self.even[at], self.odd[at]
        return jnp.where(jnp.full(x.shape, lax.rem(lax.axis_index("cells"), 2), jnp.int32) == 0, x, y)


def beside(first, second):
    return Either(second, first), Either(first, second)


def misc_at(r, k):
    m = r * NMISC + k
    return m // MROWS, MISC + m % MROWS


def misc_row(ref, r, k):
    j, row = misc_at(r, k)
    return ref[j, row : row + 1, :]


def halo_rows(ref, j, r):
    return ref[j, r * NL : (r + 1) * NL, :]


def fetches(hbm, ref, sems):
    return lambda j: pltpu.make_async_copy(hbm.at[j], ref.at[j], sems.at[j])


NBUF = 3


def edge_kernel(s_hbm, mask_h, coef_h, white_h, speed_h, angle_h, a_ref, b_ref, low, high, sems, fields, ints, small_sems):
    nf, _, rows, nc = s_hbm.shape

    def fetch(j):
        return (
            pltpu.make_async_copy(s_hbm.at[j, 0:NL, rows - 8 : rows, :], low.at[j], sems.at[0, j]),
            pltpu.make_async_copy(s_hbm.at[j, NL:ND, 0:8, :], high.at[j], sems.at[1, j]),
        )

    smalls = [pltpu.make_async_copy(mask_h, ints, small_sems.at[0])]
    for k, f in enumerate((coef_h, white_h, speed_h, angle_h)):
        smalls.append(pltpu.make_async_copy(f, fields.at[k], small_sems.at[1 + k]))
    for c in smalls:
        c.start()
    for j in range(nf):
        for c in fetch(j):
            c.start()
    for c in smalls:
        c.wait()

    def write(up_ref, dn_ref):
        @pl.loop(0, nf)
        def _(j):
            up_ref[j, MISC:, :] = jnp.zeros_like(up_ref[j, MISC:, :])
            dn_ref[j, MISC:, :] = jnp.zeros_like(dn_ref[j, MISC:, :])

        for side, out in ((slice(rows - 2, rows), up_ref), (slice(0, 2), dn_ref)):
            kappa = (time_step * LOG2E / HIGHEST) * (fields[0, side] * fields[2, side])
            angle = fields[3, side]
            for k, v in enumerate((kappa, jnp.cos(angle), jnp.sin(angle), ints[side].astype(F32), fields[1, side])):
                for r in range(2):
                    a, b = misc_at(r, k)
                    out[a, b : b + 1, :] = v[r : r + 1]

        @pl.loop(0, nf)
        def _(j):
            for c in fetch(j):
                c.wait()
            for r in range(2):
                for d in range(NL):
                    up_ref[j, r * NL + d : r * NL + d + 1, :] = low[j, d, 6 + r : 7 + r, :]
                    dn_ref[j, r * NL + d : r * NL + d + 1, :] = high[j, d, r : r + 1, :]

    by_parity(write, a_ref, b_ref)


def start_kernel(tab, s_ref, mask, t0_ref, sums):
    nf = s_ref.shape[0]
    rows, nc = mask.shape
    sums[...] = jnp.zeros_like(sums)

    @pl.loop(0, nf)
    def _(j):
        rj, w, wf = [coef(tab, j, nf, k) for k in (1, 2, 4)]
        for t in range(0, rows, 8):
            acc = [None] * 5

            def add(k, v):
                acc[k] = v if acc[k] is None else acc[k] + v

            for d in range(ND):
                x = s_ref[j, d, t : t + 8, :]
                add(0, x)
                add(1 if XP[d] else 2, float(KX[d]) * x)
                add(3 if YP[d] else 4, float(KY[d]) * x)
            for k in range(5):
                sums[0, k, t : t + 8, :] += (w if k == 0 else w * rj) * acc[k]
                sums[1, k, t : t + 8, :] += (wf if k == 0 else wf * rj) * acc[k]

    ocean = mask[...].astype(F32)
    t0_ref[2 * rows :, :] = jnp.zeros_like(t0_ref[2 * rows :, :])
    for e in range(2):
        total, xp, xm, yp, ym = [ocean * sums[e, k] for k in range(5)]
        t0_ref[e * rows : (e + 1) * rows, :] = total + (
            shift_x(xp, True) + shift_x(xm, False) + from_before(yp, 0.0) + from_after(ym, 0.0) - (xp + xm + yp + ym)
        )
        t0_ref[2 * rows + e : 2 * rows + e + 1, :] = yp[rows - 1 : rows]
        t0_ref[2 * rows + 2 + e : 2 * rows + 3 + e, :] = ym[0:1]


def wind_kernel(tab, lam_ref, coef_in, speed, angle, p_ref, al_ref, a_ref, b_ref, expo):
    nf = lam_ref.shape[0]
    rows, nc = angle.shape
    for ref in (a_ref, b_ref):
        ref[:, MISC:, :] = jnp.zeros_like(ref[:, MISC:, :])
    kappa = (time_step * LOG2E / HIGHEST) * (coef_in[...] * speed[...])
    ca, sa = jnp.cos(angle[...]), jnp.sin(angle[...])
    for d in range(ND):
        align = jnp.maximum(float(COS[d]) * ca + float(SIN[d]) * sa, 0.0)
        al = align * align
        al_ref[d] = al
        expo[d] = kappa * al

    def write(up_ref, dn_ref):
        @pl.loop(0, nf)
        def _(j):
            fr = coef(tab, j, nf, 0)
            for d in range(ND):
                p = jnp.exp2(fr * expo[d]) * lam_ref[j, d]
                p_ref[j, d] = p
                for r in range(2):
                    at = slice(r * NL + d % NL, r * NL + d % NL + 1)
                    if d < NL:
                        dn_ref[j, at, :] = p[r : r + 1]
                    else:
                        up_ref[j, at, :] = p[rows - 2 + r : rows - 1 + r]

    by_parity(write, a_ref, b_ref)


def halo_growth(fr, dirs, half, misc, r):
    cosd, sind = dirs[4 * half + 2][:, 0:1], dirs[4 * half + 3][:, 0:1]
    align = jnp.maximum(cosd * misc_row(misc, r, 1) + sind * misc_row(misc, r, 2), 0.0)
    return jnp.exp2(fr * (misc_row(misc, r, 0) * (align * align)))


def halo_adv(rj, dirs, half, near, far, transpose):
    kx, ky, cosd = [dirs[4 * half + k][:, 0:1] for k in range(3)]
    before, after = shift_x(near, not transpose), shift_x(near, transpose)
    moved = jnp.where(cosd >= 0, before, after)
    return near + rj * (kx * (moved - near) + ky * (far - near))


def grow(outer, tab, j, s_ref, ocean, coef_in, speed, al_ref, u_ref, sum_ref, work, edge, before):
    nf, _, rows, nc = s_ref.shape
    fr, rj = coef(tab, j, nf, 0), coef(tab, j, nf, 1)
    work[...] = (fr * (time_step * LOG2E / HIGHEST)) * (coef_in[...] * speed[...])
    for t in range(0, rows, 8):
        at8 = slice(t, t + 8)
        o = rj * ocean[at8]
        seen = set()
        for quad in QUADS:
            plus = YP[quad[0]]
            end = t == 0 if plus else t + 8 == rows
            if end != outer:
                continue
            n = t - 1 if plus else t + 8
            acc = [None] * 3
            for d in quad:
                kx, ky = float(KX[d]), float(KY[d])
                x = o * s_ref[j, d, at8, :]
                if outer:
                    row = edge[0, d : d + 1, :] if plus else edge[1, d - NL : d - NL + 1, :]
                else:
                    row = (rj * ocean[n : n + 1]) * s_ref[j, d, n : n + 1, :]
                y = shift_y(x, plus, row)
                u = jnp.exp2(work[at8] * al_ref[d, at8]) * ((fr - (kx + ky)) * x + kx * shift_x(x, XP[d]) + ky * y)
                u_ref[j, d, at8, :] = u
                for k, v in enumerate((u, kx * u, ky * u)):
                    acc[k] = v if acc[k] is None else acc[k] + v
            for k, key in enumerate((0, 1 if XP[quad[0]] else 2, 3 if plus else 4)):
                at = (key, j, at8)
                if key in seen:
                    sum_ref[at] += acc[k]
                else:
                    sum_ref[at] = acc[k] if before is None else before[at] + acc[k]
                seen.add(key)
        for key in range(5):
            if key not in seen:
                at = (key, j, at8)
                sum_ref[at] = jnp.zeros((8, nc), F32) if before is None else before[at]


def inner_kernel(tab, s_ref, mask, coef_in, speed, al_ref, u_ref, sum_ref, work):
    ocean = mask[...].astype(F32)

    @pl.loop(0, s_ref.shape[0])
    def _(j):
        grow(False, tab, j, s_ref, ocean, coef_in, speed, al_ref, u_ref, sum_ref, work, None, None)


def grown_kernel(tab, dirs, s_ref, mask, coef_in, speed, al_ref, s_first, s_second, u_in, before, u_ref, sum_ref, ul_ref, uh_ref, sy_ref, edge, work):
    nf, _, rows, nc = s_ref.shape
    lo, hi = beside(s_first, s_second)
    ocean = mask[...].astype(F32)

    @pl.loop(0, nf)
    def _(j):
        fr, rj = coef(tab, j, nf, 0), coef(tab, j, nf, 1)
        for half, (blk, near, far, out) in enumerate(((lo, 1, 0, ul_ref), (hi, 0, 1, uh_ref))):
            x = [misc_row(blk, r, 3) * halo_rows(blk, j, r) for r in range(2)]
            edge[half] = rj * x[near]
            u = halo_growth(fr, dirs, half, blk, near) * halo_adv(rj, dirs, half, x[near], x[far], False)
            out[j] = u
            sy_ref[half, pl.ds(j, 1), :] = jnp.sum(dirs[4 * half + 1][:, 0:1] * u, axis=0, keepdims=True)
        grow(True, tab, j, s_ref, ocean, coef_in, speed, al_ref, u_ref, sum_ref, work, edge, before)
        for t in range(0, rows, 8):
            a, b, c, d, e = [sum_ref[k, j, t : t + 8, :] for k in range(5)]
            sum_ref[0, j, t : t + 8, :] = a - rj * (b + c + d + e)


def product_kernel(tab, u_ref, p_ref, al_ref, ul_ref, uh_ref, r_ref, t_ref):
    nf, _, rows, nc = u_ref.shape

    @pl.loop(0, nf)
    def _(j):
        rj = coef(tab, j, nf, 1)
        for t in range(0, rows, 8):
            seen = set()
            for quad in QUADS:
                acc = [None] * 6
                for d in quad:
                    kx, ky = float(KX[d]), float(KY[d])
                    u, p, al = u_ref[j, d, t : t + 8, :], p_ref[j, d, t : t + 8, :], al_ref[d, t : t + 8, :]
                    if YP[d]:
                        row = ul_ref[j, d : d + 1, :] if t == 0 else u_ref[j, d, t - 1 : t, :]
                        y = jnp.where(first_row(u), row, pltpu.roll(u, 1, 0))
                    else:
                        row = uh_ref[j, d - NL : d - NL + 1, :] if t + 8 == rows else u_ref[j, d, t + 8 : t + 9, :]
                        y = jnp.where(last_row(u), row, pltpu.roll(u, 7, 0))
                    cu = (1.0 - rj * (kx + ky)) * (p * u)
                    px, py = kx * (p * shift_x(u, XP[d])), ky * (p * y)
                    for k, v in enumerate((cu, px, py, al * cu, al * px, al * py)):
                        acc[k] = v if acc[k] is None else acc[k] + v
                xk, yk = (1 if XP[quad[0]] else 2), (3 if YP[quad[0]] else 4)
                for k, ref in enumerate((r_ref, t_ref)):
                    for key, v in zip((0, xk, yk), acc[3 * k : 3 * k + 3]):
                        at = (key, j, slice(t, t + 8))
                        ref[at] = ref[at] + v if (k, key) in seen else v
                        seen.add((k, key))


def total_kernel(rows, *refs):
    parts, (tot, first, second) = refs[:-3], refs[-3:]
    total = parts[0][...]
    for part in parts[1:]:
        total = total + part[...]
    tot[...] = total

    def write(up, dn):
        up[...] = jnp.zeros_like(up)
        dn[...] = jnp.zeros_like(dn)
        for k, row in enumerate((rows - 1, 2 * rows - 1, 2 * rows, 2 * rows + 1)):
            up[k : k + 1, :] = total[row : row + 1]
        for k, row in enumerate((0, rows, 2 * rows + 2, 2 * rows + 3)):
            dn[k : k + 1, :] = total[row : row + 1]

    by_parity(write, first, second)


def advected_sum(rj, h, above, below, s):
    return h * s[0], rj * (
        shift_x(h * s[1], True) + shift_x(h * s[2], False) + from_before(h * s[3], above) + from_after(h * s[4], below)
    )


def first_kernel(nf, tab, tot, e_first, e_second, s_first, s_second, mask, white, sum_ref, sy_ref, t0_ref, t0h_ref, h0_ref, h0h_ref, t1_ref):
    rows, nc = mask.shape
    lo, hi = beside(e_first, e_second)
    lo_misc, hi_misc = beside(s_first, s_second)
    ocean = mask[...].astype(F32)
    row = lax.broadcasted_iota(jnp.int32, (rows, nc), 0)
    total = tot[...]
    field = []
    halo = []
    t0h_ref[...] = jnp.zeros_like(t0h_ref)
    for k in range(2):
        v = total[k * rows : (k + 1) * rows]
        v = v + jnp.where(row == 0, lo[2 + k : 3 + k, :], 0.0) + jnp.where(row == rows - 1, hi[2 + k : 3 + k, :], 0.0)
        field.append(ocean * v)
        t0_ref[k] = field[k]
        above = misc_row(lo_misc, 1, 3) * (lo[k : k + 1, :] + total[2 * rows + 2 + k : 2 * rows + 3 + k])
        below = misc_row(hi_misc, 0, 3) * (hi[k : k + 1, :] + total[2 * rows + k : 2 * rows + 1 + k])
        halo.append((above, below))
        t0h_ref[k : k + 1, :] = above
        t0h_ref[2 + k : 3 + k, :] = below
    damping = damping_of(*field)[3]
    damp_lo = damping_of(halo[0][0], halo[1][0])[3]
    damp_hi = damping_of(halo[0][1], halo[1][1])[3]
    energy, moment = jnp.zeros((rows, nc), F32), jnp.zeros((rows, nc), F32)
    for j in range(nf):
        rj, w, q, wf = [coef(tab, j, nf, k) for k in (1, 2, 3, 4)]
        h = gate(q, white[...], damping, ocean)
        h_lo = gate(q, misc_row(lo_misc, 1, 4), damp_lo, misc_row(lo_misc, 1, 3))
        h_hi = gate(q, misc_row(hi_misc, 0, 4), damp_hi, misc_row(hi_misc, 0, 3))
        h0_ref[j] = h
        h0h_ref[0, j : j + 1, :] = h_lo
        h0h_ref[1, j : j + 1, :] = h_hi
        centre, around = advected_sum(
            rj, h, h_lo * sy_ref[0, j : j + 1, :], h_hi * sy_ref[1, j : j + 1, :], [sum_ref[k, j] for k in range(5)]
        )
        adv = centre + around
        energy, moment = energy + w * adv, moment + wf * adv
    t1_ref[0:rows, :] = energy
    t1_ref[rows : 2 * rows, :] = moment


def gathered(rj, h, h_lo, h_hi, r):
    return h * r[0] + rj * (
        shift_x(h, True) * r[1] + shift_x(h, False) * r[2] + from_before(h, h_lo) * r[3] + from_after(h, h_hi) * r[4]
    )


def second_kernel(nf, n, tab, *refs):
    parts, (mask, white, h0_ref, h0h_ref, r_ref, t1_ref, h1_ref, d1_ref) = refs[:n], refs[n:]
    rows, nc = mask.shape
    ocean = mask[...].astype(F32)
    total = parts[0][...]
    for part in parts[1:]:
        total = total + part[...]
    energy, moment = ocean * total[:rows], ocean * total[rows:]
    t1_ref[0] = energy
    t1_ref[1] = moment
    damping = damping_of(energy, moment)[3]
    acc = jnp.zeros((rows, nc), F32)
    for j in range(nf):
        rj, q = coef(tab, j, nf, 1), coef(tab, j, nf, 3)
        h1 = gate(q, white[...], damping, ocean)
        h1_ref[j] = h1
        part = gathered(rj, h0_ref[j], h0h_ref[0, j : j + 1, :], h0h_ref[1, j : j + 1, :], [r_ref[k, j] for k in range(5)])
        acc = acc + q * (h1 * part)
    d1_ref[...] = acc


def third_kernel(nf, n, tab, *refs):
    parts = refs[:n]
    mask, white, t1, h0_ref, h0h_ref, h1_ref, sum_ref, sy_ref, r_ref = refs[n : n + 9]
    d1_ref, v1_ref, d0_ref, first, second = refs[n + 9 :]
    rows, nc = mask.shape
    ocean = mask[...].astype(F32)
    damp = parts[0][...]
    for part in parts[1:]:
        damp = damp + part[...]
    d1_ref[...] = damp
    grad_e, grad_m, _ = grads_of(t1[0], t1[1], white[...], damp)
    acc = jnp.zeros((rows, nc), F32)
    push_lo, push_hi = jnp.zeros((1, nc), F32), jnp.zeros((1, nc), F32)
    for j in range(nf):
        fr, rj, w, q = [coef(tab, j, nf, k) for k in range(4)]
        h0, h1 = h0_ref[j], h1_ref[j]
        h_lo, h_hi = h0h_ref[0, j : j + 1, :], h0h_ref[1, j : j + 1, :]
        v1 = ocean * (w * (grad_e + fr * grad_m))
        v1_ref[j] = v1
        s, r = [sum_ref[k, j] for k in range(5)], [r_ref[k, j] for k in range(5)]
        inner = (
            shift_x(h1 * r[1], False)
            + shift_x(h1 * r[2], True)
            + from_after(h1 * r[3], 0.0)
            + from_before(h1 * r[4], 0.0)
            + s[1] * shift_x(v1, False)
            + s[2] * shift_x(v1, True)
            + s[3] * from_after(v1, 0.0)
            + s[4] * from_before(v1, 0.0)
        )
        acc = acc + q * (h0 * (h1 * r[0] + v1 * s[0] + rj * inner))
        push_lo = push_lo + (q * rj) * (h_lo * (h1[0:1] * r[3][0:1] + v1[0:1] * sy_ref[0, j : j + 1, :]))
        e = rows - 1
        push_hi = push_hi + (q * rj) * (
            h_hi * (h1[e : e + 1] * r[4][e : e + 1] + v1[e : e + 1] * sy_ref[1, j : j + 1, :])
        )
    def write(up, dn):
        for k, v in enumerate((t1[0], t1[1], damp)):
            up[2 * k : 2 * k + 2, :] = v[rows - 2 : rows]
            dn[2 * k : 2 * k + 2, :] = v[0:2]
        up[6:7, :] = acc[rows - 1 : rows]
        up[7:8, :] = push_hi
        dn[6:7, :] = acc[0:1]
        dn[7:8, :] = push_lo

    by_parity(write, first, second)
    d0_ref[0:rows, :] = acc
    d0_ref[rows:, :] = jnp.zeros_like(d0_ref[rows:, :])
    d0_ref[rows : rows + 1, :] = push_lo
    d0_ref[rows + 1 : rows + 2, :] = push_hi


def fourth_kernel(nf, tab, part, b_first, b_second, s_first, s_second, a_low, a_high, t_ref, h0_ref, h1_ref, v1_ref, f1_ref, speed, out):
    rows, nc = speed.shape
    lo, hi = beside(b_first, b_second)
    lo_misc, hi_misc = beside(s_first, s_second)
    row = lax.broadcasted_iota(jnp.int32, (rows, nc), 0)
    v = part[0:rows, :]
    v = v + jnp.where(row == 0, lo[7:8, :], 0.0) + jnp.where(row == rows - 1, hi[7:8, :], 0.0)
    out[0:rows, :] = v
    out[rows : rows + 8, :] = jnp.zeros((8, nc), F32)
    out[rows : rows + 1, :] = part[rows : rows + 1, :] + lo[6:7, :]
    out[rows + 1 : rows + 2, :] = part[rows + 1 : rows + 2, :] + hi[6:7, :]
    outside = []
    for got, misc, r in ((lo, lo_misc, 1), (hi, hi_misc, 0)):
        energy, moment, damp = [got[2 * k + r : 2 * k + r + 1, :] for k in range(3)]
        white = misc_row(misc, r, 4)
        grad_e, grad_m, damping = grads_of(energy, moment, white, damp)
        outside.append((white, damping, misc_row(misc, r, 3), grad_e, grad_m))
    force = jnp.zeros((rows, nc), F32)
    low = a_low.shape[1]
    for j in range(nf):
        fr, w, q = [coef(tab, j, nf, k) for k in (0, 2, 3)]
        a = [a_low[k, j] if j < low else a_high[k, j - low] for k in range(9)]
        h1, v1 = h1_ref[j], v1_ref[j]
        edges = [(gate(q, white, damping, o), o * (w * (ge + fr * gm))) for white, damping, o, ge, gm in outside]
        force = force + (fr * h0_ref[j]) * (h1 * t_ref[0, j]) + v1 * a[0]
        for x, k, b in ((v1, 0, 1), (h1, 4, 0)):
            force = force + (
                shift_x(x, False) * a[k + 1]
                + shift_x(x, True) * a[k + 2]
                + from_after(x, edges[1][b]) * a[k + 3]
                + from_before(x, edges[0][b]) * a[k + 4]
            )
    out[rows + 8 :, :] = (speed[...] / HIGHEST) * (force + f1_ref[...])


def force_kernel(first, tab, u_ref, p_ref, al_ref, h0_ref, p_first, p_second, *refs):
    nf, _, rows, nc = u_ref.shape
    a_ref = refs[-2] if len(refs) > 1 else refs[0]
    pl_ref, ph_ref = beside(p_first, p_second)

    @pl.loop(0, a_ref.shape[1])
    def _(i):
        j = first + i
        fr, rj = coef(tab, j, nf, 0), coef(tab, j, nf, 1)
        for t in range(0, rows, 8):
            seen = set()
            for quad in QUADS:
                acc = [None] * 5
                for d in quad:
                    kx, ky = float(KX[d]), float(KY[d])
                    u, p, al = u_ref[j, d, t : t + 8, :], p_ref[j, d, t : t + 8, :], al_ref[d, t : t + 8, :]
                    if YP[d]:
                        row = ph_ref[j, d : d + 1, :] if t + 8 == rows else p_ref[j, d, t + 8 : t + 9, :]
                        y = from_after(p, row)
                    else:
                        row = pl_ref[j, d : d + 1, :] if t == 0 else p_ref[j, d, t - 1 : t, :]
                        y = from_before(p, row)
                    au = al * u
                    xau, yau = kx * au, ky * au
                    for k, v in enumerate(((1.0 - rj * (kx + ky)) * au, xau, yau, xau * shift_x(p, not XP[d]), yau * y)):
                        acc[k] = v if acc[k] is None else acc[k] + v
                xk, yk = (1 if XP[quad[0]] else 2), (3 if YP[quad[0]] else 4)
                for key, v in zip((0, xk, yk, 4 + xk, 4 + yk), acc):
                    at = (key, i, slice(t, t + 8))
                    a_ref[at] = a_ref[at] + v if key in seen else v
                    seen.add(key)
        h0 = h0_ref[j]
        for k in range(9):
            a_ref[k, i] = (fr * h0 if k == 0 else h0) * a_ref[k, i]
    if len(refs) > 1:
        h0h_ref, h1_ref, t_ref, _, f1_ref = refs
        force = jnp.zeros((rows, nc), F32)
        for j in range(nf):
            fr, rj = coef(tab, j, nf, 0), coef(tab, j, nf, 1)
            edges = [h0h_ref[k, j : j + 1, :] for k in range(2)]
            part = gathered(rj, h0_ref[j], edges[0], edges[1], [t_ref[k, j] for k in range(5)])
            force = force + fr * (h1_ref[j] * part)
        f1_ref[...] = force


def back_kernel(tab, dirs, p_ref, coef_in, al_ref, h0_ref, h0h_ref, h1_ref, v1_ref, p_first, p_second, s_first, s_second, b_first, b_second, speed, z_ref, zl_ref, zh_ref, edge, halo, scaled, work):
    nf, _, rows, nc = p_ref.shape
    pl_ref, ph_ref = beside(p_first, p_second)
    lo_misc, hi_misc = beside(s_first, s_second)
    lo, hi = beside(b_first, b_second)
    sides = ((0, ph_ref, hi_misc, hi, 0, 1, 1, zh_ref), (1, pl_ref, lo_misc, lo, 1, 0, 0, zl_ref))
    for side, (_, _, misc, got, *_) in enumerate(sides):
        for r in range(2):
            energy, moment, damp = [got[2 * k + r : 2 * k + r + 1, :] for k in range(3)]
            white = misc_row(misc, r, 4)
            grad_e, grad_m, damping = grads_of(energy, moment, white, damp)
            for k, v in enumerate((grad_e, grad_m, white * damping)):
                halo[side, r, k : k + 1, :] = v

    @pl.loop(0, nf)
    def _(j):
        fr, rj = coef(tab, j, nf, 0), coef(tab, j, nf, 1)
        w, q = coef(tab, j, nf, 2), coef(tab, j, nf, 3)
        for side, (half, blk, misc, _, near, far, which, out) in enumerate(sides):
            x = []
            for r in range(2):
                ocean = misc_row(misc, r, 3)
                h = gate(q, halo[side, r, 2:3, :], 1.0, ocean)
                v = ocean * (w * (halo[side, r, 0:1, :] + fr * halo[side, r, 1:2, :]))
                x.append(halo_rows(blk, j, r) * h + v)
            edge[side] = x[near]
            moved = halo_adv(rj, dirs, half, x[near], x[far], True) * halo_growth(fr, dirs, half, misc, near)
            out[j] = moved * h0h_ref[which, pl.ds(j, 1), :]
        tiles = range(rows // 8)
        at8 = [slice(8 * t, 8 * t + 8) for t in tiles]
        work[...] = (fr * (time_step * LOG2E / HIGHEST)) * (coef_in[...] * speed[...])
        for t in tiles:
            scaled[at8[t]] = rj * h0_ref[j, at8[t]]
        for d in range(ND):
            kx, ky = float(KX[d]), float(KY[d])
            x = [p_ref[j, d, at8[t]] * h1_ref[j, at8[t]] + v1_ref[j, at8[t]] for t in tiles]
            row = edge[0, d : d + 1, :] if YP[d] else edge[1, d - NL : d - NL + 1, :]
            y = rows_from(x, not YP[d], row)
            for t in tiles:
                back = (fr - (kx + ky)) * x[t] + kx * shift_x(x[t], not XP[d]) + ky * y[t]
                z_ref[j, d, at8[t]] = back * (jnp.exp2(work[at8[t]] * al_ref[d, at8[t]]) * scaled[at8[t]])


def out_kernel(n, tab, *refs):
    parts, refs = refs[:n], refs[n:]
    z_ref, zl_ref, zh_ref, t0, t0h, t1, d1, mask, white, s_first, s_second = refs[:11]
    lo_misc, hi_misc = beside(s_first, s_second)
    out_hbm, gi_ref, gw_ref, own, halo, edge, work, buf, sems = refs[11:]
    nf, _, rows, nc = z_ref.shape
    ocean = mask[...].astype(F32)
    total = parts[0][...]
    for part in parts[1:]:
        total = total + part[...]
    damp = total[0:rows]
    gi_ref[...] = time_step * total[rows + 8 :]
    grad_e, grad_m, damping = grads_of(t0[0], t0[1], white[...], damp)
    own[0] = grad_e
    own[1] = grad_m
    gw_ref[...] = -time_step * (damping * damp + damping_of(t1[0], t1[1])[3] * d1[...])
    above, below = total[rows : rows + 1], total[rows + 1 : rows + 2]
    sides = ((hi_misc, 0, 2, below, zh_ref), (lo_misc, 1, 0, above, zl_ref))
    for side, (misc, r, k, damp, _) in enumerate(sides):
        e, m, _ = grads_of(t0h[k : k + 1, :], t0h[k + 1 : k + 2, :], misc_row(misc, r, 4), damp)
        halo[side, 0:1, :] = e
        halo[side, 1:2, :] = m

    def put(j, half):
        part = slice(0, NL) if half == 0 else slice(NL, ND)
        return pltpu.make_async_copy(buf.at[j % NBUF, part], out_hbm.at[j, part], sems.at[j % NBUF, half])

    @pl.loop(0, nf)
    def _(j):
        slot = j % NBUF
        fr, rj, w = [coef(tab, j, nf, k) for k in range(3)]
        for side, (misc, r, _, _, z) in enumerate(sides):
            edge[side] = z[j] + misc_row(misc, r, 3) * (w * (halo[side, 0:1, :] + fr * halo[side, 1:2, :]))
        tiles = range(rows // 8)
        o = [ocean[8 * t : 8 * t + 8] for t in tiles]
        v = [o[t] * (w * (own[0, 8 * t : 8 * t + 8] + fr * own[1, 8 * t : 8 * t + 8])) for t in tiles]
        for t in tiles:
            work[0, 8 * t : 8 * t + 8] = v[t]
            work[1, 8 * t : 8 * t + 8] = rj * o[t]

        @pl.when(j >= NBUF)
        def _():
            for half in range(2):
                put(j - NBUF, half).wait()

        for d in range(ND):
            kx, ky = float(KX[d]), float(KY[d])
            x = [z + work[0, 8 * t : 8 * t + 8] for t, z in enumerate(slab(z_ref, j, d))]
            row = edge[0, d : d + 1, :] if YP[d] else edge[1, d - NL : d - NL + 1, :]
            y = rows_from(x, not YP[d], row)
            for t in tiles:
                back = (fr - (kx + ky)) * x[t] + kx * shift_x(x[t], not XP[d]) + ky * y[t]
                buf[slot, d, 8 * t : 8 * t + 8, :] = work[1, 8 * t : 8 * t + 8] * back
            if d == NL - 1:
                put(j, 0).start()
        put(j, 1).start()

    for j in range(max(0, nf - NBUF), nf):
        for half in range(2):
            put(j, half).wait()


VMEM = pl.BlockSpec(memory_space=pltpu.VMEM)
SMEM = pl.BlockSpec(memory_space=pltpu.SMEM)
HBM = pl.BlockSpec(memory_space=pltpu.HBM)


def f32(*shape):
    return jax.ShapeDtypeStruct(shape, F32)


def vmem(*shape):
    return pltpu.VMEM(shape, F32)


def call(kernel, name, outs, args, scratch=(), hbm=(), held=(), out_hbm=(), limit=6, alias=None):
    put = {**dict.fromkeys(hbm, pltpu.HBM), **dict.fromkeys(held, pltpu.VMEM)}
    args = [pltpu.with_memory_space_constraint(a, put[k]) if k in put else a for k, a in enumerate(args)]
    return pl.pallas_call(
        kernel,
        name=name,
        out_shape=outs,
        in_specs=[HBM if k in hbm else SMEM if a.ndim == 1 else VMEM for k, a in enumerate(args)],
        out_specs=[HBM if k in out_hbm else VMEM for k in range(len(outs))],
        scratch_shapes=list(scratch),
        input_output_aliases=alias or {},
        compiler_params=pltpu.CompilerParams(vmem_limit_bytes=limit * MIB),
        cost_estimate=pl.CostEstimate(flops=1, bytes_accessed=1, transcendentals=0),
    )(*args)


def peers(x):
    n = lax.axis_size("spec")
    if n & (n - 1) == 0:
        return [lax.ppermute(x, "spec", [(i, i ^ k) for i in range(n)]) for k in range(1, n)]
    return [lax.ppermute(x, "spec", [(i, (i + k) % n) for i in range(n)]) for k in range(1, n)]


def exchange(first, second):
    n = lax.axis_size("cells")
    swaps = [[(i, i + 1) for i in range(odd, n - 1, 2)] for odd in range(2)]
    return [lax.ppermute(x, "cells", pairs + [(b, a) for a, b in pairs]) for x, pairs in zip((first, second), swaps)]


def after(first, *later):
    return lax.optimization_barrier((first, *later))[1:]


def shards(spectrum_start, input_coef, white_coef, wind_speed, wind_angle, sea_mask, cotangent):
    nf, _, rows, nc = spectrum_start.shape
    n = lax.axis_size("spec")
    tab, dirs = jnp.asarray(TABLE), jnp.asarray(DIRS)
    big = vmem(nf, ND, rows, nc)
    band = f32(nf, MISC + MROWS, nc)
    line, duo, hs, sums = f32(nf, NL, nc), f32(2, nf, nc), f32(nf, rows, nc), f32(5, nf, rows, nc)
    flat, two, push = f32(rows, nc), f32(2, rows, nc), f32(8, nc)
    stream = [vmem(NBUF, ND, rows, nc), pltpu.SemaphoreType.DMA((NBUF, 2))]
    heavy = dict(limit=8)

    s_up, s_dn = call(
        edge_kernel, "edge", [band, band], [spectrum_start, sea_mask, input_coef, white_coef, wind_speed, wind_angle],
        [
            vmem(nf, NL, 8, nc), vmem(nf, NL, 8, nc), pltpu.SemaphoreType.DMA((2, nf)), vmem(4, rows, nc),
            pltpu.VMEM((rows, nc), jnp.int32), pltpu.SemaphoreType.DMA((5,)),
        ],
        hbm=range(6), **heavy,
    )
    s_lo, s_hi = exchange(s_up, s_dn)
    (mask,) = after(s_up, sea_mask)
    (t0_part,) = call(
        start_kernel, "start", [f32(2 * rows + 8, nc)], [tab, spectrum_start, mask], [vmem(2, 5, rows, nc)], held=(1,), **heavy
    )
    t0_parts = peers(t0_part)
    (speed,) = after(t0_part, wind_speed)
    p, al, p_up, p_dn = call(
        wind_kernel, "wind", [big, vmem(ND, rows, nc), band, band], [tab, cotangent, input_coef, speed, wind_angle],
        [vmem(ND, rows, nc)], held=(1,), **heavy,
    )
    u_inner, s5_inner = call(
        inner_kernel, "inner", [big, sums], [tab, spectrum_start, sea_mask, input_coef, wind_speed, al], [vmem(rows, nc)],
        held=(1, 5), **heavy,
    )
    (t0_own,) = after(s5_inner, t0_part)
    tot0, e_up, e_dn = call(functools.partial(total_kernel, rows), "total", [f32(2 * rows + 8, nc), push, push], [t0_own, *t0_parts])
    e_lo, e_hi = exchange(e_up, e_dn)
    (mask,) = after(tot0, sea_mask)
    u, s5, u_lo, u_hi, sy = call(
        grown_kernel, "grown", [big, sums, line, line, duo], [tab, dirs, spectrum_start, mask, input_coef, wind_speed, al, s_lo, s_hi, u_inner, s5_inner],
        [vmem(2, NL, nc), vmem(rows, nc)], held=(2, 6, 9), alias={9: 0}, **heavy,
    )
    t0, t0h, h0, h0h, t1_part = call(
        functools.partial(first_kernel, nf), "first", [two, push, hs, duo, f32(2 * rows, nc)],
        [tab, tot0, e_lo, e_hi, s_lo, s_hi, sea_mask, white_coef, s5, sy],
    )
    t1_parts = peers(t1_part)
    p_up, p_dn = after(t1_part, p_up, p_dn)
    p_lo, p_hi = exchange(p_up, p_dn)
    r5, t5 = call(product_kernel, "product", [sums, sums], [tab, u, p, al, u_lo, u_hi], held=(1, 2, 3), **heavy)
    (t1_own,) = after(r5, t1_part)
    t1, h1, d1_part = call(
        functools.partial(second_kernel, nf, n), "second", [two, hs, flat],
        [tab, t1_own, *t1_parts, sea_mask, white_coef, h0, h0h, r5],
    )
    d1_parts = peers(d1_part)
    half = max(1, nf // 2)
    forces = lambda first, count, outs, h0, *more: call(
        functools.partial(force_kernel, first), "force", [f32(9, count, rows, nc), *outs], [tab, u, p, al, h0, p_lo, p_hi, *more],
        held=(1, 2, 3), **heavy
    )
    (h0_late,) = after(d1_part, h0)
    (a_low,) = forces(0, half, [], h0_late)
    a_low, d1_own = lax.optimization_barrier((a_low, d1_part))
    d1_parts = [d1_own] + d1_parts
    d1, v1, d0_part, b_up, b_dn = call(
        functools.partial(third_kernel, nf, n), "third", [flat, hs, f32(rows + 8, nc), push, push],
        [tab, *d1_parts, sea_mask, white_coef, t1, h0, h0h, h1, s5, sy, r5],
    )
    b_lo, b_hi = exchange(b_up, b_dn)
    (h0_late,) = after(b_up, h0)
    a_high, f1 = forces(half, nf - half, [flat], h0_late, h0h, h1, t5)
    (red,) = call(
        functools.partial(fourth_kernel, nf), "fourth", [f32(2 * rows + 8, nc)],
        [tab, d0_part, b_lo, b_hi, s_lo, s_hi, a_low, a_high, t5, h0, h1, v1, f1, wind_speed],
    )
    reds = peers(red)
    (late_speed,) = after(red, wind_speed)
    z, z_lo, z_hi = call(
        back_kernel, "back", [big, line, line],
        [tab, dirs, p, input_coef, al, h0, h0h, h1, v1, p_lo, p_hi, s_lo, s_hi, b_lo, b_hi, late_speed],
        [vmem(2, NL, nc), vmem(2, 2, 8, nc), vmem(rows, nc), vmem(rows, nc)], held=(2, 4), **heavy,
    )
    (red_own,) = after(z_lo, red)
    reds = [red_own] + reds
    out, grad_input, grad_white = call(
        functools.partial(out_kernel, n), "out", [f32(nf, ND, rows, nc), flat, flat],
        [tab, *reds, z, z_lo, z_hi, t0, t0h, t1, d1, sea_mask, white_coef, s_lo, s_hi],
        [vmem(2, rows, nc), vmem(2, 8, nc), vmem(2, NL, nc), vmem(2, rows, nc)] + stream, held=(1 + n,), out_hbm=(0,), **heavy,
    )
    return out, grad_input, grad_white


def solution(mesh):
    return jax.shard_map(
        shards,
        mesh=mesh,
        in_specs=(
            P("spec", None, "cells", None),
            P("cells", None),
            P("cells", None),
            P("cells", None),
            P("cells", None),
            P("cells", None),
            P("spec", None, "cells", None),
        ),
        out_specs=(P("spec", None, "cells", None), P("cells", None), P("cells", None)),
        check_vma=False,
    )
```

```python
import functools
import math

import jax
import jax.numpy as jnp
import numpy as np
from jax import lax
from jax.experimental import pallas as pl
from jax.experimental.pallas import tpu as pltpu
from jax.sharding import PartitionSpec as P

NF = 32
ND = 36
STEPS = 2

epsilon = 1e-06
energy_ref = 0.5
time_step = 0.5
courant = 0.7
ratio_step = 1.1

F32 = jnp.float32
LOG2E = math.log2(math.e)

_every = np.exp(np.arange(NF, dtype=np.float32) * np.float32(math.log(ratio_step))).astype(np.float32)
_total = _every.sum(dtype=np.float32)
HIGHEST = float(_every[-1])
MEAN_RATIO = float((_every * _every).sum(dtype=np.float32) / _total)
_weights = _every / (np.float32(ND) * _total)
_q = (_every / _every[-1]) ** 2
NTAB = 5
TABLE = np.stack([_every, 1 / _every, _weights, _q, _weights * _every], axis=1).astype(np.float32).reshape(-1)

_angle = (np.float32(2.0 * math.pi) * np.arange(ND, dtype=np.float32) / np.float32(ND)).astype(np.float32)
COS, SIN = np.cos(_angle).astype(np.float32), np.sin(_angle).astype(np.float32)
KX, KY = np.float32(courant) * np.abs(COS), np.float32(courant) * np.abs(SIN)
XP, YP = [bool(c >= 0) for c in COS], [bool(s >= 0) for s in SIN]
NL = sum(YP)
NH = ND - NL
assert YP == [True] * NL + [False] * NH and NL == NH
QUADS = [[d for d in range(ND) if (XP[d], YP[d]) == quad] for quad in ((1, 1), (0, 1), (0, 0), (1, 0))]
DIRS = np.stack([v[a:b] for a, b in ((0, NL), (NL, ND)) for v in (KX, KY, COS, SIN)]).astype(np.float32)
DIRS = np.ascontiguousarray(np.broadcast_to(DIRS[:, :, None], DIRS.shape + (128,)))
MISC = 2 * NL
MROWS = 4
NMISC = 5

MIB = 1 << 20


def coef(tab, j, nf, which):
    return tab[(lax.axis_index("spec") * nf + j) * NTAB + which]


def shift_x(x, plus):
    return pltpu.roll(x, 1 if plus else x.shape[1] - 1, 1)


def first_row(x):
    return lax.broadcasted_iota(jnp.int32, x.shape, 0) == 0


def last_row(x):
    return lax.broadcasted_iota(jnp.int32, x.shape, 0) == x.shape[0] - 1


def from_before(x, above):
    return jnp.where(first_row(x), above, pltpu.roll(x, 1, 0))


def from_after(x, below):
    return jnp.where(last_row(x), below, pltpu.roll(x, x.shape[0] - 1, 0))


def shift_y(x, plus, outside):
    return from_before(x, outside) if plus else from_after(x, outside)


def damping_of(energy, moment):
    shifted = energy + epsilon
    ratio = moment / (shifted * MEAN_RATIO)
    r2 = ratio * ratio
    steep = energy * (r2 * r2) / energy_ref
    return shifted, ratio, steep, steep * steep * ratio


def grads_of(energy, moment, white, damp_total):
    shifted, ratio, steep, damping = damping_of(energy, moment)
    grad_damp = -time_step * white * damp_total
    grad_ratio = 9.0 * grad_damp * steep * steep
    r2 = ratio * ratio
    grad_energy = grad_damp * 2.0 * steep * (r2 * r2) * ratio / energy_ref - grad_ratio * ratio / shifted
    grad_moment = grad_ratio / (shifted * MEAN_RATIO)
    return grad_energy, grad_moment, damping


def gate(q, white, damping, ocean):
    return ocean * jnp.exp2((-time_step * LOG2E) * q * (white * damping))


def rows_from(tiles, plus, outside):
    moved = [pltpu.roll(x, 1 if plus else 7, 0) for x in tiles]
    mark = first_row(tiles[0]) if plus else last_row(tiles[0])
    feed = [outside] + moved[:-1] if plus else moved[1:] + [outside]
    return [jnp.where(mark, a, b) for a, b in zip(feed, moved)]


def slab(ref, *index):
    return [ref[(*index, slice(t, t + 8))] for t in range(0, ref.shape[-2], 8)]


def by_parity(write, first, second):
    odd = lax.rem(lax.axis_index("cells"), 2)

    @pl.when(odd == 0)
    def _():
        write(first, second)

    @pl.when(odd == 1)
    def _():
        write(second, first)


class Either:
    def __init__(self, even, odd):
        self.even, self.odd, self.shape = even, odd, even.shape

    def __getitem__(self, at):
        x, y = self.even[at], self.odd[at]
        return jnp.where(jnp.full(x.shape, lax.rem(lax.axis_index("cells"), 2), jnp.int32) == 0, x, y)


def beside(first, second):
    return Either(second, first), Either(first, second)


def misc_at(r, k):
    m = r * NMISC + k
    return m // MROWS, MISC + m % MROWS


def misc_row(ref, r, k):
    j, row = misc_at(r, k)
    return ref[j, row : row + 1, :]


def halo_rows(ref, j, r):
    return ref[j, r * NL : (r + 1) * NL, :]


def fetches(hbm, ref, sems):
    return lambda j: pltpu.make_async_copy(hbm.at[j], ref.at[j], sems.at[j])


NBUF = 3


def edge_kernel(s_hbm, mask_h, coef_h, white_h, speed_h, angle_h, a_ref, b_ref, low, high, sems, fields, ints, small_sems):
    nf, _, rows, nc = s_hbm.shape

    def fetch(j):
        return (
            pltpu.make_async_copy(s_hbm.at[j, 0:NL, rows - 8 : rows, :], low.at[j], sems.at[0, j]),
            pltpu.make_async_copy(s_hbm.at[j, NL:ND, 0:8, :], high.at[j], sems.at[1, j]),
        )

    smalls = [pltpu.make_async_copy(mask_h, ints, small_sems.at[0])]
    for k, f in enumerate((coef_h, white_h, speed_h, angle_h)):
        smalls.append(pltpu.make_async_copy(f, fields.at[k], small_sems.at[1 + k]))
    for c in smalls:
        c.start()
    for j in range(nf):
        for c in fetch(j):
            c.start()
    for c in smalls:
        c.wait()

    def write(up_ref, dn_ref):
        @pl.loop(0, nf)
        def _(j):
            up_ref[j, MISC:, :] = jnp.zeros_like(up_ref[j, MISC:, :])
            dn_ref[j, MISC:, :] = jnp.zeros_like(dn_ref[j, MISC:, :])

        for side, out in ((slice(rows - 2, rows), up_ref), (slice(0, 2), dn_ref)):
            kappa = (time_step * LOG2E / HIGHEST) * (fields[0, side] * fields[2, side])
            angle = fields[3, side]
            for k, v in enumerate((kappa, jnp.cos(angle), jnp.sin(angle), ints[side].astype(F32), fields[1, side])):
                for r in range(2):
                    a, b = misc_at(r, k)
                    out[a, b : b + 1, :] = v[r : r + 1]

        @pl.loop(0, nf)
        def _(j):
            for c in fetch(j):
                c.wait()
            for r in range(2):
                for d in range(NL):
                    up_ref[j, r * NL + d : r * NL + d + 1, :] = low[j, d, 6 + r : 7 + r, :]
                    dn_ref[j, r * NL + d : r * NL + d + 1, :] = high[j, d, r : r + 1, :]

    by_parity(write, a_ref, b_ref)


def start_kernel(tab, s_ref, mask, t0_ref, sums):
    nf = s_ref.shape[0]
    rows, nc = mask.shape
    sums[...] = jnp.zeros_like(sums)

    @pl.loop(0, nf)
    def _(j):
        rj, w, wf = [coef(tab, j, nf, k) for k in (1, 2, 4)]
        for t in range(0, rows, 8):
            acc = [None] * 5

            def add(k, v):
                acc[k] = v if acc[k] is None else acc[k] + v

            for d in range(ND):
                x = s_ref[j, d, t : t + 8, :]
                add(0, x)
                add(1 if XP[d] else 2, float(KX[d]) * x)
                add(3 if YP[d] else 4, float(KY[d]) * x)
            for k in range(5):
                sums[0, k, t : t + 8, :] += (w if k == 0 else w * rj) * acc[k]
                sums[1, k, t : t + 8, :] += (wf if k == 0 else wf * rj) * acc[k]

    ocean = mask[...].astype(F32)
    t0_ref[2 * rows :, :] = jnp.zeros_like(t0_ref[2 * rows :, :])
    for e in range(2):
        total, xp, xm, yp, ym = [ocean * sums[e, k] for k in range(5)]
        t0_ref[e * rows : (e + 1) * rows, :] = total + (
            shift_x(xp, True) + shift_x(xm, False) + from_before(yp, 0.0) + from_after(ym, 0.0) - (xp + xm + yp + ym)
        )
        t0_ref[2 * rows + e : 2 * rows + e + 1, :] = yp[rows - 1 : rows]
        t0_ref[2 * rows + 2 + e : 2 * rows + 3 + e, :] = ym[0:1]


def wind_kernel(tab, lam_ref, coef_in, speed, angle, p_ref, al_ref, a_ref, b_ref, expo):
    nf = lam_ref.shape[0]
    rows, nc = angle.shape
    for ref in (a_ref, b_ref):
        ref[:, MISC:, :] = jnp.zeros_like(ref[:, MISC:, :])
    kappa = (time_step * LOG2E / HIGHEST) * (coef_in[...] * speed[...])
    ca, sa = jnp.cos(angle[...]), jnp.sin(angle[...])
    for d in range(ND):
        align = jnp.maximum(float(COS[d]) * ca + float(SIN[d]) * sa, 0.0)
        al = align * align
        al_ref[d] = al
        expo[d] = kappa * al

    def write(up_ref, dn_ref):
        @pl.loop(0, nf)
        def _(j):
            fr = coef(tab, j, nf, 0)
            for d in range(ND):
                p = jnp.exp2(fr * expo[d]) * lam_ref[j, d]
                p_ref[j, d] = p
                for r in range(2):
                    at = slice(r * NL + d % NL, r * NL + d % NL + 1)
                    if d < NL:
                        dn_ref[j, at, :] = p[r : r + 1]
                    else:
                        up_ref[j, at, :] = p[rows - 2 + r : rows - 1 + r]

    by_parity(write, a_ref, b_ref)


def halo_growth(fr, dirs, half, misc, r):
    cosd, sind = dirs[4 * half + 2][:, 0:1], dirs[4 * half + 3][:, 0:1]
    align = jnp.maximum(cosd * misc_row(misc, r, 1) + sind * misc_row(misc, r, 2), 0.0)
    return jnp.exp2(fr * (misc_row(misc, r, 0) * (align * align)))


def halo_adv(rj, dirs, half, near, far, transpose):
    kx, ky, cosd = [dirs[4 * half + k][:, 0:1] for k in range(3)]
    before, after = shift_x(near, not transpose), shift_x(near, transpose)
    moved = jnp.where(cosd >= 0, before, after)
    return near + rj * (kx * (moved - near) + ky * (far - near))


def grow(outer, tab, j, s_ref, ocean, coef_in, speed, al_ref, u_ref, sum_ref, work, edge, before):
    nf, _, rows, nc = s_ref.shape
    fr, rj = coef(tab, j, nf, 0), coef(tab, j, nf, 1)
    work[...] = (fr * (time_step * LOG2E / HIGHEST)) * (coef_in[...] * speed[...])
    for t in range(0, rows, 8):
        at8 = slice(t, t + 8)
        o = rj * ocean[at8]
        seen = set()
        for quad in QUADS:
            plus = YP[quad[0]]
            end = t == 0 if plus else t + 8 == rows
            if end != outer:
                continue
            n = t - 1 if plus else t + 8
            acc = [None] * 3
            for d in quad:
                kx, ky = float(KX[d]), float(KY[d])
                x = o * s_ref[j, d, at8, :]
                if outer:
                    row = edge[0, d : d + 1, :] if plus else edge[1, d - NL : d - NL + 1, :]
                else:
                    row = (rj * ocean[n : n + 1]) * s_ref[j, d, n : n + 1, :]
                y = shift_y(x, plus, row)
                u = jnp.exp2(work[at8] * al_ref[d, at8]) * ((fr - (kx + ky)) * x + kx * shift_x(x, XP[d]) + ky * y)
                u_ref[j, d, at8, :] = u
                for k, v in enumerate((u, kx * u, ky * u)):
                    acc[k] = v if acc[k] is None else acc[k] + v
            for k, key in enumerate((0, 1 if XP[quad[0]] else 2, 3 if plus else 4)):
                at = (key, j, at8)
                if key in seen:
                    sum_ref[at] += acc[k]
                else:
                    sum_ref[at] = acc[k] if before is None else before[at] + acc[k]
                seen.add(key)
        for key in range(5):
            if key not in seen:
                at = (key, j, at8)
                sum_ref[at] = jnp.zeros((8, nc), F32) if before is None else before[at]


def inner_kernel(tab, s_ref, mask, coef_in, speed, al_ref, u_ref, sum_ref, work):
    ocean = mask[...].astype(F32)

    @pl.loop(0, s_ref.shape[0])
    def _(j):
        grow(False, tab, j, s_ref, ocean, coef_in, speed, al_ref, u_ref, sum_ref, work, None, None)


def grown_kernel(tab, dirs, s_ref, mask, coef_in, speed, al_ref, s_first, s_second, u_in, before, u_ref, sum_ref, ul_ref, uh_ref, sy_ref, edge, work):
    nf, _, rows, nc = s_ref.shape
    lo, hi = beside(s_first, s_second)
    ocean = mask[...].astype(F32)

    @pl.loop(0, nf)
    def _(j):
        fr, rj = coef(tab, j, nf, 0), coef(tab, j, nf, 1)
        for half, (blk, near, far, out) in enumerate(((lo, 1, 0, ul_ref), (hi, 0, 1, uh_ref))):
            x = [misc_row(blk, r, 3) * halo_rows(blk, j, r) for r in range(2)]
            edge[half] = rj * x[near]
            u = halo_growth(fr, dirs, half, blk, near) * halo_adv(rj, dirs, half, x[near], x[far], False)
            out[j] = u
            sy_ref[half, pl.ds(j, 1), :] = jnp.sum(dirs[4 * half + 1][:, 0:1] * u, axis=0, keepdims=True)
        grow(True, tab, j, s_ref, ocean, coef_in, speed, al_ref, u_ref, sum_ref, work, edge, before)
        for t in range(0, rows, 8):
            a, b, c, d, e = [sum_ref[k, j, t : t + 8, :] for k in range(5)]
            sum_ref[0, j, t : t + 8, :] = a - rj * (b + c + d + e)


def product_kernel(tab, u_ref, p_ref, al_ref, ul_ref, uh_ref, r_ref, t_ref):
    nf, _, rows, nc = u_ref.shape

    @pl.loop(0, nf)
    def _(j):
        rj = coef(tab, j, nf, 1)
        for t in range(0, rows, 8):
            seen = set()
            for quad in QUADS:
                acc = [None] * 6
                for d in quad:
                    kx, ky = float(KX[d]), float(KY[d])
                    u, p, al = u_ref[j, d, t : t + 8, :], p_ref[j, d, t : t + 8, :], al_ref[d, t : t + 8, :]
                    if YP[d]:
                        row = ul_ref[j, d : d + 1, :] if t == 0 else u_ref[j, d, t - 1 : t, :]
                        y = jnp.where(first_row(u), row, pltpu.roll(u, 1, 0))
                    else:
                        row = uh_ref[j, d - NL : d - NL + 1, :] if t + 8 == rows else u_ref[j, d, t + 8 : t + 9, :]
                        y = jnp.where(last_row(u), row, pltpu.roll(u, 7, 0))
                    cu = (1.0 - rj * (kx + ky)) * (p * u)
                    px, py = kx * (p * shift_x(u, XP[d])), ky * (p * y)
                    for k, v in enumerate((cu, px, py, al * cu, al * px, al * py)):
                        acc[k] = v if acc[k] is None else acc[k] + v
                xk, yk = (1 if XP[quad[0]] else 2), (3 if YP[quad[0]] else 4)
                for k, ref in enumerate((r_ref, t_ref)):
                    for key, v in zip((0, xk, yk), acc[3 * k : 3 * k + 3]):
                        at = (key, j, slice(t, t + 8))
                        ref[at] = ref[at] + v if (k, key) in seen else v
                        seen.add((k, key))


def total_kernel(rows, *refs):
    parts, (tot, first, second) = refs[:-3], refs[-3:]
    total = parts[0][...]
    for part in parts[1:]:
        total = total + part[...]
    tot[...] = total

    def write(up, dn):
        up[...] = jnp.zeros_like(up)
        dn[...] = jnp.zeros_like(dn)
        for k, row in enumerate((rows - 1, 2 * rows - 1, 2 * rows, 2 * rows + 1)):
            up[k : k + 1, :] = total[row : row + 1]
        for k, row in enumerate((0, rows, 2 * rows + 2, 2 * rows + 3)):
            dn[k : k + 1, :] = total[row : row + 1]

    by_parity(write, first, second)


def advected_sum(rj, h, above, below, s):
    return h * s[0], rj * (
        shift_x(h * s[1], True) + shift_x(h * s[2], False) + from_before(h * s[3], above) + from_after(h * s[4], below)
    )


def first_kernel(nf, tab, tot, e_first, e_second, s_first, s_second, mask, white, sum_ref, sy_ref, t0_ref, t0h_ref, h0_ref, h0h_ref, t1_ref):
    rows, nc = mask.shape
    lo, hi = beside(e_first, e_second)
    lo_misc, hi_misc = beside(s_first, s_second)
    ocean = mask[...].astype(F32)
    row = lax.broadcasted_iota(jnp.int32, (rows, nc), 0)
    total = tot[...]
    field = []
    halo = []
    t0h_ref[...] = jnp.zeros_like(t0h_ref)
    for k in range(2):
        v = total[k * rows : (k + 1) * rows]
        v = v + jnp.where(row == 0, lo[2 + k : 3 + k, :], 0.0) + jnp.where(row == rows - 1, hi[2 + k : 3 + k, :], 0.0)
        field.append(ocean * v)
        t0_ref[k] = field[k]
        above = misc_row(lo_misc, 1, 3) * (lo[k : k + 1, :] + total[2 * rows + 2 + k : 2 * rows + 3 + k])
        below = misc_row(hi_misc, 0, 3) * (hi[k : k + 1, :] + total[2 * rows + k : 2 * rows + 1 + k])
        halo.append((above, below))
        t0h_ref[k : k + 1, :] = above
        t0h_ref[2 + k : 3 + k, :] = below
    damping = damping_of(*field)[3]
    damp_lo = damping_of(halo[0][0], halo[1][0])[3]
    damp_hi = damping_of(halo[0][1], halo[1][1])[3]
    energy, moment = jnp.zeros((rows, nc), F32), jnp.zeros((rows, nc), F32)
    for j in range(nf):
        rj, w, q, wf = [coef(tab, j, nf, k) for k in (1, 2, 3, 4)]
        h = gate(q, white[...], damping, ocean)
        h_lo = gate(q, misc_row(lo_misc, 1, 4), damp_lo, misc_row(lo_misc, 1, 3))
        h_hi = gate(q, misc_row(hi_misc, 0, 4), damp_hi, misc_row(hi_misc, 0, 3))
        h0_ref[j] = h
        h0h_ref[0, j : j + 1, :] = h_lo
        h0h_ref[1, j : j + 1, :] = h_hi
        centre, around = advected_sum(
            rj, h, h_lo * sy_ref[0, j : j + 1, :], h_hi * sy_ref[1, j : j + 1, :], [sum_ref[k, j] for k in range(5)]
        )
        adv = centre + around
        energy, moment = energy + w * adv, moment + wf * adv
    t1_ref[0:rows, :] = energy
    t1_ref[rows : 2 * rows, :] = moment


def gathered(rj, h, h_lo, h_hi, r):
    return h * r[0] + rj * (
        shift_x(h, True) * r[1] + shift_x(h, False) * r[2] + from_before(h, h_lo) * r[3] + from_after(h, h_hi) * r[4]
    )


def second_kernel(nf, n, tab, *refs):
    parts, (mask, white, h0_ref, h0h_ref, r_ref, t1_ref, h1_ref, d1_ref) = refs[:n], refs[n:]
    rows, nc = mask.shape
    ocean = mask[...].astype(F32)
    total = parts[0][...]
    for part in parts[1:]:
        total = total + part[...]
    energy, moment = ocean * total[:rows], ocean * total[rows:]
    t1_ref[0] = energy
    t1_ref[1] = moment
    damping = damping_of(energy, moment)[3]
    acc = jnp.zeros((rows, nc), F32)
    for j in range(nf):
        rj, q = coef(tab, j, nf, 1), coef(tab, j, nf, 3)
        h1 = gate(q, white[...], damping, ocean)
        h1_ref[j] = h1
        part = gathered(rj, h0_ref[j], h0h_ref[0, j : j + 1, :], h0h_ref[1, j : j + 1, :], [r_ref[k, j] for k in range(5)])
        acc = acc + q * (h1 * part)
    d1_ref[...] = acc


def third_kernel(nf, n, tab, *refs):
    parts = refs[:n]
    mask, white, speed, t1, h0_ref, h0h_ref, h1_ref, sum_ref, sy_ref, r_ref, t_ref = refs[n : n + 11]
    d1_ref, v1_ref, d0_ref, f1_ref, first, second = refs[n + 11 :]
    rows, nc = mask.shape
    ocean = mask[...].astype(F32)
    damp = parts[0][...]
    for part in parts[1:]:
        damp = damp + part[...]
    d1_ref[...] = damp
    grad_e, grad_m, _ = grads_of(t1[0], t1[1], white[...], damp)
    acc, force = jnp.zeros((rows, nc), F32), jnp.zeros((rows, nc), F32)
    push_lo, push_hi = jnp.zeros((1, nc), F32), jnp.zeros((1, nc), F32)
    for j in range(nf):
        fr, rj, w, q = [coef(tab, j, nf, k) for k in range(4)]
        h0, h1 = h0_ref[j], h1_ref[j]
        h_lo, h_hi = h0h_ref[0, j : j + 1, :], h0h_ref[1, j : j + 1, :]
        v1 = ocean * (w * (grad_e + fr * grad_m))
        v1_ref[j] = v1
        s, r = [sum_ref[k, j] for k in range(5)], [r_ref[k, j] for k in range(5)]
        inner = (
            shift_x(h1 * r[1], False)
            + shift_x(h1 * r[2], True)
            + from_after(h1 * r[3], 0.0)
            + from_before(h1 * r[4], 0.0)
            + s[1] * shift_x(v1, False)
            + s[2] * shift_x(v1, True)
            + s[3] * from_after(v1, 0.0)
            + s[4] * from_before(v1, 0.0)
        )
        acc = acc + q * (h0 * (h1 * r[0] + v1 * s[0] + rj * inner))
        push_lo = push_lo + (q * rj) * (h_lo * (h1[0:1] * r[3][0:1] + v1[0:1] * sy_ref[0, j : j + 1, :]))
        e = rows - 1
        push_hi = push_hi + (q * rj) * (
            h_hi * (h1[e : e + 1] * r[4][e : e + 1] + v1[e : e + 1] * sy_ref[1, j : j + 1, :])
        )
        part = gathered(rj, h0, h_lo, h_hi, [t_ref[k, j] for k in range(5)])
        force = force + fr * (h1 * part)
    def write(up, dn):
        for k, v in enumerate((t1[0], t1[1], damp)):
            up[2 * k : 2 * k + 2, :] = v[rows - 2 : rows]
            dn[2 * k : 2 * k + 2, :] = v[0:2]
        up[6:7, :] = acc[rows - 1 : rows]
        up[7:8, :] = push_hi
        dn[6:7, :] = acc[0:1]
        dn[7:8, :] = push_lo

    by_parity(write, first, second)
    d0_ref[0:rows, :] = acc
    d0_ref[rows:, :] = jnp.zeros_like(d0_ref[rows:, :])
    d0_ref[rows : rows + 1, :] = push_lo
    d0_ref[rows + 1 : rows + 2, :] = push_hi
    f1_ref[...] = (speed[...] / HIGHEST) * force


def fourth_kernel(nf, tab, part, b_first, b_second, s_first, s_second, a_low, a_high, t_ref, h0_ref, h1_ref, v1_ref, f1_ref, speed, out):
    rows, nc = speed.shape
    lo, hi = beside(b_first, b_second)
    lo_misc, hi_misc = beside(s_first, s_second)
    row = lax.broadcasted_iota(jnp.int32, (rows, nc), 0)
    v = part[0:rows, :]
    v = v + jnp.where(row == 0, lo[7:8, :], 0.0) + jnp.where(row == rows - 1, hi[7:8, :], 0.0)
    out[0:rows, :] = v
    out[rows : rows + 8, :] = jnp.zeros((8, nc), F32)
    out[rows : rows + 1, :] = part[rows : rows + 1, :] + lo[6:7, :]
    out[rows + 1 : rows + 2, :] = part[rows + 1 : rows + 2, :] + hi[6:7, :]
    outside = []
    for got, misc, r in ((lo, lo_misc, 1), (hi, hi_misc, 0)):
        energy, moment, damp = [got[2 * k + r : 2 * k + r + 1, :] for k in range(3)]
        white = misc_row(misc, r, 4)
        grad_e, grad_m, damping = grads_of(energy, moment, white, damp)
        outside.append((white, damping, misc_row(misc, r, 3), grad_e, grad_m))
    force = jnp.zeros((rows, nc), F32)
    low = a_low.shape[1]
    for j in range(nf):
        fr, w, q = [coef(tab, j, nf, k) for k in (0, 2, 3)]
        a = [a_low[k, j] if j < low else a_high[k, j - low] for k in range(9)]
        h1, v1 = h1_ref[j], v1_ref[j]
        edges = [(gate(q, white, damping, o), o * (w * (ge + fr * gm))) for white, damping, o, ge, gm in outside]
        force = force + (fr * h0_ref[j]) * (h1 * t_ref[0, j]) + v1 * a[0]
        for x, k, b in ((v1, 0, 1), (h1, 4, 0)):
            force = force + (
                shift_x(x, False) * a[k + 1]
                + shift_x(x, True) * a[k + 2]
                + from_after(x, edges[1][b]) * a[k + 3]
                + from_before(x, edges[0][b]) * a[k + 4]
            )
    out[rows + 8 :, :] = (speed[...] / HIGHEST) * force + f1_ref[...]


def force_kernel(first, tab, u_ref, p_ref, al_ref, h0_ref, p_first, p_second, a_ref):
    nf, _, rows, nc = u_ref.shape
    pl_ref, ph_ref = beside(p_first, p_second)

    @pl.loop(0, a_ref.shape[1])
    def _(i):
        j = first + i
        fr, rj = coef(tab, j, nf, 0), coef(tab, j, nf, 1)
        for t in range(0, rows, 8):
            seen = set()
            for quad in QUADS:
                acc = [None] * 5
                for d in quad:
                    kx, ky = float(KX[d]), float(KY[d])
                    u, p, al = u_ref[j, d, t : t + 8, :], p_ref[j, d, t : t + 8, :], al_ref[d, t : t + 8, :]
                    if YP[d]:
                        row = ph_ref[j, d : d + 1, :] if t + 8 == rows else p_ref[j, d, t + 8 : t + 9, :]
                        y = from_after(p, row)
                    else:
                        row = pl_ref[j, d : d + 1, :] if t == 0 else p_ref[j, d, t - 1 : t, :]
                        y = from_before(p, row)
                    au = al * u
                    xau, yau = kx * au, ky * au
                    for k, v in enumerate(((1.0 - rj * (kx + ky)) * au, xau, yau, xau * shift_x(p, not XP[d]), yau * y)):
                        acc[k] = v if acc[k] is None else acc[k] + v
                xk, yk = (1 if XP[quad[0]] else 2), (3 if YP[quad[0]] else 4)
                for key, v in zip((0, xk, yk, 4 + xk, 4 + yk), acc):
                    at = (key, i, slice(t, t + 8))
                    a_ref[at] = a_ref[at] + v if key in seen else v
                    seen.add(key)
        h0 = h0_ref[j]
        for k in range(9):
            a_ref[k, i] = (fr * h0 if k == 0 else h0) * a_ref[k, i]


def back_kernel(tab, dirs, p_ref, coef_in, al_ref, h0_ref, h0h_ref, h1_ref, v1_ref, p_first, p_second, s_first, s_second, b_first, b_second, speed, z_ref, zl_ref, zh_ref, edge, halo, scaled, work):
    nf, _, rows, nc = p_ref.shape
    pl_ref, ph_ref = beside(p_first, p_second)
    lo_misc, hi_misc = beside(s_first, s_second)
    lo, hi = beside(b_first, b_second)
    sides = ((0, ph_ref, hi_misc, hi, 0, 1, 1, zh_ref), (1, pl_ref, lo_misc, lo, 1, 0, 0, zl_ref))
    for side, (_, _, misc, got, *_) in enumerate(sides):
        for r in range(2):
            energy, moment, damp = [got[2 * k + r : 2 * k + r + 1, :] for k in range(3)]
            white = misc_row(misc, r, 4)
            grad_e, grad_m, damping = grads_of(energy, moment, white, damp)
            for k, v in enumerate((grad_e, grad_m, white * damping)):
                halo[side, r, k : k + 1, :] = v

    @pl.loop(0, nf)
    def _(j):
        fr, rj = coef(tab, j, nf, 0), coef(tab, j, nf, 1)
        w, q = coef(tab, j, nf, 2), coef(tab, j, nf, 3)
        for side, (half, blk, misc, _, near, far, which, out) in enumerate(sides):
            x = []
            for r in range(2):
                ocean = misc_row(misc, r, 3)
                h = gate(q, halo[side, r, 2:3, :], 1.0, ocean)
                v = ocean * (w * (halo[side, r, 0:1, :] + fr * halo[side, r, 1:2, :]))
                x.append(halo_rows(blk, j, r) * h + v)
            edge[side] = x[near]
            moved = halo_adv(rj, dirs, half, x[near], x[far], True) * halo_growth(fr, dirs, half, misc, near)
            out[j] = moved * h0h_ref[which, pl.ds(j, 1), :]
        tiles = range(rows // 8)
        at8 = [slice(8 * t, 8 * t + 8) for t in tiles]
        work[...] = (fr * (time_step * LOG2E / HIGHEST)) * (coef_in[...] * speed[...])
        for t in tiles:
            scaled[at8[t]] = rj * h0_ref[j, at8[t]]
        for d in range(ND):
            kx, ky = float(KX[d]), float(KY[d])
            x = [p_ref[j, d, at8[t]] * h1_ref[j, at8[t]] + v1_ref[j, at8[t]] for t in tiles]
            row = edge[0, d : d + 1, :] if YP[d] else edge[1, d - NL : d - NL + 1, :]
            y = rows_from(x, not YP[d], row)
            for t in tiles:
                back = (fr - (kx + ky)) * x[t] + kx * shift_x(x[t], not XP[d]) + ky * y[t]
                z_ref[j, d, at8[t]] = back * (jnp.exp2(work[at8[t]] * al_ref[d, at8[t]]) * scaled[at8[t]])


def out_kernel(n, tab, *refs):
    parts, refs = refs[:n], refs[n:]
    z_ref, zl_ref, zh_ref, t0, t0h, t1, d1, mask, white, s_first, s_second = refs[:11]
    lo_misc, hi_misc = beside(s_first, s_second)
    out_hbm, gi_ref, gw_ref, own, halo, edge, work, buf, sems = refs[11:]
    nf, _, rows, nc = z_ref.shape
    ocean = mask[...].astype(F32)
    total = parts[0][...]
    for part in parts[1:]:
        total = total + part[...]
    damp = total[0:rows]
    gi_ref[...] = time_step * total[rows + 8 :]
    grad_e, grad_m, damping = grads_of(t0[0], t0[1], white[...], damp)
    own[0] = grad_e
    own[1] = grad_m
    gw_ref[...] = -time_step * (damping * damp + damping_of(t1[0], t1[1])[3] * d1[...])
    above, below = total[rows : rows + 1], total[rows + 1 : rows + 2]
    sides = ((hi_misc, 0, 2, below, zh_ref), (lo_misc, 1, 0, above, zl_ref))
    for side, (misc, r, k, damp, _) in enumerate(sides):
        e, m, _ = grads_of(t0h[k : k + 1, :], t0h[k + 1 : k + 2, :], misc_row(misc, r, 4), damp)
        halo[side, 0:1, :] = e
        halo[side, 1:2, :] = m

    def put(j, half):
        part = slice(0, NL) if half == 0 else slice(NL, ND)
        return pltpu.make_async_copy(buf.at[j % NBUF, part], out_hbm.at[j, part], sems.at[j % NBUF, half])

    @pl.loop(0, nf)
    def _(j):
        slot = j % NBUF
        fr, rj, w = [coef(tab, j, nf, k) for k in range(3)]
        for side, (misc, r, _, _, z) in enumerate(sides):
            edge[side] = z[j] + misc_row(misc, r, 3) * (w * (halo[side, 0:1, :] + fr * halo[side, 1:2, :]))
        tiles = range(rows // 8)
        o = [ocean[8 * t : 8 * t + 8] for t in tiles]
        v = [o[t] * (w * (own[0, 8 * t : 8 * t + 8] + fr * own[1, 8 * t : 8 * t + 8])) for t in tiles]
        for t in tiles:
            work[0, 8 * t : 8 * t + 8] = v[t]
            work[1, 8 * t : 8 * t + 8] = rj * o[t]

        @pl.when(j >= NBUF)
        def _():
            for half in range(2):
                put(j - NBUF, half).wait()

        for d in range(ND):
            kx, ky = float(KX[d]), float(KY[d])
            x = [z + work[0, 8 * t : 8 * t + 8] for t, z in enumerate(slab(z_ref, j, d))]
            row = edge[0, d : d + 1, :] if YP[d] else edge[1, d - NL : d - NL + 1, :]
            y = rows_from(x, not YP[d], row)
            for t in tiles:
                back = (fr - (kx + ky)) * x[t] + kx * shift_x(x[t], not XP[d]) + ky * y[t]
                buf[slot, d, 8 * t : 8 * t + 8, :] = work[1, 8 * t : 8 * t + 8] * back
            if d == NL - 1:
                put(j, 0).start()
        put(j, 1).start()

    for j in range(max(0, nf - NBUF), nf):
        for half in range(2):
            put(j, half).wait()


VMEM = pl.BlockSpec(memory_space=pltpu.VMEM)
SMEM = pl.BlockSpec(memory_space=pltpu.SMEM)
HBM = pl.BlockSpec(memory_space=pltpu.HBM)


def f32(*shape):
    return jax.ShapeDtypeStruct(shape, F32)


def vmem(*shape):
    return pltpu.VMEM(shape, F32)


def call(kernel, name, outs, args, scratch=(), hbm=(), held=(), out_hbm=(), limit=6, alias=None):
    put = {**dict.fromkeys(hbm, pltpu.HBM), **dict.fromkeys(held, pltpu.VMEM)}
    args = [pltpu.with_memory_space_constraint(a, put[k]) if k in put else a for k, a in enumerate(args)]
    return pl.pallas_call(
        kernel,
        name=name,
        out_shape=outs,
        in_specs=[HBM if k in hbm else SMEM if a.ndim == 1 else VMEM for k, a in enumerate(args)],
        out_specs=[HBM if k in out_hbm else VMEM for k in range(len(outs))],
        scratch_shapes=list(scratch),
        input_output_aliases=alias or {},
        compiler_params=pltpu.CompilerParams(vmem_limit_bytes=limit * MIB),
        cost_estimate=pl.CostEstimate(flops=1, bytes_accessed=1, transcendentals=0),
    )(*args)


def peers(x):
    n = lax.axis_size("spec")
    if n & (n - 1) == 0:
        return [lax.ppermute(x, "spec", [(i, i ^ k) for i in range(n)]) for k in range(1, n)]
    return [lax.ppermute(x, "spec", [(i, (i + k) % n) for i in range(n)]) for k in range(1, n)]


def exchange(first, second):
    n = lax.axis_size("cells")
    swaps = [[(i, i + 1) for i in range(odd, n - 1, 2)] for odd in range(2)]
    return [lax.ppermute(x, "cells", pairs + [(b, a) for a, b in pairs]) for x, pairs in zip((first, second), swaps)]


def after(first, *later):
    return lax.optimization_barrier((first, *later))[1:]


def shards(spectrum_start, input_coef, white_coef, wind_speed, wind_angle, sea_mask, cotangent):
    nf, _, rows, nc = spectrum_start.shape
    n = lax.axis_size("spec")
    tab, dirs = jnp.asarray(TABLE), jnp.asarray(DIRS)
    big = vmem(nf, ND, rows, nc)
    band = f32(nf, MISC + MROWS, nc)
    line, duo, hs, sums = f32(nf, NL, nc), f32(2, nf, nc), f32(nf, rows, nc), f32(5, nf, rows, nc)
    flat, two, push = f32(rows, nc), f32(2, rows, nc), f32(8, nc)
    stream = [vmem(NBUF, ND, rows, nc), pltpu.SemaphoreType.DMA((NBUF, 2))]
    heavy = dict(limit=8)

    s_up, s_dn = call(
        edge_kernel, "edge", [band, band], [spectrum_start, sea_mask, input_coef, white_coef, wind_speed, wind_angle],
        [
            vmem(nf, NL, 8, nc), vmem(nf, NL, 8, nc), pltpu.SemaphoreType.DMA((2, nf)), vmem(4, rows, nc),
            pltpu.VMEM((rows, nc), jnp.int32), pltpu.SemaphoreType.DMA((5,)),
        ],
        hbm=range(6), **heavy,
    )
    s_lo, s_hi = exchange(s_up, s_dn)
    (mask,) = after(s_up, sea_mask)
    (t0_part,) = call(
        start_kernel, "start", [f32(2 * rows + 8, nc)], [tab, spectrum_start, mask], [vmem(2, 5, rows, nc)], held=(1,), **heavy
    )
    t0_parts = peers(t0_part)
    (speed,) = after(t0_part, wind_speed)
    p, al, p_up, p_dn = call(
        wind_kernel, "wind", [big, vmem(ND, rows, nc), band, band], [tab, cotangent, input_coef, speed, wind_angle],
        [vmem(ND, rows, nc)], held=(1,), **heavy,
    )
    u_inner, s5_inner = call(
        inner_kernel, "inner", [big, sums], [tab, spectrum_start, sea_mask, input_coef, wind_speed, al], [vmem(rows, nc)],
        held=(1, 5), **heavy,
    )
    (t0_own,) = after(s5_inner, t0_part)
    tot0, e_up, e_dn = call(functools.partial(total_kernel, rows), "total", [f32(2 * rows + 8, nc), push, push], [t0_own, *t0_parts])
    e_lo, e_hi = exchange(e_up, e_dn)
    (mask,) = after(tot0, sea_mask)
    u, s5, u_lo, u_hi, sy = call(
        grown_kernel, "grown", [big, sums, line, line, duo], [tab, dirs, spectrum_start, mask, input_coef, wind_speed, al, s_lo, s_hi, u_inner, s5_inner],
        [vmem(2, NL, nc), vmem(rows, nc)], held=(2, 6, 9), alias={9: 0}, **heavy,
    )
    t0, t0h, h0, h0h, t1_part = call(
        functools.partial(first_kernel, nf), "first", [two, push, hs, duo, f32(2 * rows, nc)],
        [tab, tot0, e_lo, e_hi, s_lo, s_hi, sea_mask, white_coef, s5, sy],
    )
    t1_parts = peers(t1_part)
    p_up, p_dn = after(t1_part, p_up, p_dn)
    p_lo, p_hi = exchange(p_up, p_dn)
    r5, t5 = call(product_kernel, "product", [sums, sums], [tab, u, p, al, u_lo, u_hi], held=(1, 2, 3), **heavy)
    (t1_own,) = after(r5, t1_part)
    t1, h1, d1_part = call(
        functools.partial(second_kernel, nf, n), "second", [two, hs, flat],
        [tab, t1_own, *t1_parts, sea_mask, white_coef, h0, h0h, r5],
    )
    d1_parts = peers(d1_part)
    half = max(1, nf * 5 // 8)
    forces = lambda first, count, h0: call(
        functools.partial(force_kernel, first), "force", [f32(9, count, rows, nc)], [tab, u, p, al, h0, p_lo, p_hi], held=(1, 2, 3), **heavy
    )[0]
    (h0_late,) = after(d1_part, h0)
    a_low = forces(0, half, h0_late)
    a_low, d1_own = lax.optimization_barrier((a_low, d1_part))
    d1_parts = [d1_own] + d1_parts
    d1, v1, d0_part, f1, b_up, b_dn = call(
        functools.partial(third_kernel, nf, n), "third", [flat, hs, f32(rows + 8, nc), flat, push, push],
        [tab, *d1_parts, sea_mask, white_coef, wind_speed, t1, h0, h0h, h1, s5, sy, r5, t5],
    )
    b_lo, b_hi = exchange(b_up, b_dn)
    (h0_late,) = after(b_up, h0)
    a_high = forces(half, nf - half, h0_late)
    (red,) = call(
        functools.partial(fourth_kernel, nf), "fourth", [f32(2 * rows + 8, nc)],
        [tab, d0_part, b_lo, b_hi, s_lo, s_hi, a_low, a_high, t5, h0, h1, v1, f1, wind_speed],
    )
    reds = peers(red)
    (late_speed,) = after(red, wind_speed)
    z, z_lo, z_hi = call(
        back_kernel, "back", [big, line, line],
        [tab, dirs, p, input_coef, al, h0, h0h, h1, v1, p_lo, p_hi, s_lo, s_hi, b_lo, b_hi, late_speed],
        [vmem(2, NL, nc), vmem(2, 2, 8, nc), vmem(rows, nc), vmem(rows, nc)], held=(2, 4), **heavy,
    )
    (red_own,) = after(z_lo, red)
    reds = [red_own] + reds
    out, grad_input, grad_white = call(
        functools.partial(out_kernel, n), "out", [f32(nf, ND, rows, nc), flat, flat],
        [tab, *reds, z, z_lo, z_hi, t0, t0h, t1, d1, sea_mask, white_coef, s_lo, s_hi],
        [vmem(2, rows, nc), vmem(2, 8, nc), vmem(2, NL, nc), vmem(2, rows, nc)] + stream, held=(1 + n,), out_hbm=(0,), **heavy,
    )
    return out, grad_input, grad_white


def solution(mesh):
    return jax.shard_map(
        shards,
        mesh=mesh,
        in_specs=(
            P("spec", None, "cells", None),
            P("cells", None),
            P("cells", None),
            P("cells", None),
            P("cells", None),
            P("cells", None),
            P("spec", None, "cells", None),
        ),
        out_specs=(P("spec", None, "cells", None), P("cells", None), P("cells", None)),
        check_vma=False,
    )
```
